32 devices in a mesh: dp: 8 (over y, x, core), tensor: 4 (over z).
Axes of the slice: x: 2, y: 2, z: 4, core: 2. Of those that a mesh axis runs over, the one named last changes fastest.
Arguments:
- tokens: bfloat16 [4096, 2048], P('dp'), may hold values from -6 to 6
- segment_ids: int32 [8, 512], P('dp'), may hold values from 0 to 15, never falling along the last dimension, each value on 1 to 256 neighbouring positions
- norm_gain: bfloat16 [2048], replicated, may hold values from 0.099609375 to 1.8984375
- norm_bias: bfloat16 [2048], replicated, may hold values from -2 to 2
- qkv_weight: bfloat16 [2048, 6144], P(None, 'tensor'), may hold values from -0.125 to 0.125
- qkv_bias: bfloat16 [6144], P('tensor'), may hold values from -2 to 2
- out_weight: bfloat16 [2048, 2048], P('tensor'), may hold values from -0.5 to 0.5
- gate_weight: bfloat16 [2048, 5632], P(None, 'tensor'), may hold values from -0.125 to 0.125
- up_weight: bfloat16 [2048, 5632], P(None, 'tensor'), may hold values from -0.125 to 0.125
- down_weight: bfloat16 [5632, 2048], P('tensor'), may hold values from -0.078125 to 0.078125
- cotangent: bfloat16 [4096, 2048], P('dp'), may hold values from -6 to 6
Outputs:
- output: bfloat16 [4096, 2048], P('dp')
- grad_input: bfloat16 [4096, 2048], P('dp')
- grad_gain: float32 [2048], replicated
- grad_norm_bias: float32 [2048], replicated
- grad_qkv_weight: float32 [2048, 6144], P('dp', 'tensor')
- grad_qkv_bias: float32 [6144], P('tensor')
- grad_out_weight: float32 [2048, 2048], P('tensor', 'dp')
- grad_gate_weight: float32 [2048, 5632], P('dp', 'tensor')
- grad_up_weight: float32 [2048, 5632], P('dp', 'tensor')
- grad_down_weight: float32 [5632, 2048], P('tensor', 'dp')
The draws below stay inside these ranges and needn't reach their ends.
Inputs may be any that keep to these rules, and one draw needn't show every extreme that they name: `segment_ids`: ids never fall along a sequence; each document has 1 to 256 tokens, and every sequence has one document of exactly 256 tokens.
All inputs are finite; a program needn't handle non-finite values.
Results may differ from the reference program's by a relative error of at most 0.0096.
Values may be sent and summed in bfloat16 or wider, within the bound.
A program may use at most 256 MiB of HBM per device.

```python
import math
import jax
import jax.numpy as jnp
import numpy as np
from jax import lax

D = 2048
H = 32
DH = 64
ROT = 16
FF = 5632
LEN = 512
NSEQ = 8
TOKENS = 4096


def raised(values, rng, source, target, parts, factor):
    def block_of(axis_at):
        return (jnp.arange(values.shape[axis_at]) // (values.shape[axis_at] // parts)).reshape((-1,) + (1,) * (values.ndim - 1 - axis_at))

    one_side = jax.random.permutation(rng, parts)[block_of(target)]
    far = (block_of(target) + parts // 2) % parts
    return jnp.where((block_of(source) == one_side) | (block_of(source) == far), factor * values, values)


def level_of(key, dims, pieces, low, high):
    loudness = 1.0
    for dim, parts in pieces:
        heights = jax.random.uniform(jax.random.fold_in(jax.random.fold_in(key, 6), dim), (parts,), jnp.float32, low / len(pieces), high / len(pieces))
        loudness = loudness * jnp.repeat(jnp.exp(heights), dims[dim] // parts).reshape((-1,) + (1,) * (len(dims) - 1 - dim))
    return loudness


def split_up(count, total, limit, lean):
    portions = [(1 << 20) // math.isqrt(rank ** lean) + 1 for rank in range(2, count + 1)]
    spare, counts = total - limit - (count - 1), [1] * (count - 1)
    while spare > 0:
        candidates = [i for i in range(count - 1) if counts[i] < limit]
        pool, remaining = sum([portions[i] for i in candidates]), spare
        for i in candidates:
            addition = min(limit - counts[i], max(1, remaining * portions[i] // pool), spare)
            counts[i] = counts[i] + addition
            spare = spare - addition
    return np.array([limit] + counts)


def uneven_parts(key, number_of, total, reach, skew):
    if number_of == 2:
        one = jax.random.randint(key, (), max(1, total - reach), min(reach, total - 1) + 1)
        return jnp.stack([one, total - one])
    tallies = jnp.asarray(split_up(number_of, total, reach, skew), jnp.int32)
    twos = (number_of - 1) // 2
    donor, taker = tallies[1:1 + 2 * twos:2], tallies[2:2 + 2 * twos:2]
    room = jnp.minimum(donor - 1, reach - taker)
    moved = jax.random.randint(jax.random.fold_in(key, 1), (twos,), 0, 1 << 20) % (room + 1)
    tallies = tallies.at[1:1 + 2 * twos:2].set(donor - moved).at[2:2 + 2 * twos:2].set(taker + moved)
    return tallies[jax.random.permutation(jax.random.fold_in(key, 2), number_of)]


def bell_draw(key, extent, deviation, most, split=(), held_as=jnp.bfloat16):
    level = level_of(key, extent, split, -0.22, 0.18) if split else 1.0
    values = jax.random.normal(key, extent, jnp.float32) * deviation * level
    return jnp.minimum(jnp.maximum(values, -most), most).astype(held_as)


def bell_draw_with(key, shape, scale, bound, split, heavy, kind=jnp.bfloat16):
    drawn = scale * jax.random.normal(key, shape, jnp.float32)
    if split:
        drawn = drawn * level_of(key, shape, split, -0.22, 0.18)
    return jnp.clip(raised(drawn, jax.random.fold_in(key, 3), *heavy), -bound, bound).astype(kind)


def setup_inputs(seed: int = 0) -> dict:
    keys = jax.random.split(jax.random.key(seed), 12)
    tokens = bell_draw_with(keys[0], (TOKENS, D), 1.0, 6.0, ((0, 8),), (0, 1, 8, 2.0))
    segment_ids = jax.vmap(lambda own: jnp.searchsorted(jnp.cumsum(uneven_parts(own, max(4, LEN // 32), LEN, LEN // 2, 2)), jnp.arange(LEN), side="right"))(jax.random.split(keys[1], NSEQ)).reshape((NSEQ, LEN)).astype(jnp.int32)
    norm_gain = jnp.clip(1.0 + 0.18 * jax.random.normal(keys[2], (D,), jnp.float32), 0.099609375, 1.8984375).astype(jnp.bfloat16)
    norm_bias = bell_draw(keys[3], (D,), 0.3, 2.0)
    qkv_weight = bell_draw(keys[4], (D, 3 * H * DH), D ** -0.5, 0.125, ((1, 4),))
    qkv_bias = bell_draw(keys[5], (3 * H * DH,), 0.3, 2.0, ((0, 4),))
    out_weight = bell_draw(keys[6], (H * DH, D), (H * DH // 16) ** -0.5, 0.5, ((0, 4),))
    gate_weight = bell_draw(keys[7], (D, FF), D ** -0.5, 0.125, ((1, 4),))
    up_weight = bell_draw(keys[8], (D, FF), D ** -0.5, 0.125, ((1, 4),))
    down_weight = bell_draw(keys[9], (FF, D), FF ** -0.5, 0.078125, ((0, 4),))
    cotangent = bell_draw_with(keys[10], (TOKENS, D), 1.0, 6.0, ((0, 8),), (0, 1, 8, 2.0))
    return {"tokens": tokens, "segment_ids": segment_ids, "norm_gain": norm_gain, "norm_bias": norm_bias, "qkv_weight": qkv_weight, "qkv_bias": qkv_bias, "out_weight": out_weight, "gate_weight": gate_weight, "up_weight": up_weight, "down_weight": down_weight, "cotangent": cotangent}


@jax.custom_vjp
def low(v):
    return lax.optimization_barrier(v.astype(jnp.bfloat16)).astype(jnp.float32)

@jax.custom_vjp
def low_back(v):
    return v

def low_keep(v):
    return (low(v), None)

def low_pass(kept, grad):
    return (grad,)

def back_keep(v):
    return (v, None)

def back_low(kept, grad):
    return (low(grad),)
low.defvjp(low_keep, low_pass)
low_back.defvjp(back_keep, back_low)
HIGHEST = lax.Precision.HIGHEST
EPSILON = 1e-05
NEGATIVE = -1e+30

def positions_of(segments):
    column = jnp.arange(segments.shape[0], dtype=jnp.int32)
    starts = jnp.concatenate([jnp.ones((1,), dtype=bool), segments[1:] != segments[:-1]])
    doc_start = lax.cummax(jnp.where(starts, column, 0), axis=0)
    return column - doc_start

def rotate(tensor, cosine, sine_table):
    half_rot = ROT // 2
    first_half = tensor[..., :half_rot]
    second_half = tensor[..., half_rot:ROT]
    return jnp.concatenate([first_half * cosine - second_half * sine_table, second_half * cosine + first_half * sine_table, tensor[..., ROT:]], axis=-1)

def layer(inputs, gain_full, norm_shift, qkv_w, qkv_b, out_w, gate_w, up_w, down_w, segments):
    length = inputs.shape[0]
    row_mean = lax.optimization_barrier(jnp.mean(inputs, -1, keepdims=True))
    centered = inputs - row_mean
    inverse_std = lax.rsqrt(lax.optimization_barrier(jnp.mean(centered * centered, -1, keepdims=True)) + EPSILON)
    normed = centered * inverse_std
    hidden_in = low(normed * gain_full + norm_shift)
    joined_qkv = low_back(jnp.dot(hidden_in, qkv_w, precision=HIGHEST) + qkv_b).reshape(length, H, 3, DH)
    positions = positions_of(segments)
    half_rot = ROT // 2
    frequency = jnp.power(10000.0, -2.0 * jnp.arange(half_rot, dtype=jnp.float32) / ROT)
    angles = positions.astype(jnp.float32)[:, None] * frequency[None, :]
    cosine = jnp.cos(angles)[:, None, :]
    sine_table = jnp.sin(angles)[:, None, :]
    queries = low(rotate(joined_qkv[:, :, 0], cosine, sine_table) * DH ** (-0.5))
    key_rows = low(rotate(joined_qkv[:, :, 1], cosine, sine_table))
    value_rows = low(joined_qkv[:, :, 2])
    block_rows = min(512, length)
    block_count = length // block_rows
    key_index = jnp.arange(length, dtype=jnp.int32)

    def attend_block(packed):
        query_block, segment_block, index_block = packed
        scores = low_back(jnp.einsum('qhd,khd->hqk', query_block, key_rows, precision=HIGHEST))
        allowed = (segment_block[:, None] == segments[None, :]) & (index_block[:, None] >= key_index[None, :])
        scores = jnp.where(allowed[None], scores, NEGATIVE)
        top_score = lax.optimization_barrier(jnp.max(scores, -1, keepdims=True))
        weights = jnp.exp(scores - top_score)
        probability = weights / lax.optimization_barrier(jnp.sum(weights, -1, keepdims=True))
        return jnp.einsum('hqk,khd->qhd', low(probability), value_rows, precision=HIGHEST)
    context = lax.map(jax.checkpoint(attend_block), (queries.reshape(block_count, block_rows, H, DH), segments.reshape(block_count, block_rows), key_index.reshape(block_count, block_rows)))
    context = low(low_back(context.reshape(length, H * DH)))
    attention_part = jnp.dot(context, out_w, precision=HIGHEST)
    gate_pre = low_back(jnp.dot(hidden_in, gate_w, precision=HIGHEST))
    up_pre = low_back(jnp.dot(hidden_in, up_w, precision=HIGHEST))
    mixed = low(jax.nn.silu(gate_pre) * up_pre)
    return inputs + attention_part + jnp.dot(mixed, down_w, precision=HIGHEST)

def reference(tokens, segment_ids, norm_gain, norm_bias, qkv_weight, qkv_bias, out_weight, gate_weight, up_weight, down_weight, cotangent):
    params = tuple((param.astype(jnp.float32) for param in (norm_gain, norm_bias, qkv_weight, qkv_bias, out_weight, gate_weight, up_weight, down_weight)))
    seq_tokens = tokens.reshape(NSEQ, LEN, D)
    seq_grads = cotangent.reshape(NSEQ, LEN, D)

    def one_sequence(totals, packed):
        token_rows, segments, grad_rows = packed

        def forward(inputs, gain_full, norm_shift, qkv_w, qkv_b, out_w, gate_w, up_w, down_w):
            return layer(inputs, gain_full, norm_shift, qkv_w, qkv_b, out_w, gate_w, up_w, down_w, segments)
        result, pullback = jax.vjp(forward, token_rows.astype(jnp.float32), params[0], params[1], params[2], params[3], params[4], params[5], params[6], params[7])
        grads = pullback(grad_rows.astype(jnp.float32))
        totals = tuple((total + grad for total, grad in zip(totals, grads[1:])))
        return (totals, (result.astype(jnp.bfloat16), grads[0].astype(jnp.bfloat16)))
    zeros_init = tuple((jnp.zeros_like(param) for param in params))
    totals, (outputs, grad_inputs) = lax.scan(one_sequence, zeros_init, (seq_tokens, segment_ids, seq_grads))
    return (outputs.reshape(TOKENS, D), grad_inputs.reshape(TOKENS, D), totals[0], totals[1], totals[2], totals[3], totals[4], totals[5], totals[6], totals[7])
```

```python
import functools

import jax
import jax.numpy as jnp
from jax import lax
from jax.experimental import pallas as pl
from jax.experimental.pallas import tpu as pltpu
from jax.sharding import PartitionSpec as P

DH = 64
ROT = 16


EPSILON = 1e-05
NEGATIVE = -1e30


def positions_of(segments):
    column = jnp.arange(segments.shape[1], dtype=jnp.int32)
    starts = jnp.concatenate(
        [jnp.ones((segments.shape[0], 1), dtype=bool), segments[:, 1:] != segments[:, :-1]], axis=1
    )
    doc_start = lax.cummax(jnp.where(starts, column[None, :], 0), axis=1)
    return column[None, :] - doc_start


def rotary_tables(positions):
    half_rot = ROT // 2
    frequency = jnp.power(10000.0, -2.0 * jnp.arange(half_rot, dtype=jnp.float32) / ROT)
    angles = positions.astype(jnp.float32)[:, None] * frequency[None, :]
    return (jnp.cos(angles)[:, None, :], jnp.sin(angles)[:, None, :])


def rotate(tensor, cosine, sine_table):
    half_rot = ROT // 2
    first_half = tensor[..., :half_rot]
    second_half = tensor[..., half_rot:ROT]
    return jnp.concatenate(
        [
            first_half * cosine - second_half * sine_table,
            second_half * cosine + first_half * sine_table,
            tensor[..., ROT:],
        ],
        axis=-1,
    )


def rotate_back(tensor, cosine, sine_table):
    half_rot = ROT // 2
    first_half = tensor[..., :half_rot]
    second_half = tensor[..., half_rot:ROT]
    return jnp.concatenate(
        [
            first_half * cosine + second_half * sine_table,
            second_half * cosine - first_half * sine_table,
            tensor[..., ROT:],
        ],
        axis=-1,
    )


def masked_scores(query_block, seq_keys, seq_segments, begin_row, block_rows):
    key_index = jnp.arange(seq_keys.shape[0], dtype=jnp.int32)
    allowed = (seq_segments[begin_row : begin_row + block_rows, None] == seq_segments[None, :]) & (
        key_index[:, None] >= key_index[None, :]
    )
    scores = jnp.einsum("qhd,khd->hqk", query_block, seq_keys, preferred_element_type=jnp.float32)
    return jnp.where(allowed[None], scores, NEGATIVE)


def attend_forward(packed):
    seq_queries, seq_keys, seq_values, seq_segments = packed
    length = seq_queries.shape[0]
    block_rows = min(512, length)
    scores = masked_scores(seq_queries, seq_keys, seq_segments, 0, block_rows)
    top_score = jnp.max(scores, -1, keepdims=True)
    weights = jnp.exp(scores - top_score)
    denominator = jnp.sum(weights, -1, keepdims=True)
    probability = (weights / denominator).astype(jnp.bfloat16)
    contexts = [
        jnp.einsum("hqk,khd->qhd", probability, seq_values, preferred_element_type=jnp.float32)
    ]
    log_totals = [top_score + jnp.log(denominator)]
    return (jnp.concatenate(contexts, 0), jnp.concatenate(log_totals, 1))


def attend_backward(packed):
    seq_queries, seq_keys, seq_values, seq_segments, seq_log_total, seq_grad_context = packed
    length = seq_queries.shape[0]
    block_rows = min(512, length)
    grad_keys = jnp.zeros(seq_keys.shape, jnp.float32)
    grad_values = jnp.zeros(seq_values.shape, jnp.float32)
    scores = masked_scores(seq_queries, seq_keys, seq_segments, 0, block_rows)
    probability = jnp.exp(scores - seq_log_total[:, 0:block_rows])
    grad_prob = jnp.einsum(
        "qhd,khd->hqk", seq_grad_context, seq_values, preferred_element_type=jnp.float32
    )
    row_dot = jnp.sum(probability * grad_prob, -1, keepdims=True)
    grad_scores = (probability * (grad_prob - row_dot)).astype(jnp.bfloat16)
    grad_queries = [
        jnp.einsum("hqk,khd->qhd", grad_scores, seq_keys, preferred_element_type=jnp.float32)
    ]
    grad_keys = grad_keys + jnp.einsum(
        "hqk,qhd->khd", grad_scores, seq_queries, preferred_element_type=jnp.float32
    )
    grad_values = grad_values + jnp.einsum(
        "hqk,qhd->khd",
        probability.astype(jnp.bfloat16),
        seq_grad_context,
        preferred_element_type=jnp.float32,
    )
    return (jnp.concatenate(grad_queries, 0), grad_keys, grad_values)


def contract_rows(left_side, right_side):
    return lax.dot_general(
        left_side, right_side, (((0,), (0,)), ((), ())), preferred_element_type=jnp.float32
    )


def contract_cols(left_side, right_side):
    return lax.dot_general(
        left_side, right_side, (((1,), (1,)), ((), ())), preferred_element_type=jnp.float32
    )


def norm_back(grad_normed_out, normed, inverse_std, gain_full):
    grad_normed = grad_normed_out * gain_full
    return inverse_std * (
        grad_normed
        - jnp.mean(grad_normed, -1, keepdims=True)
        - normed * jnp.mean(grad_normed * normed, -1, keepdims=True)
    )


def local(
    tokens,
    segment_ids,
    norm_gain,
    norm_bias,
    qkv_weight,
    qkv_bias,
    out_weight,
    gate_weight,
    up_weight,
    down_weight,
    cotangent,
):
    row_count = tokens.shape[0]
    seq_count, length = segment_ids.shape
    head_count = qkv_weight.shape[1] // (3 * DH)
    score_scale = DH ** (-0.5)
    inputs = tokens.astype(jnp.float32)
    row_mean = jnp.mean(inputs, -1, keepdims=True)
    centered = inputs - row_mean
    inverse_std = lax.rsqrt(jnp.mean(centered * centered, -1, keepdims=True) + EPSILON)
    normed = centered * inverse_std
    gain_full = norm_gain.astype(jnp.float32)
    hidden_in = (normed * gain_full + norm_bias.astype(jnp.float32)).astype(jnp.bfloat16)
    joined_qkv = (
        jnp.dot(hidden_in, qkv_weight, preferred_element_type=jnp.float32)
        + qkv_bias.astype(jnp.float32)
    ).reshape(row_count, head_count, 3, DH)
    positions = positions_of(segment_ids).reshape(row_count)
    cosine, sine_table = rotary_tables(positions)
    queries = (rotate(joined_qkv[:, :, 0], cosine, sine_table) * score_scale).astype(jnp.bfloat16)
    key_rows = rotate(joined_qkv[:, :, 1], cosine, sine_table).astype(jnp.bfloat16)
    value_rows = joined_qkv[:, :, 2].astype(jnp.bfloat16)
    seq_shape = (seq_count, length, head_count, DH)
    seq_queries = queries.reshape(seq_shape)
    seq_keys = key_rows.reshape(seq_shape)
    seq_values = value_rows.reshape(seq_shape)
    context, log_total = lax.map(attend_forward, (seq_queries, seq_keys, seq_values, segment_ids))
    context = context.reshape(row_count, head_count * DH).astype(jnp.bfloat16)
    gate_pre = jnp.dot(hidden_in, gate_weight, preferred_element_type=jnp.float32)
    up_pre = jnp.dot(hidden_in, up_weight, preferred_element_type=jnp.float32)
    sigmoid_gate = jax.nn.sigmoid(gate_pre)
    activated = gate_pre * sigmoid_gate
    mixed = (activated * up_pre).astype(jnp.bfloat16)
    partial_out = jnp.dot(context, out_weight, preferred_element_type=jnp.float32) + jnp.dot(
        mixed, down_weight, preferred_element_type=jnp.float32
    )
    summed = lax.psum(partial_out, "tensor")
    output = (inputs + summed).astype(jnp.bfloat16)
    grad_context = contract_cols(cotangent, out_weight).astype(jnp.bfloat16)
    grad_out_w = contract_rows(context, cotangent)
    grad_down_w = contract_rows(mixed, cotangent)
    grad_out_part, grad_down_part = (
        lax.psum_scatter(grad_out_w, "dp", scatter_dimension=1, tiled=True),
        lax.psum_scatter(grad_down_w, "dp", scatter_dimension=1, tiled=True),
    )
    grad_mixed = contract_cols(cotangent, down_weight)
    grad_up = (grad_mixed * activated).astype(jnp.bfloat16)
    grad_gate = (
        grad_mixed * up_pre * sigmoid_gate * (1.0 + gate_pre * (1.0 - sigmoid_gate))
    ).astype(jnp.bfloat16)
    grad_gate_w = contract_rows(hidden_in, grad_gate)
    grad_up_w = contract_rows(hidden_in, grad_up)
    grad_hidden = contract_cols(grad_gate, gate_weight) + contract_cols(grad_up, up_weight)
    grad_queries, grad_keys, grad_values = lax.map(
        attend_backward,
        (
            seq_queries,
            seq_keys,
            seq_values,
            segment_ids,
            log_total,
            grad_context.reshape(seq_shape),
        ),
    )
    flat_shape = (row_count, head_count, DH)
    grad_queries = rotate_back(grad_queries.reshape(flat_shape) * score_scale, cosine, sine_table)
    grad_keys = rotate_back(grad_keys.reshape(flat_shape), cosine, sine_table)
    grad_joined = (
        jnp.stack([grad_queries, grad_keys, grad_values.reshape(flat_shape)], axis=2)
        .reshape(row_count, head_count * 3 * DH)
        .astype(jnp.bfloat16)
    )
    bias_local = jnp.sum(grad_joined.astype(jnp.float32), 0)
    grad_qkv_w = contract_rows(hidden_in, grad_joined)
    grad_hidden = grad_hidden + contract_cols(grad_joined, qkv_weight)
    grad_qkv_part, grad_gate_part, grad_up_part = (
        lax.psum_scatter(grad_qkv_w, "dp", scatter_dimension=0, tiled=True),
        lax.psum_scatter(grad_gate_w, "dp", scatter_dimension=0, tiled=True),
        lax.psum_scatter(grad_up_w, "dp", scatter_dimension=0, tiled=True),
    )
    grad_total = lax.psum(grad_hidden, "tensor")
    grad_input = (
        cotangent.astype(jnp.float32) + norm_back(grad_total, normed, inverse_std, gain_full)
    ).astype(jnp.bfloat16)
    grad_gain, grad_shift, grad_bias = lax.psum(
        (jnp.sum(grad_total * normed, 0), jnp.sum(grad_total, 0), bias_local), "dp"
    )
    return (
        output,
        grad_input,
        grad_gain,
        grad_shift,
        grad_qkv_part,
        grad_bias,
        grad_out_part,
        grad_gate_part,
        grad_up_part,
        grad_down_part,
    )


BF = jnp.bfloat16
F32 = jnp.float32
MESH = pl.DeviceIdType.MESH
W = 256
PR = 32


def comm_kernel(
    dims,
    hid_h, cot_h, tok_h, ctx_h, gj_h, gain_ref, bias_ref, qkv_h, out_h, gate_h, up_h, down_h,
    out_o, gin_o, sv_o, sums_o,
    hid_t, cot, cot_s, tok, ctx, gj, w_a, w_b, w_d, acc, gu, s1, own, recv1, recv2, recv3,
    zs, ze, zm, stage, svb, svr,
    ld_sem, w_sem, s1_send, s1_recv, s2_send, s2_recv, s3_send, s3_recv,
    e_send, e_recv, m_send, m_recv, o_send, o_recv, o_loc, st_sem, v_send, v_recv,
):
    rows, width, full, tail, n_out, n_qkv, n_batch = dims
    n_piece = rows // PR
    hid = zs.at[1]
    dp = lax.axis_index("dp")
    zi = lax.axis_index("tensor")
    c = lax.rem(dp, 2)
    x = lax.rem(dp // 2, 2)
    y = dp // 4
    core_dev = {"dp": dp + 1 - 2 * c}
    x_dev = {"dp": dp + 2 - 4 * x}
    y_dev = {"dp": dp + 4 - 8 * y}
    is_mid = (zi == 1) | (zi == 2)
    is_end = (zi == 0) | (zi == 3)
    end_of = jnp.where(zi == 1, 0, 3)
    mid_of_end = jnp.where(zi == 0, 1, 2)
    end_dev = {"tensor": end_of}
    mid_dev = {"tensor": mid_of_end}
    other_mid = {"tensor": 3 - zi}

    def load(src, dst, k):
        return pltpu.make_async_copy(src, dst, ld_sem.at[k])

    def w_out(j):
        return pltpu.make_async_copy(out_h.at[pl.ds(j * W, W), :], w_d, w_sem.at[2])

    def w_down(i):
        return pltpu.make_async_copy(down_h.at[pl.ds(i * W, W), :], w_d, w_sem.at[2])

    def w_gate(i):
        return pltpu.make_async_copy(gate_h.at[:, pl.ds(i * W, W)], w_a, w_sem.at[0])

    def w_up(i):
        return pltpu.make_async_copy(up_h.at[:, pl.ds(i * W, W)], w_b, w_sem.at[1])

    def w_qkv(j):
        return pltpu.make_async_copy(qkv_h.at[:, pl.ds(j * W, W)], w_a, w_sem.at[0])

    t0 = full * W
    w_gate_t = pltpu.make_async_copy(gate_h.at[:, pl.ds(t0, tail)], w_a.at[:, 0:tail], w_sem.at[0])
    w_up_t = pltpu.make_async_copy(up_h.at[:, pl.ds(t0, tail)], w_a.at[:, tail : 2 * tail], w_sem.at[1])
    w_down_t = pltpu.make_async_copy(down_h.at[pl.ds(t0, tail), :], w_d.at[0:tail, :], w_sem.at[2])

    ctx_ld = load(ctx_h, ctx, 0)
    hid_ld = load(hid_h, hid, 1)
    cot_ld = load(cot_h, cot, 2)
    gj_ld = load(gj_h, gj, 3)
    tok_ld = load(tok_h, tok, 4)
    cs_ld = [
        load(cot_h.at[:, (2 * q + s) * W : (2 * q + s + 1) * W], cot_s.at[s, :, q * W : (q + 1) * W], 5 + 2 * q + s)
        for q in range(4)
        for s in range(2)
    ]
    ctx_ld.start()
    w_out(0).start()
    for cp in cs_ld:
        cp.start()
    hid_ld.start()
    w_gate(0).start()
    w_up(0).start()
    cot_ld.start()
    gj_ld.start()
    tok_ld.start()

    barrier = pltpu.get_barrier_semaphore()
    for dev in (core_dev, x_dev, y_dev):
        pl.semaphore_signal(barrier, inc=1, device_id=dev, device_id_type=MESH)

    @pl.when(is_mid)
    def _():
        pl.semaphore_signal(barrier, inc=1, device_id=end_dev, device_id_type=MESH)
        pl.semaphore_signal(barrier, inc=1, device_id=other_mid, device_id_type=MESH)

    @pl.when(is_end)
    def _():
        pl.semaphore_signal(barrier, inc=1, device_id=mid_dev, device_id_type=MESH)

    pl.semaphore_wait(barrier, jnp.where(is_mid, 5, 4))

    def rdma(src, dst, send, recv, dev):
        return pltpu.make_async_remote_copy(
            src_ref=src, dst_ref=dst, send_sem=send, recv_sem=recv, device_id=dev, device_id_type=MESH
        )

    def c1(b):
        slot = lax.rem(b, 4)
        return rdma(s1.at[slot], recv1.at[b], s1_send.at[slot], s1_recv.at[b], core_dev)

    def c2(b, h):
        if h == 0:
            return rdma(recv1.at[b, :, 1 - x, 0], recv2.at[b, 0], s2_send.at[b, 0], s2_recv.at[b, 0], x_dev)
        return rdma(recv1.at[b, 1 - y, :, 1], recv2.at[b, 1], s2_send.at[b, 1], s2_recv.at[b, 1], y_dev)

    def c3(b, h):
        if h == 0:
            return rdma(recv2.at[b, 0, 1 - y], recv3.at[b, 0], s3_send.at[b, 0], s3_recv.at[b, 0], y_dev)
        return rdma(recv2.at[b, 1, 1 - x], recv3.at[b, 1], s3_send.at[b, 1], s3_recv.at[b, 1], x_dev)

    def up32(v):
        return v.astype(F32)

    def ev1(b):
        slot = lax.rem(b, 4)
        c1(b).wait_recv()
        for yy in range(2):
            for xx in range(2):
                for h in range(2):
                    v = up32(recv1[b, yy, xx, h]) + up32(own[slot, yy, xx, h])
                    recv1[b, yy, xx, h] = v.astype(BF)
        c2(b, 0).start()
        c2(b, 1).start()

    def ev2(b):
        c2(b, 0).wait_recv()
        c2(b, 1).wait_recv()
        for k in range(2):
            v = up32(recv2[b, 0, k]) + up32(recv1[b, k, x, 0])
            recv2[b, 0, k] = v.astype(BF)
            v = up32(recv2[b, 1, k]) + up32(recv1[b, y, k, 1])
            recv2[b, 1, k] = v.astype(BF)
        c3(b, 0).start()
        c3(b, 1).start()

    def st_copy(b):
        slot = lax.rem(b, 2)
        return pltpu.make_async_copy(stage.at[slot], sums_o.at[b], st_sem.at[slot])

    def ev3(b):
        slot = lax.rem(b, 2)
        c3(b, 0).wait_recv()
        c3(b, 1).wait_recv()

        @pl.when(b >= 2)
        def _():
            st_copy(b - 2).wait()

        stage[slot, 0] = up32(recv2[b, 0, y]) + up32(recv3[b, 0])
        stage[slot, 1] = up32(recv2[b, 1, x]) + up32(recv3[b, 1])
        st_copy(b).start()

    def before_put(b):
        @pl.when(b >= 4)
        def _():
            c1(b - 4).wait_send()

    def after_put(b):
        c1(b).start()

        @pl.when(b >= 2)
        def _():
            ev1(b - 2)

    def put_rows(b, grad):
        slot = lax.rem(b, 4)
        before_put(b)
        for part, dst in ((1 - c, s1), (c, own)):
            left = hid_t[:, part].reshape(4 * W, rows)
            res = jnp.dot(left, grad, preferred_element_type=F32).astype(BF)
            dst[slot] = res.reshape(2, 2, 2, W // 2, W)
        after_put(b)

    def put_cols(b, left_t):
        slot = lax.rem(b, 4)
        h = left_t.shape[0]
        before_put(b)
        for part, dst in ((1 - c, s1), (c, own)):
            res = jnp.dot(left_t, cot_s[part], preferred_element_type=F32).astype(BF)
            for q in range(4):
                piece = res[:, q * W : (q + 1) * W].reshape(2, h // 2, W)
                dst[slot, q // 2, q % 2, :, 0 : h // 2, :] = piece
                if h < W:
                    dst[slot, q // 2, q % 2, :, h // 2 :, :] = jnp.zeros((2, (W - h) // 2, W), BF)
        after_put(b)

    NB = 512

    def acc_cols(left, w_ref, k, first):
        for n in range(width // NB):
            cols = slice(n * NB, (n + 1) * NB)
            res = jnp.dot(left, w_ref[0:k, cols], preferred_element_type=F32)
            if first:
                acc[:, cols] = res
            else:
                acc[:, cols] += res

    def acc_rows(grad, w_ref):
        for n in range(width // NB):
            cols = slice(n * NB, (n + 1) * NB)
            acc[:, cols] += lax.dot_general(
                grad, w_ref[cols, :], (((1,), (1,)), ((), ())), preferred_element_type=F32
            )

    def z_rows(p):
        return pl.ds(pl.multiple_of(p * PR, PR), PR)

    def ce(a, p):
        i = a * n_piece + p
        return rdma(zs.at[a, z_rows(p)], ze.at[a, z_rows(p)], e_send.at[i], e_recv.at[i], mid_dev)

    def cm(a, p):
        i = a * n_piece + p
        return rdma(zs.at[a, z_rows(p)], zm.at[a, z_rows(p)], m_send.at[i], m_recv.at[i], other_mid)

    def co(a, p, ref):
        i = a * n_piece + p
        return rdma(ze.at[a, z_rows(p)], ref.at[z_rows(p)], o_send.at[i], o_recv.at[i], end_dev)

    def cl(a, p, ref):
        i = a * n_piece + p
        return pltpu.make_async_copy(ze.at[a, z_rows(p)], ref.at[z_rows(p)], o_loc.at[i])

    def ev_e(e):
        a, p = e // n_piece, lax.rem(e, n_piece)

        @pl.when(is_mid)
        def _():
            ce(a, p).wait_recv()
            r = z_rows(p)
            zs[a, r, :] = (up32(zs[a, r, :]) + up32(ze[a, r, :])).astype(BF)
            cm(a, p).start()

    def norm_rows(r):
        v = up32(tok[r, :])
        mu = jnp.mean(v, -1, keepdims=True)
        v = v - mu
        inv = lax.rsqrt(jnp.mean(v * v, -1, keepdims=True) + EPSILON)
        return v * inv, inv

    def ev_m(e):
        a, p = e // n_piece, lax.rem(e, n_piece)

        @pl.when(is_mid)
        def _():
            cm(a, p).wait_recv()
            r = z_rows(p)

            @pl.when(a == 0)
            def _():
                total = up32(zs[0, r, :]) + up32(zm[0, r, :])
                ze[0, r, :] = (up32(tok[r, :]) + total).astype(BF)
                co(0, p, out_o).start()
                cl(0, p, out_o).start()

            @pl.when(a == 1)
            def _():
                total = up32(zs[1, r, :]) + up32(zm[1, r, :])
                normed, inv = norm_rows(r)
                back = norm_back(total, normed, inv, gain_ref[...].astype(F32))
                ze[1, r, :] = (up32(cot[r, :]) + back).astype(BF)
                co(1, p, gin_o).start()
                cl(1, p, gin_o).start()

    ctx_ld.wait()
    for cp in cs_ld:
        cp.wait()
    for j in range(n_out):
        left = ctx[:, j * W : (j + 1) * W]
        w_out(j).wait()
        acc_cols(left, w_d, W, j == 0)
        if j + 1 < n_out:
            w_out(j + 1).start()
        else:
            w_down(0).start()
        put_cols(jnp.int32(j), left.T)
    hid_ld.wait()
    for q in range(4):
        for s in range(2):
            lo = (2 * q + s) * W
            hid_t[q, s] = hid[:, lo : lo + W].T

    def act_of(g, u):
        return (g * jax.nn.sigmoid(g) * u).astype(BF)

    def fwd(i, keep):
        w_gate(i).wait()
        g = jnp.dot(hid[...], w_a[...], preferred_element_type=F32)
        w_up(i).wait()
        u = jnp.dot(hid[...], w_b[...], preferred_element_type=F32)

        @pl.when(i + 1 < full)
        def _():
            w_gate(i + 1).start()
            w_up(i + 1).start()

        @pl.when(i + 1 == full)
        def _():
            w_gate_t.start()
            w_up_t.start()

        gu[i, 0] = g.astype(BF)
        gu[i, 1] = u.astype(BF)
        mixed = act_of(g, u)
        w_down(i).wait()
        acc_cols(mixed, w_d, W, False)

        @pl.when(i + 1 < full)
        def _():
            w_down(i + 1).start()

        @pl.when(i + 1 == full)
        def _():
            w_down_t.start()

        put_cols(n_out + i, mixed.T)
        return keep

    lax.fori_loop(0, full, fwd, 0)
    w_gate_t.wait()
    w_up_t.wait()
    both = jnp.dot(hid[...], w_a[...], preferred_element_type=F32)
    gj_ld.wait()
    w_qkv(0).start()
    gu[full, 0] = both.astype(BF)
    mixed = act_of(both[:, 0:tail], both[:, tail:])
    w_down_t.wait()
    acc_cols(mixed, w_d, tail, False)
    w_down(0).start()
    b0 = n_out + full

    tok_ld.wait()
    cot_ld.wait()

    def to_line(a):
        def step(p, keep):
            r = z_rows(p)
            v = acc[r, :]
            zs[a, r, :] = v.astype(BF)
            if a == 0:
                acc[r, :] = jnp.zeros_like(v)
            else:
                normed, _inv = norm_rows(r)
                svb[0, 0:1, :] += jnp.sum(v * normed, 0, keepdims=True)
                svb[0, 1:2, :] += jnp.sum(v, 0, keepdims=True)

            @pl.when(is_end)
            def _():
                ce(a, p).start()

            return keep

        lax.fori_loop(0, n_piece, step, 0)

    to_line(0)
    put_cols(jnp.int32(b0), mixed.T)
    b0 = b0 + 1

    def joined(j, keep):
        grad = gj[j]
        w_qkv(j).wait()
        acc_rows(grad, w_a)

        @pl.when(j + 1 < n_qkv)
        def _():
            w_qkv(j + 1).start()

        @pl.when(j + 1 == n_qkv)
        def _():
            w_gate(0).start()
            w_up(0).start()

        put_rows(b0 + j, grad)
        return keep

    lax.fori_loop(0, n_qkv, joined, 0)
    b1 = b0 + n_qkv

    def gate_grads(gm, g, u):
        sg = jax.nn.sigmoid(g)
        g_up = (gm * (g * sg)).astype(BF)
        g_gate = (gm * u * sg * (1.0 + g * (1.0 - sg))).astype(BF)
        return g_gate, g_up

    def cols_t(left, w_ref, k):
        return lax.dot_general(left, w_ref[0:k, :], (((1,), (1,)), ((), ())), preferred_element_type=F32)

    def bwd(i, keep):
        w_down(i).wait()
        gm = cols_t(cot[...], w_d, W)

        @pl.when(i + 1 < full)
        def _():
            w_down(i + 1).start()

        @pl.when(i + 1 == full)
        def _():
            w_down_t.start()

        g_gate, g_up = gate_grads(gm, up32(gu[i, 0]), up32(gu[i, 1]))
        w_gate(i).wait()
        acc_rows(g_gate, w_a)
        w_up(i).wait()
        acc_rows(g_up, w_b)

        @pl.when(i + 1 < full)
        def _():
            w_gate(i + 1).start()
            w_up(i + 1).start()

        @pl.when(i + 1 == full)
        def _():
            w_gate_t.start()
            w_up_t.start()

        put_rows(b1 + 2 * i, g_gate)
        put_rows(b1 + 2 * i + 1, g_up)
        ev_e(i)

        @pl.when(i >= 2)
        def _():
            ev_m(i - 2)

        return keep

    lax.fori_loop(0, full, bwd, 0)
    w_down_t.wait()
    gm = cols_t(cot[...], w_d, tail)
    both = up32(gu[full, 0])
    g_gate, g_up = gate_grads(gm, both[:, 0:tail], both[:, tail:])
    both = jnp.concatenate([g_gate, g_up], axis=1)
    w_gate_t.wait()
    w_up_t.wait()
    acc_rows(both, w_a)
    svb[0] = jnp.zeros_like(svb[0])
    svb[0, 2:3, 0 : n_qkv * W] = bias_ref[...]
    to_line(1)
    b2 = b1 + 2 * full
    put_rows(jnp.int32(b2), both)
    ev1(jnp.int32(b2 - 1))
    ev1(jnp.int32(b2))

    def cv(k, dev):
        return rdma(svb.at[k], svr.at[k], v_send.at[k], v_recv.at[k], dev)

    for k, dev in enumerate((core_dev, x_dev, y_dev)):
        cp = cv(k, dev)
        cp.start()
        cp.wait_recv()
        svb[k + 1] = svb[k] + svr[k]

    @pl.when(is_end)
    def _():
        cv(3, mid_dev).start()

    first_e = full
    first_m = full - 2
    n_e = 2 * n_piece

    def drain(k, keep):
        @pl.when(k + first_e < n_e)
        def _():
            ev_e(k + first_e)

        @pl.when(k < n_batch)
        def _():
            ev2(k)

        @pl.when(k + first_m < n_e)
        def _():
            ev_m(k + first_m)

        @pl.when((k >= 3) & (k - 3 < n_batch))
        def _():
            ev3(k - 3)

        return keep

    lax.fori_loop(0, max(n_batch + 3, n_e - first_m), drain, 0)

    @pl.when(is_mid)
    def _():
        cv(3, end_dev).wait_recv()
        svb[4] = svb[3] + svr[3]
        cp = cv(4, other_mid)
        cp.start()
        cp.wait_recv()
        svb[5] = svb[4] + svr[4]
        last = cv(5, end_dev)
        last.start()
        sv_o[0:2, :] = svb[5, 0:2, :]
        cp.wait_send()
        last.wait_send()

    @pl.when(is_end)
    def _():
        cv(3, mid_dev).wait_send()
        cv(5, mid_dev).wait_recv()
        sv_o[0:2, :] = svr[5, 0:2, :]

    sv_o[2:8, :] = svb[3, 2:8, :]

    for k, dev in enumerate((core_dev, x_dev, y_dev)):
        cv(k, dev).wait_send()

    def finish(b, keep):
        for h in range(2):
            c2(b, h).wait_send()
            c3(b, h).wait_send()
        return keep

    lax.fori_loop(0, n_batch, finish, 0)
    for k in range(4):
        c1(jnp.int32(n_batch - 4 + k)).wait_send()
    for k in range(2):
        st_copy(jnp.int32(n_batch - 2 + k)).wait()

    def finish_line(p, keep):
        for a, ref in ((0, out_o), (1, gin_o)):
            @pl.when(is_mid)
            def _():
                cm(a, p).wait_send()
                co(a, p, ref).wait_send()
                cl(a, p, ref).wait()

            @pl.when(is_end)
            def _():
                ce(a, p).wait_send()
                co(a, p, ref).wait_recv()

        return keep

    lax.fori_loop(0, n_piece, finish_line, 0)


def comm_call(hidden, cot, tokens, ctx, gj, gain, bias_sum, qkv_w, out_w, gate_w, up_w, down_w):
    rows, width = hidden.shape
    hd = ctx.shape[1]
    ff = gate_w.shape[1]
    full, tail = ff // W, ff % W
    n_out, n_qkv = hd // W, qkv_w.shape[1] // W
    n_batch = n_out + full + 1 + n_qkv + 2 * full + 1
    n_z = 2 * (rows // PR)
    dims = (rows, width, full, tail, n_out, n_qkv, n_batch)
    piece = (W // 2, W)
    vm, dma = pltpu.VMEM, pltpu.SemaphoreType.DMA
    any_spec = pl.BlockSpec(memory_space=pl.ANY)
    vm_spec = pl.BlockSpec(memory_space=pltpu.VMEM)
    gj3 = gj.reshape(rows, n_qkv, W).transpose(1, 0, 2)
    return pl.pallas_call(
        functools.partial(comm_kernel, dims),
        out_shape=(
            jax.ShapeDtypeStruct((rows, width), BF),
            jax.ShapeDtypeStruct((rows, width), BF),
            jax.ShapeDtypeStruct((8, width), F32),
            jax.ShapeDtypeStruct((n_batch, 2) + piece, F32),
        ),
        in_specs=[any_spec] * 5 + [vm_spec] * 2 + [any_spec] * 5,
        out_specs=(any_spec, any_spec, vm_spec, any_spec),
        scratch_shapes=[
            vm((4, 2, W, rows), BF),
            vm((rows, width), BF),
            vm((2, rows, width // 2), BF),
            vm((rows, width), BF),
            vm((rows, hd), BF),
            vm((n_qkv, rows, W), BF),
            vm((width, W), BF),
            vm((width, W), BF),
            vm((W, width), BF),
            vm((rows, width), F32),
            vm((full + 1, 2, rows, W), BF),
            vm((4, 2, 2, 2) + piece, BF),
            vm((4, 2, 2, 2) + piece, BF),
            vm((n_batch, 2, 2, 2) + piece, BF),
            vm((n_batch, 2, 2) + piece, BF),
            vm((n_batch, 2) + piece, BF),
            vm((2, rows, width), BF),
            vm((2, rows, width), BF),
            vm((2, rows, width), BF),
            vm((2, 2) + piece, F32),
            vm((6, 8, width), F32),
            vm((6, 8, width), F32),
            dma((13,)),
            dma((3,)),
            dma((4,)),
            dma((n_batch,)),
            dma((n_batch, 2)),
            dma((n_batch, 2)),
            dma((n_batch, 2)),
            dma((n_batch, 2)),
            dma((n_z,)),
            dma((n_z,)),
            dma((n_z,)),
            dma((n_z,)),
            dma((n_z,)),
            dma((n_z,)),
            dma((n_z,)),
            dma((2,)),
            dma((6,)),
            dma((6,)),
        ],
        compiler_params=pltpu.CompilerParams(
            collective_id=0, has_side_effects=True, vmem_limit_bytes=67043328
        ),
        name="ffn_and_sums",
    )(hidden, cot, tokens, ctx, gj3, gain[None, :], bias_sum[None, :], qkv_w, out_w, gate_w, up_w, down_w)


def fast(
    n_dp,
    n_tensor,
    tokens,
    segment_ids,
    norm_gain,
    norm_bias,
    qkv_weight,
    qkv_bias,
    out_weight,
    gate_weight,
    up_weight,
    down_weight,
    cotangent,
):
    args = (tokens, segment_ids, norm_gain, norm_bias, qkv_weight, qkv_bias, out_weight, gate_weight, up_weight, down_weight, cotangent)
    row_count, width = tokens.shape
    ff = gate_weight.shape[1]
    fits = (
        (n_dp, n_tensor) == (8, 4)
        and segment_ids.shape == (1, row_count)
        and (row_count, width) == (512, 8 * W)
        and ff % W == W // 2
        and qkv_weight.shape[1] % W == 0
        and out_weight.shape[0] % W == 0
    )
    if not fits:
        return local(*args)
    seq_count, length = segment_ids.shape
    head_count = qkv_weight.shape[1] // (3 * DH)
    score_scale = DH ** (-0.5)
    inputs = tokens.astype(jnp.float32)
    row_mean = jnp.mean(inputs, -1, keepdims=True)
    centered = inputs - row_mean
    inverse_std = lax.rsqrt(jnp.mean(centered * centered, -1, keepdims=True) + EPSILON)
    normed = centered * inverse_std
    gain_full = norm_gain.astype(jnp.float32)
    hidden_in = (normed * gain_full + norm_bias.astype(jnp.float32)).astype(jnp.bfloat16)
    joined_qkv = (
        jnp.dot(hidden_in, qkv_weight, preferred_element_type=jnp.float32)
        + qkv_bias.astype(jnp.float32)
    ).reshape(row_count, head_count, 3, DH)
    positions = positions_of(segment_ids).reshape(row_count)
    cosine, sine_table = rotary_tables(positions)
    queries = (rotate(joined_qkv[:, :, 0], cosine, sine_table) * score_scale).astype(jnp.bfloat16)
    key_rows = rotate(joined_qkv[:, :, 1], cosine, sine_table).astype(jnp.bfloat16)
    value_rows = joined_qkv[:, :, 2].astype(jnp.bfloat16)
    seq_shape = (seq_count, length, head_count, DH)
    seq_queries = queries.reshape(seq_shape)
    seq_keys = key_rows.reshape(seq_shape)
    seq_values = value_rows.reshape(seq_shape)
    context, log_total = lax.map(attend_forward, (seq_queries, seq_keys, seq_values, segment_ids))
    context = context.reshape(row_count, head_count * DH).astype(jnp.bfloat16)
    grad_context = contract_cols(cotangent, out_weight).astype(jnp.bfloat16)
    grad_queries, grad_keys, grad_values = lax.map(
        attend_backward,
        (seq_queries, seq_keys, seq_values, segment_ids, log_total, grad_context.reshape(seq_shape)),
    )
    flat_shape = (row_count, head_count, DH)
    grad_queries = rotate_back(grad_queries.reshape(flat_shape) * score_scale, cosine, sine_table)
    grad_keys = rotate_back(grad_keys.reshape(flat_shape), cosine, sine_table)
    grad_joined = (
        jnp.stack([grad_queries, grad_keys, grad_values.reshape(flat_shape)], axis=2)
        .reshape(row_count, head_count * 3 * DH)
        .astype(jnp.bfloat16)
    )
    bias_local = jnp.sum(grad_joined.astype(jnp.float32), 0)
    output, grad_input, small, sums = comm_call(
        hidden_in, cotangent, tokens, context, grad_joined, norm_gain, bias_local,
        qkv_weight, out_weight, gate_weight, up_weight, down_weight,
    )
    full, tail = ff // W, ff % W
    n_out, n_qkv = out_weight.shape[0] // W, qkv_weight.shape[1] // W
    n_batch = sums.shape[0]
    b0 = n_out + full
    b1 = b0 + 1 + n_qkv
    flat = sums.reshape(n_batch, W, W)

    def side(first, count, step):
        return [flat[first + step * i] for i in range(count)]

    last = flat[n_batch - 1]
    tail_down = sums[b0, :, : tail // 2, :].reshape(tail, W)
    return (
        output,
        grad_input,
        small[0],
        small[1],
        jnp.concatenate(side(b0 + 1, n_qkv, 1), 1),
        small[2, : n_qkv * W],
        jnp.concatenate(side(0, n_out, 1), 0),
        jnp.concatenate(side(b1, full, 2) + [last[:, :tail]], 1),
        jnp.concatenate(side(b1 + 1, full, 2) + [last[:, tail:]], 1),
        jnp.concatenate(side(n_out, full, 1) + [tail_down], 0),
    )


def solution(mesh):
    body = functools.partial(fast, mesh.shape["dp"], mesh.shape["tensor"])
    return jax.shard_map(
        body,
        mesh=mesh,
        in_specs=(
            P("dp", None),
            P("dp", None),
            P(),
            P(),
            P(None, "tensor"),
            P("tensor"),
            P("tensor", None),
            P(None, "tensor"),
            P(None, "tensor"),
            P("tensor", None),
            P("dp", None),
        ),
        out_specs=(
            P("dp", None),
            P("dp", None),
            P(),
            P(),
            P("dp", "tensor"),
            P("tensor"),
            P("tensor", "dp"),
            P("dp", "tensor"),
            P("dp", "tensor"),
            P("tensor", "dp"),
        ),
        check_vma=False,
    )
```

```python
import functools

import jax
import jax.numpy as jnp
from jax import lax
from jax.experimental import pallas as pl
from jax.experimental.pallas import tpu as pltpu
from jax.sharding import PartitionSpec as P

DH = 64
ROT = 16


EPSILON = 1e-05
NEGATIVE = -1e30


def positions_of(segments):
    column = jnp.arange(segments.shape[1], dtype=jnp.int32)
    starts = jnp.concatenate(
        [jnp.ones((segments.shape[0], 1), dtype=bool), segments[:, 1:] != segments[:, :-1]], axis=1
    )
    doc_start = lax.cummax(jnp.where(starts, column[None, :], 0), axis=1)
    return column[None, :] - doc_start


def rotary_tables(positions):
    half_rot = ROT // 2
    frequency = jnp.power(10000.0, -2.0 * jnp.arange(half_rot, dtype=jnp.float32) / ROT)
    angles = positions.astype(jnp.float32)[:, None] * frequency[None, :]
    return (jnp.cos(angles)[:, None, :], jnp.sin(angles)[:, None, :])


def rotate(tensor, cosine, sine_table):
    half_rot = ROT // 2
    first_half = tensor[..., :half_rot]
    second_half = tensor[..., half_rot:ROT]
    return jnp.concatenate(
        [
            first_half * cosine - second_half * sine_table,
            second_half * cosine + first_half * sine_table,
            tensor[..., ROT:],
        ],
        axis=-1,
    )


def rotate_back(tensor, cosine, sine_table):
    half_rot = ROT // 2
    first_half = tensor[..., :half_rot]
    second_half = tensor[..., half_rot:ROT]
    return jnp.concatenate(
        [
            first_half * cosine + second_half * sine_table,
            second_half * cosine - first_half * sine_table,
            tensor[..., ROT:],
        ],
        axis=-1,
    )


def masked_scores(query_block, seq_keys, seq_segments, begin_row, block_rows):
    key_index = jnp.arange(seq_keys.shape[0], dtype=jnp.int32)
    allowed = (seq_segments[begin_row : begin_row + block_rows, None] == seq_segments[None, :]) & (
        key_index[:, None] >= key_index[None, :]
    )
    scores = jnp.einsum("qhd,khd->hqk", query_block, seq_keys, preferred_element_type=jnp.float32)
    return jnp.where(allowed[None], scores, NEGATIVE)


def attend_forward(packed):
    seq_queries, seq_keys, seq_values, seq_segments = packed
    length = seq_queries.shape[0]
    block_rows = min(512, length)
    scores = masked_scores(seq_queries, seq_keys, seq_segments, 0, block_rows)
    top_score = jnp.max(scores, -1, keepdims=True)
    weights = jnp.exp(scores - top_score)
    denominator = jnp.sum(weights, -1, keepdims=True)
    probability = (weights / denominator).astype(jnp.bfloat16)
    contexts = [
        jnp.einsum("hqk,khd->qhd", probability, seq_values, preferred_element_type=jnp.float32)
    ]
    log_totals = [top_score + jnp.log(denominator)]
    return (jnp.concatenate(contexts, 0), jnp.concatenate(log_totals, 1))


def attend_backward(packed):
    seq_queries, seq_keys, seq_values, seq_segments, seq_log_total, seq_grad_context = packed
    length = seq_queries.shape[0]
    block_rows = min(512, length)
    grad_keys = jnp.zeros(seq_keys.shape, jnp.float32)
    grad_values = jnp.zeros(seq_values.shape, jnp.float32)
    scores = masked_scores(seq_queries, seq_keys, seq_segments, 0, block_rows)
    probability = jnp.exp(scores - seq_log_total[:, 0:block_rows])
    grad_prob = jnp.einsum(
        "qhd,khd->hqk", seq_grad_context, seq_values, preferred_element_type=jnp.float32
    )
    row_dot = jnp.sum(probability * grad_prob, -1, keepdims=True)
    grad_scores = (probability * (grad_prob - row_dot)).astype(jnp.bfloat16)
    grad_queries = [
        jnp.einsum("hqk,khd->qhd", grad_scores, seq_keys, preferred_element_type=jnp.float32)
    ]
    grad_keys = grad_keys + jnp.einsum(
        "hqk,qhd->khd", grad_scores, seq_queries, preferred_element_type=jnp.float32
    )
    grad_values = grad_values + jnp.einsum(
        "hqk,qhd->khd",
        probability.astype(jnp.bfloat16),
        seq_grad_context,
        preferred_element_type=jnp.float32,
    )
    return (jnp.concatenate(grad_queries, 0), grad_keys, grad_values)


def contract_rows(left_side, right_side):
    return lax.dot_general(
        left_side, right_side, (((0,), (0,)), ((), ())), preferred_element_type=jnp.float32
    )


def contract_cols(left_side, right_side):
    return lax.dot_general(
        left_side, right_side, (((1,), (1,)), ((), ())), preferred_element_type=jnp.float32
    )


def norm_back(grad_normed_out, normed, inverse_std, gain_full):
    grad_normed = grad_normed_out * gain_full
    return inverse_std * (
        grad_normed
        - jnp.mean(grad_normed, -1, keepdims=True)
        - normed * jnp.mean(grad_normed * normed, -1, keepdims=True)
    )


def local(
    tokens,
    segment_ids,
    norm_gain,
    norm_bias,
    qkv_weight,
    qkv_bias,
    out_weight,
    gate_weight,
    up_weight,
    down_weight,
    cotangent,
):
    row_count = tokens.shape[0]
    seq_count, length = segment_ids.shape
    head_count = qkv_weight.shape[1] // (3 * DH)
    score_scale = DH ** (-0.5)
    inputs = tokens.astype(jnp.float32)
    row_mean = jnp.mean(inputs, -1, keepdims=True)
    centered = inputs - row_mean
    inverse_std = lax.rsqrt(jnp.mean(centered * centered, -1, keepdims=True) + EPSILON)
    normed = centered * inverse_std
    gain_full = norm_gain.astype(jnp.float32)
    hidden_in = (normed * gain_full + norm_bias.astype(jnp.float32)).astype(jnp.bfloat16)
    joined_qkv = (
        jnp.dot(hidden_in, qkv_weight, preferred_element_type=jnp.float32)
        + qkv_bias.astype(jnp.float32)
    ).reshape(row_count, head_count, 3, DH)
    positions = positions_of(segment_ids).reshape(row_count)
    cosine, sine_table = rotary_tables(positions)
    queries = (rotate(joined_qkv[:, :, 0], cosine, sine_table) * score_scale).astype(jnp.bfloat16)
    key_rows = rotate(joined_qkv[:, :, 1], cosine, sine_table).astype(jnp.bfloat16)
    value_rows = joined_qkv[:, :, 2].astype(jnp.bfloat16)
    seq_shape = (seq_count, length, head_count, DH)
    seq_queries = queries.reshape(seq_shape)
    seq_keys = key_rows.reshape(seq_shape)
    seq_values = value_rows.reshape(seq_shape)
    context, log_total = lax.map(attend_forward, (seq_queries, seq_keys, seq_values, segment_ids))
    context = context.reshape(row_count, head_count * DH).astype(jnp.bfloat16)
    gate_pre = jnp.dot(hidden_in, gate_weight, preferred_element_type=jnp.float32)
    up_pre = jnp.dot(hidden_in, up_weight, preferred_element_type=jnp.float32)
    sigmoid_gate = jax.nn.sigmoid(gate_pre)
    activated = gate_pre * sigmoid_gate
    mixed = (activated * up_pre).astype(jnp.bfloat16)
    partial_out = jnp.dot(context, out_weight, preferred_element_type=jnp.float32) + jnp.dot(
        mixed, down_weight, preferred_element_type=jnp.float32
    )
    summed = lax.psum(partial_out, "tensor")
    output = (inputs + summed).astype(jnp.bfloat16)
    grad_context = contract_cols(cotangent, out_weight).astype(jnp.bfloat16)
    grad_out_w = contract_rows(context, cotangent)
    grad_down_w = contract_rows(mixed, cotangent)
    grad_out_part, grad_down_part = (
        lax.psum_scatter(grad_out_w, "dp", scatter_dimension=1, tiled=True),
        lax.psum_scatter(grad_down_w, "dp", scatter_dimension=1, tiled=True),
    )
    grad_mixed = contract_cols(cotangent, down_weight)
    grad_up = (grad_mixed * activated).astype(jnp.bfloat16)
    grad_gate = (
        grad_mixed * up_pre * sigmoid_gate * (1.0 + gate_pre * (1.0 - sigmoid_gate))
    ).astype(jnp.bfloat16)
    grad_gate_w = contract_rows(hidden_in, grad_gate)
    grad_up_w = contract_rows(hidden_in, grad_up)
    grad_hidden = contract_cols(grad_gate, gate_weight) + contract_cols(grad_up, up_weight)
    grad_queries, grad_keys, grad_values = lax.map(
        attend_backward,
        (
            seq_queries,
            seq_keys,
            seq_values,
            segment_ids,
            log_total,
            grad_context.reshape(seq_shape),
        ),
    )
    flat_shape = (row_count, head_count, DH)
    grad_queries = rotate_back(grad_queries.reshape(flat_shape) * score_scale, cosine, sine_table)
    grad_keys = rotate_back(grad_keys.reshape(flat_shape), cosine, sine_table)
    grad_joined = (
        jnp.stack([grad_queries, grad_keys, grad_values.reshape(flat_shape)], axis=2)
        .reshape(row_count, head_count * 3 * DH)
        .astype(jnp.bfloat16)
    )
    bias_local = jnp.sum(grad_joined.astype(jnp.float32), 0)
    grad_qkv_w = contract_rows(hidden_in, grad_joined)
    grad_hidden = grad_hidden + contract_cols(grad_joined, qkv_weight)
    grad_qkv_part, grad_gate_part, grad_up_part = (
        lax.psum_scatter(grad_qkv_w, "dp", scatter_dimension=0, tiled=True),
        lax.psum_scatter(grad_gate_w, "dp", scatter_dimension=0, tiled=True),
        lax.psum_scatter(grad_up_w, "dp", scatter_dimension=0, tiled=True),
    )
    grad_total = lax.psum(grad_hidden, "tensor")
    grad_input = (
        cotangent.astype(jnp.float32) + norm_back(grad_total, normed, inverse_std, gain_full)
    ).astype(jnp.bfloat16)
    grad_gain, grad_shift, grad_bias = lax.psum(
        (jnp.sum(grad_total * normed, 0), jnp.sum(grad_total, 0), bias_local), "dp"
    )
    return (
        output,
        grad_input,
        grad_gain,
        grad_shift,
        grad_qkv_part,
        grad_bias,
        grad_out_part,
        grad_gate_part,
        grad_up_part,
        grad_down_part,
    )


BF = jnp.bfloat16
F32 = jnp.float32
MESH = pl.DeviceIdType.MESH
W = 256
PR = 32
SMALL_AT = 2


def comm_kernel(
    dims,
    hid_h, cot_h, tok_h, ctx_h, gj_h, gain_ref, bias_ref, qkv_h, out_h, gate_h, up_h, down_h,
    out_o, gin_o, sv_o, sums_o,
    hid_t, cot, cot_s, tok, ctx, gj, w_a, w_b, w_d, acc, gu, s1, own, recv1, recv2, recv3,
    zs, ze, zm, stage, svb, svr, svq,
    ld_sem, w_sem, s1_send, s1_recv, s2_send, s2_recv, s3_send, s3_recv,
    e_send, e_recv, m_send, m_recv, o_send, o_recv, o_loc, st_sem, v_send, v_recv,
):
    rows, width, full, tail, n_out, n_qkv, n_batch = dims
    n_piece = rows // PR
    hid = zs.at[1]
    dp = lax.axis_index("dp")
    zi = lax.axis_index("tensor")
    c = lax.rem(dp, 2)
    x = lax.rem(dp // 2, 2)
    y = dp // 4
    core_dev = {"dp": dp + 1 - 2 * c}
    x_dev = {"dp": dp + 2 - 4 * x}
    y_dev = {"dp": dp + 4 - 8 * y}
    is_mid = (zi == 1) | (zi == 2)
    is_end = (zi == 0) | (zi == 3)
    end_of = jnp.where(zi == 1, 0, 3)
    mid_of_end = jnp.where(zi == 0, 1, 2)
    end_dev = {"tensor": end_of}
    mid_dev = {"tensor": mid_of_end}
    other_mid = {"tensor": 3 - zi}

    def load(src, dst, k):
        return pltpu.make_async_copy(src, dst, ld_sem.at[k])

    def w_out(j):
        return pltpu.make_async_copy(out_h.at[pl.ds(j * W, W), :], w_d, w_sem.at[2])

    def w_down(i):
        return pltpu.make_async_copy(down_h.at[pl.ds(i * W, W), :], w_d, w_sem.at[2])

    def w_gate(i):
        return pltpu.make_async_copy(gate_h.at[:, pl.ds(i * W, W)], w_a, w_sem.at[0])

    def w_up(i):
        return pltpu.make_async_copy(up_h.at[:, pl.ds(i * W, W)], w_b, w_sem.at[1])

    def w_qkv(j):
        return pltpu.make_async_copy(qkv_h.at[:, pl.ds(j * W, W)], w_a, w_sem.at[0])

    t0 = full * W
    w_gate_t = pltpu.make_async_copy(gate_h.at[:, pl.ds(t0, tail)], w_a.at[:, 0:tail], w_sem.at[0])
    w_up_t = pltpu.make_async_copy(up_h.at[:, pl.ds(t0, tail)], w_a.at[:, tail : 2 * tail], w_sem.at[1])
    w_down_t = pltpu.make_async_copy(down_h.at[pl.ds(t0, tail), :], w_d.at[0:tail, :], w_sem.at[2])

    ctx_ld = load(ctx_h, ctx, 0)
    hid_ld = load(hid_h, hid, 1)
    cot_ld = load(cot_h, cot, 2)
    gj_ld = load(gj_h, gj, 3)
    tok_ld = load(tok_h, tok, 4)
    cs_ld = [
        load(cot_h.at[:, (2 * q + s) * W : (2 * q + s + 1) * W], cot_s.at[s, :, q * W : (q + 1) * W], 5 + 2 * q + s)
        for q in range(4)
        for s in range(2)
    ]
    ctx_ld.start()
    w_out(0).start()
    for cp in cs_ld:
        cp.start()
    hid_ld.start()
    w_gate(0).start()
    w_up(0).start()
    cot_ld.start()
    gj_ld.start()
    tok_ld.start()

    barrier = pltpu.get_barrier_semaphore()
    for dev in (core_dev, x_dev, y_dev, {"dp": dp + 2 - 4 * x + 4 - 8 * y}):
        pl.semaphore_signal(barrier, inc=1, device_id=dev, device_id_type=MESH)

    @pl.when(is_mid)
    def _():
        pl.semaphore_signal(barrier, inc=1, device_id=end_dev, device_id_type=MESH)
        pl.semaphore_signal(barrier, inc=1, device_id=other_mid, device_id_type=MESH)

    @pl.when(is_end)
    def _():
        pl.semaphore_signal(barrier, inc=1, device_id=mid_dev, device_id_type=MESH)

    pl.semaphore_wait(barrier, jnp.where(is_mid, 6, 5))

    def rdma(src, dst, send, recv, dev):
        return pltpu.make_async_remote_copy(
            src_ref=src, dst_ref=dst, send_sem=send, recv_sem=recv, device_id=dev, device_id_type=MESH
        )

    def c1(b):
        slot = lax.rem(b, 4)
        return rdma(s1.at[slot], recv1.at[b], s1_send.at[slot], s1_recv.at[b], core_dev)

    def c2(b, h):
        if h == 0:
            return rdma(recv1.at[b, :, 1 - x, 0], recv2.at[b, 0], s2_send.at[b, 0], s2_recv.at[b, 0], x_dev)
        return rdma(recv1.at[b, 1 - y, :, 1], recv2.at[b, 1], s2_send.at[b, 1], s2_recv.at[b, 1], y_dev)

    def c3(b, h):
        if h == 0:
            return rdma(recv2.at[b, 0, 1 - y], recv3.at[b, 0], s3_send.at[b, 0], s3_recv.at[b, 0], y_dev)
        return rdma(recv2.at[b, 1, 1 - x], recv3.at[b, 1], s3_send.at[b, 1], s3_recv.at[b, 1], x_dev)

    def up32(v):
        return v.astype(F32)

    def ev1(b):
        slot = lax.rem(b, 4)
        c1(b).wait_recv()
        for yy in range(2):
            for xx in range(2):
                for h in range(2):
                    recv1[b, yy, xx, h] += own[slot, yy, xx, h]
        c2(b, 0).start()
        c2(b, 1).start()

    def ev2(b):
        c2(b, 0).wait_recv()
        c2(b, 1).wait_recv()
        for k in range(2):
            recv2[b, 0, k] += recv1[b, k, x, 0]
            recv2[b, 1, k] += recv1[b, y, k, 1]
        c3(b, 0).start()
        c3(b, 1).start()

    def st_copy(b):
        slot = lax.rem(b, 2)
        return pltpu.make_async_copy(stage.at[slot], sums_o.at[b], st_sem.at[slot])

    def ev3(b):
        slot = lax.rem(b, 2)
        c3(b, 0).wait_recv()
        c3(b, 1).wait_recv()

        @pl.when(b >= 2)
        def _():
            st_copy(b - 2).wait()

        stage[slot, 0] = up32(recv2[b, 0, y]) + up32(recv3[b, 0])
        stage[slot, 1] = up32(recv2[b, 1, x]) + up32(recv3[b, 1])
        st_copy(b).start()

    def before_put(b):
        @pl.when(b >= 4)
        def _():
            c1(b - 4).wait_send()

    def after_put(b):
        c1(b).start()

        @pl.when(b >= 2)
        def _():
            ev1(b - 2)

    def put_rows(b, grad):
        slot = lax.rem(b, 4)
        before_put(b)
        for part, dst in ((1 - c, s1), (c, own)):
            left = hid_t[:, part].reshape(4 * W, rows)
            res = jnp.dot(left, grad, preferred_element_type=F32).astype(BF)
            dst[slot] = res.reshape(2, 2, 2, W // 2, W)
        after_put(b)

    def put_cols(b, left_t):
        slot = lax.rem(b, 4)
        h = left_t.shape[0]
        before_put(b)
        for part, dst in ((1 - c, s1), (c, own)):
            res = jnp.dot(left_t, cot_s[part], preferred_element_type=F32).astype(BF)
            for q in range(4):
                piece = res[:, q * W : (q + 1) * W].reshape(2, h // 2, W)
                dst[slot, q // 2, q % 2, :, 0 : h // 2, :] = piece
                if h < W:
                    dst[slot, q // 2, q % 2, :, h // 2 :, :] = jnp.zeros((2, (W - h) // 2, W), BF)
        after_put(b)

    NB = 512

    def acc_cols(left, w_ref, k, first):
        for n in range(width // NB):
            cols = slice(n * NB, (n + 1) * NB)
            res = jnp.dot(left, w_ref[0:k, cols], preferred_element_type=F32)
            if first:
                acc[:, cols] = res
            else:
                acc[:, cols] += res

    def acc_rows(grad, w_ref):
        for n in range(width // NB):
            cols = slice(n * NB, (n + 1) * NB)
            acc[:, cols] += lax.dot_general(
                grad, w_ref[cols, :], (((1,), (1,)), ((), ())), preferred_element_type=F32
            )

    def z_rows(p):
        return pl.ds(pl.multiple_of(p * PR, PR), PR)

    def ce(a, p):
        i = a * n_piece + p
        return rdma(zs.at[a, z_rows(p)], ze.at[a, z_rows(p)], e_send.at[i], e_recv.at[i], mid_dev)

    def cm(a, p):
        i = a * n_piece + p
        return rdma(zs.at[a, z_rows(p)], zm.at[a, z_rows(p)], m_send.at[i], m_recv.at[i], other_mid)

    def co(a, p, ref):
        i = a * n_piece + p
        return rdma(ze.at[a, z_rows(p)], ref.at[z_rows(p)], o_send.at[i], o_recv.at[i], end_dev)

    def cl(a, p, ref):
        i = a * n_piece + p
        return pltpu.make_async_copy(ze.at[a, z_rows(p)], ref.at[z_rows(p)], o_loc.at[i])

    def ev_e(e):
        a, p = e // n_piece, lax.rem(e, n_piece)

        @pl.when(is_mid)
        def _():
            ce(a, p).wait_recv()
            r = z_rows(p)
            zs[a, r, :] += ze[a, r, :]
            cm(a, p).start()

    def norm_rows(r):
        v = up32(tok[r, :])
        mu = jnp.mean(v, -1, keepdims=True)
        v = v - mu
        inv = lax.rsqrt(jnp.mean(v * v, -1, keepdims=True) + EPSILON)
        return v * inv, inv

    def ev_m(e):
        a, p = e // n_piece, lax.rem(e, n_piece)

        @pl.when(is_mid)
        def _():
            cm(a, p).wait_recv()
            r = z_rows(p)

            @pl.when(a == 0)
            def _():
                total = up32(zs[0, r, :]) + up32(zm[0, r, :])
                ze[0, r, :] = (up32(tok[r, :]) + total).astype(BF)
                co(0, p, out_o).start()
                cl(0, p, out_o).start()

            @pl.when(a == 1)
            def _():
                total = up32(zs[1, r, :]) + up32(zm[1, r, :])
                normed, inv = norm_rows(r)
                back = norm_back(total, normed, inv, gain_ref[...].astype(F32))
                ze[1, r, :] = (up32(cot[r, :]) + back).astype(BF)
                co(1, p, gin_o).start()
                cl(1, p, gin_o).start()

    ctx_ld.wait()
    for cp in cs_ld:
        cp.wait()
    for j in range(n_out):
        left = ctx[:, j * W : (j + 1) * W]
        w_out(j).wait()
        acc_cols(left, w_d, W, j == 0)
        if j + 1 < n_out:
            w_out(j + 1).start()
        else:
            w_down(0).start()
        put_cols(jnp.int32(j), left.T)
    hid_ld.wait()
    for q in range(4):
        for s in range(2):
            lo = (2 * q + s) * W
            hid_t[q, s] = hid[:, lo : lo + W].T

    def act_of(g, u):
        return (g * jax.nn.sigmoid(g) * u).astype(BF)

    def fwd(i, keep):
        w_gate(i).wait()
        g = jnp.dot(hid[...], w_a[...], preferred_element_type=F32)
        w_up(i).wait()
        u = jnp.dot(hid[...], w_b[...], preferred_element_type=F32)

        @pl.when(i + 1 < full)
        def _():
            w_gate(i + 1).start()
            w_up(i + 1).start()

        @pl.when(i + 1 == full)
        def _():
            w_gate_t.start()
            w_up_t.start()

        gu[i, 0] = g.astype(BF)
        gu[i, 1] = u.astype(BF)
        mixed = act_of(g, u)
        w_down(i).wait()
        acc_cols(mixed, w_d, W, False)

        @pl.when(i + 1 < full)
        def _():
            w_down(i + 1).start()

        @pl.when(i + 1 == full)
        def _():
            w_down_t.start()

        put_cols(n_out + i, mixed.T)
        return keep

    lax.fori_loop(0, full, fwd, 0)
    w_gate_t.wait()
    w_up_t.wait()
    both = jnp.dot(hid[...], w_a[...], preferred_element_type=F32)
    gj_ld.wait()
    w_qkv(0).start()
    gu[full, 0] = both.astype(BF)
    mixed = act_of(both[:, 0:tail], both[:, tail:])
    w_down_t.wait()
    acc_cols(mixed, w_d, tail, False)
    w_down(0).start()
    b0 = n_out + full

    tok_ld.wait()
    cot_ld.wait()

    def cv(k, dev):
        return rdma(svb.at[k], svr.at[k], v_send.at[k], v_recv.at[k], dev)

    def cw(k, dev):
        return rdma(svb.at[4], svq.at[y, x], v_send.at[4 + k], v_recv.at[4 + k], dev)

    square = (x_dev, y_dev, {"dp": dp + 2 - 4 * x + 4 - 8 * y})

    def small_1():
        @pl.when(is_mid)
        def _():
            cv(0, end_dev).wait_recv()
            svb[1] = svb[0] + svr[0]
            cv(1, other_mid).start()

    def small_2():
        @pl.when(is_mid)
        def _():
            cv(1, other_mid).wait_recv()
            svb[2] = svb[1] + svr[1]
            svb[3, 0:2, :] = svb[2, 0:2, :]
            cv(2, end_dev).start()

    def small_3():
        @pl.when(is_end)
        def _():
            cv(2, mid_dev).wait_recv()
            svb[3, 0:2, :] = svr[2, 0:2, :]

        svb[3, 2:8, :] = svb[0, 2:8, :]
        cv(3, core_dev).start()

    def small_4():
        cv(3, core_dev).wait_recv()
        svb[4] = svb[3] + svr[3]
        svq[y, x] = svb[4]
        for k, dev in enumerate(square):
            cw(k, dev).start()

    def small_5():
        for k, dev in enumerate(square):
            cw(k, dev).wait_recv()
        sv_o[...] = (svq[0, 0] + svq[0, 1]) + (svq[1, 0] + svq[1, 1])

    def small_sent():
        @pl.when(is_end)
        def _():
            cv(0, mid_dev).wait_send()

        @pl.when(is_mid)
        def _():
            cv(1, other_mid).wait_send()
            cv(2, end_dev).wait_send()

        cv(3, core_dev).wait_send()
        for k, dev in enumerate(square):
            cw(k, dev).wait_send()

    def to_line(a):
        def step(p, keep):
            r = z_rows(p)
            v = acc[r, :]
            zs[a, r, :] = v.astype(BF)
            if a == 0:
                acc[r, :] = jnp.zeros_like(v)
            else:
                normed, _inv = norm_rows(r)
                svb[0, 0:1, :] += jnp.sum(v * normed, 0, keepdims=True)
                svb[0, 1:2, :] += jnp.sum(v, 0, keepdims=True)

            return keep

        def send(p, keep):
            ce(a, p).start()
            return keep

        lax.fori_loop(0, n_piece, step, 0)

        @pl.when(is_end)
        def _():
            if a == 1:
                cv(0, mid_dev).start()
            lax.fori_loop(0, n_piece, send, 0)

    to_line(0)
    put_cols(jnp.int32(b0), mixed.T)
    b0 = b0 + 1

    def joined(j, keep):
        grad = jnp.concatenate([gj[2 * j], gj[2 * j + 1]], axis=1)
        w_qkv(j).wait()
        acc_rows(grad, w_a)

        @pl.when(j + 1 < n_qkv)
        def _():
            w_qkv(j + 1).start()

        @pl.when(j + 1 == n_qkv)
        def _():
            w_gate(0).start()
            w_up(0).start()

        put_rows(b0 + j, grad)

        @pl.when((j >= 3) & (lax.rem(j, 2) == 1))
        def _():
            ev_e((j - 3) // 2)

        return keep

    lax.fori_loop(0, n_qkv, joined, 0)
    b1 = b0 + n_qkv

    def gate_grads(gm, g, u):
        sg = jax.nn.sigmoid(g)
        g_up = (gm * (g * sg)).astype(BF)
        g_gate = (gm * u * sg * (1.0 + g * (1.0 - sg))).astype(BF)
        return g_gate, g_up

    def cols_t(left, w_ref, k):
        return lax.dot_general(left, w_ref[0:k, :], (((1,), (1,)), ((), ())), preferred_element_type=F32)

    e0 = (n_qkv - 2) // 2

    def bwd(i, keep):
        w_down(i).wait()
        gm = cols_t(cot[...], w_d, W)

        @pl.when(i + 1 < full)
        def _():
            w_down(i + 1).start()

        @pl.when(i + 1 == full)
        def _():
            w_down_t.start()

        g_gate, g_up = gate_grads(gm, up32(gu[i, 0]), up32(gu[i, 1]))
        w_gate(i).wait()
        acc_rows(g_gate, w_a)
        w_up(i).wait()
        acc_rows(g_up, w_b)

        @pl.when(i + 1 < full)
        def _():
            w_gate(i + 1).start()
            w_up(i + 1).start()

        @pl.when(i + 1 == full)
        def _():
            w_gate_t.start()
            w_up_t.start()

        for half, grad in enumerate((g_gate, g_up)):
            put_rows(b1 + 2 * i + half, grad)
            ev_e(e0 + 2 * i + half)
            ev2(2 * i + half)
            ev_m(e0 - 2 + 2 * i + half)
        return keep

    lax.fori_loop(0, full, bwd, 0)
    w_down_t.wait()
    gm = cols_t(cot[...], w_d, tail)
    both = up32(gu[full, 0])
    g_gate, g_up = gate_grads(gm, both[:, 0:tail], both[:, tail:])
    both = jnp.concatenate([g_gate, g_up], axis=1)
    w_gate_t.wait()
    w_up_t.wait()
    acc_rows(both, w_a)
    svb[0] = jnp.zeros_like(svb[0])
    svb[0, 2:3, 0 : n_qkv * W] = bias_ref[...]
    to_line(1)
    b2 = b1 + 2 * full
    e0 = e0 + 2 * full
    put_rows(jnp.int32(b2), both)
    ev_e(jnp.int32(e0))
    ev_m(jnp.int32(e0 - 2))
    ev1(jnp.int32(b2 - 1))
    ev1(jnp.int32(b2))

    n_e = 2 * n_piece
    e0 = e0 + 1
    two = 2 * full
    late = 7
    smalls = (small_1, small_2, small_3, small_4)

    def drain(k, keep):
        @pl.when(k + two < n_batch)
        def _():
            ev2(k + two)

        @pl.when(k + e0 < n_e)
        def _():
            ev_e(k + e0)

        @pl.when(k + e0 - 2 < n_e)
        def _():
            ev_m(k + e0 - 2)

        for i, small in enumerate(smalls):
            pl.when(k == SMALL_AT + i)(small)

        for h in range(2):
            b = 2 * (k - late) + h

            @pl.when((b >= 0) & (b < n_batch))
            def _():
                ev3(b)

        return keep

    lax.fori_loop(0, max(late + (n_batch + 1) // 2, n_e - e0 + 2), drain, 0)
    small_5()

    small_sent()

    def finish(b, keep):
        for h in range(2):
            c2(b, h).wait_send()
            c3(b, h).wait_send()
        return keep

    lax.fori_loop(0, n_batch, finish, 0)
    for k in range(4):
        c1(jnp.int32(n_batch - 4 + k)).wait_send()
    for k in range(2):
        st_copy(jnp.int32(n_batch - 2 + k)).wait()

    def finish_line(p, keep):
        for a, ref in ((0, out_o), (1, gin_o)):
            @pl.when(is_mid)
            def _():
                cm(a, p).wait_send()
                co(a, p, ref).wait_send()
                cl(a, p, ref).wait()

            @pl.when(is_end)
            def _():
                ce(a, p).wait_send()
                co(a, p, ref).wait_recv()

        return keep

    lax.fori_loop(0, n_piece, finish_line, 0)


def comm_call(hidden, cot, tokens, ctx, gj, gain, bias_sum, qkv_w, out_w, gate_w, up_w, down_w):
    rows, width = hidden.shape
    hd = ctx.shape[1]
    ff = gate_w.shape[1]
    full, tail = ff // W, ff % W
    n_out, n_qkv = hd // W, qkv_w.shape[1] // W
    n_batch = n_out + full + 1 + n_qkv + 2 * full + 1
    n_z = 2 * (rows // PR)
    dims = (rows, width, full, tail, n_out, n_qkv, n_batch)
    piece = (W // 2, W)
    vm, dma = pltpu.VMEM, pltpu.SemaphoreType.DMA
    any_spec = pl.BlockSpec(memory_space=pl.ANY)
    vm_spec = pl.BlockSpec(memory_space=pltpu.VMEM)
    return pl.pallas_call(
        functools.partial(comm_kernel, dims),
        out_shape=(
            jax.ShapeDtypeStruct((rows, width), BF),
            jax.ShapeDtypeStruct((rows, width), BF),
            jax.ShapeDtypeStruct((8, width), F32),
            jax.ShapeDtypeStruct((n_batch, 2) + piece, F32),
        ),
        in_specs=[any_spec] * 5 + [vm_spec] * 2 + [any_spec] * 5,
        out_specs=(any_spec, any_spec, vm_spec, any_spec),
        scratch_shapes=[
            vm((4, 2, W, rows), BF),
            vm((rows, width), BF),
            vm((2, rows, width // 2), BF),
            vm((rows, width), BF),
            vm((rows, hd), BF),
            vm((2 * n_qkv, rows, W // 2), BF),
            vm((width, W), BF),
            vm((width, W), BF),
            vm((W, width), BF),
            vm((rows, width), F32),
            vm((full + 1, 2, rows, W), BF),
            vm((4, 2, 2, 2) + piece, BF),
            vm((4, 2, 2, 2) + piece, BF),
            vm((n_batch, 2, 2, 2) + piece, BF),
            vm((n_batch, 2, 2) + piece, BF),
            vm((n_batch, 2) + piece, BF),
            vm((2, rows, width), BF),
            vm((2, rows, width), BF),
            vm((2, rows, width), BF),
            vm((2, 2) + piece, F32),
            vm((5, 8, width), F32),
            vm((4, 8, width), F32),
            vm((2, 2, 8, width), F32),
            dma((13,)),
            dma((3,)),
            dma((4,)),
            dma((n_batch,)),
            dma((n_batch, 2)),
            dma((n_batch, 2)),
            dma((n_batch, 2)),
            dma((n_batch, 2)),
            dma((n_z,)),
            dma((n_z,)),
            dma((n_z,)),
            dma((n_z,)),
            dma((n_z,)),
            dma((n_z,)),
            dma((n_z,)),
            dma((2,)),
            dma((7,)),
            dma((7,)),
        ],
        compiler_params=pltpu.CompilerParams(
            collective_id=0, has_side_effects=True, vmem_limit_bytes=67043328
        ),
        name="ffn_and_sums",
    )(hidden, cot, tokens, ctx, gj, gain[None, :], bias_sum, qkv_w, out_w, gate_w, up_w, down_w)


QB = 128


def attn_kernel(
    heads_scale, tok, seg_ref, gain_ref, shift_ref, freq_ref, w_ref, b_ref, ow_ref, cot,
    hid, ctx_o, gj_o, bias_o,
    bias_m, tab,
):
    rows = tok.shape[0]
    nq = rows // QB
    half = ROT // 2

    @pl.when(pl.program_id(0) == 0)
    def _():
        def norm_step(n, keep):
            r = pl.ds(pl.multiple_of(n * 64, 64), 64)
            v = tok[r, :].astype(F32)
            v = v - jnp.mean(v, -1, keepdims=True)
            v = v * lax.rsqrt(jnp.mean(v * v, -1, keepdims=True) + EPSILON)
            hid[r, :] = (v * gain_ref[...].astype(F32) + shift_ref[...].astype(F32)).astype(BF)
            return keep

        lax.fori_loop(0, rows // 64, norm_step, 0)
        seg = seg_ref[...].astype(F32)
        seg_t = jnp.broadcast_to(seg, (8, rows)).T
        lane = lax.broadcasted_iota(jnp.int32, (QB, QB), 1)
        head_lane = lane % DH
        for i in range(nq):
            lo = max(0, i - 2) * QB
            n = (i + 1) * QB - lo
            q_at = lax.broadcasted_iota(jnp.int32, (QB, n), 0) + i * QB
            k_at = lax.broadcasted_iota(jnp.int32, (QB, n), 1) + lo
            same = seg_t[i * QB : (i + 1) * QB, 0:1] == seg[:, lo : lo + n]
            allowed = same & (q_at >= k_at)
            bias_m[i, :, 0:n] = jnp.where(allowed, 0.0, NEGATIVE)
            place = jnp.sum(jnp.where(allowed, 1.0, 0.0), -1, keepdims=True) - 1.0
            angle = place * freq_ref[...]
            cosine, sine = jnp.cos(angle), jnp.sin(angle)
            for blk in range(3):
                live = head_lane < ROT
                if blk == 1:
                    live = live & (lane >= DH)
                if blk == 2:
                    live = live & (lane < DH)
                scale = jnp.ones((QB, QB), F32)
                if blk == 0:
                    scale = jnp.where(lane < DH, heads_scale, 1.0)
                if blk == 1:
                    scale = jnp.where(lane >= DH, heads_scale, 1.0)
                r = slice(i * QB, (i + 1) * QB)
                tab[blk, 0, r] = jnp.where(live, cosine, 1.0) * scale
                tab[blk, 1, r] = jnp.where(live & (head_lane < half), -sine, 0.0) * scale
                tab[blk, 2, r] = jnp.where(live & (head_lane >= half), sine, 0.0) * scale

    def dot_t(a, b):
        return lax.dot_general(a, b, (((1,), (1,)), ((), ())), preferred_element_type=F32)

    def dot(a, b):
        return jnp.dot(a, b, preferred_element_type=F32)

    joined = dot(hid[...], w_ref[...]) + b_ref[...].astype(F32)
    turned = []
    for blk in range(3):
        v = joined[:, blk * QB : (blk + 1) * QB]
        v = v * tab[blk, 0] + pltpu.roll(v, QB - half, 1) * tab[blk, 1] + pltpu.roll(v, half, 1) * tab[blk, 2]
        turned.append(v.astype(BF))
    gctx = dot_t(cot[...], ow_ref[...]).astype(BF)
    lo_h, hi_h = slice(0, DH), slice(DH, 2 * DH)
    heads = (
        (turned[0][:, lo_h], turned[0][:, hi_h], turned[1][:, lo_h], gctx[:, lo_h]),
        (turned[1][:, hi_h], turned[2][:, lo_h], turned[2][:, hi_h], gctx[:, hi_h]),
    )
    grads, contexts = [], []
    for q, k, v, gc in heads:
        probs, grad_s, out, grad_q = [], [], [], []
        for i in range(nq):
            lo = max(0, i - 2) * QB
            hi = (i + 1) * QB
            s = dot_t(q[i * QB : hi], k[lo:hi]) + bias_m[i, :, 0 : hi - lo]
            e = jnp.exp(s - jnp.max(s, -1, keepdims=True))
            p = e * (1.0 / jnp.sum(e, -1, keepdims=True))
            pb = p.astype(BF)
            out.append(dot(pb, v[lo:hi]))
            gp = dot_t(gc[i * QB : hi], v[lo:hi])
            gs = (p * (gp - jnp.sum(p * gp, -1, keepdims=True))).astype(BF)
            grad_q.append(dot(gs, k[lo:hi]))
            probs.append(pb)
            grad_s.append(gs)
        grad_k, grad_v = [], []
        for j in range(nq):
            top = min(j + 3, nq)

            def stack(parts):
                cut = []
                for i in range(j, top):
                    at = (j - max(0, i - 2)) * QB
                    cut.append(parts[i][:, at : at + QB].T)
                return jnp.concatenate(cut, 1)

            grad_k.append(dot(stack(grad_s), q[j * QB : top * QB]))
            grad_v.append(dot(stack(probs), gc[j * QB : top * QB]))
        contexts.append(jnp.concatenate(out, 0))
        grads.append([jnp.concatenate(part, 0) for part in (grad_q, grad_k, grad_v)])
    ctx_o[...] = jnp.concatenate(contexts, 1).astype(BF)
    (q0, k0, v0), (q1, k1, v1) = grads
    for blk, pair in enumerate(((q0, k0), (v0, q1), (k1, v1))):
        g = jnp.concatenate(pair, 1)
        g = g * tab[blk, 0] - pltpu.roll(g, QB - half, 1) * tab[blk, 1] - pltpu.roll(g, half, 1) * tab[blk, 2]
        g = g.astype(BF)
        gj_o[blk] = g
        bias_o[:, blk * QB : (blk + 1) * QB] = jnp.sum(g.astype(F32), 0, keepdims=True)


def attn_call(tokens, segment_ids, gain, shift, qkv_w, qkv_b, out_w, cot):
    rows, width = tokens.shape
    hd = out_w.shape[0]
    steps = hd // (2 * DH)
    three = 3 * QB
    lane = jnp.arange(QB) % DH % (ROT // 2)
    freq = jnp.power(10000.0, -2.0 * lane.astype(F32) / ROT)[None, :]
    whole = lambda shape: pl.BlockSpec(shape, lambda i: (0,) * len(shape))
    once = lambda shape: pl.BlockSpec(shape, lambda i: (0,) * len(shape), pipeline_mode=pl.Buffered(1))
    return pl.pallas_call(
        functools.partial(attn_kernel, DH ** (-0.5)),
        grid=(steps,),
        out_shape=(
            jax.ShapeDtypeStruct((rows, width), BF),
            jax.ShapeDtypeStruct((rows, hd), BF),
            jax.ShapeDtypeStruct((3 * steps, rows, QB), BF),
            jax.ShapeDtypeStruct((1, 3 * hd), F32),
        ),
        in_specs=[
            once((rows, width)),
            whole((1, rows)),
            whole((1, width)),
            whole((1, width)),
            whole((1, QB)),
            pl.BlockSpec((width, three), lambda i: (0, i)),
            pl.BlockSpec((1, three), lambda i: (0, i)),
            pl.BlockSpec((QB, width), lambda i: (i, 0)),
            once((rows, width)),
        ],
        out_specs=(
            whole((rows, width)),
            pl.BlockSpec((rows, QB), lambda i: (0, i)),
            pl.BlockSpec((3, rows, QB), lambda i: (i, 0, 0)),
            pl.BlockSpec((1, three), lambda i: (0, i)),
        ),
        scratch_shapes=[pltpu.VMEM((rows // QB, QB, three), F32), pltpu.VMEM((3, 3, rows, QB), F32)],
        compiler_params=pltpu.CompilerParams(vmem_limit_bytes=60 << 20),
        name="attention",
    )(tokens, segment_ids, gain[None, :], shift[None, :], freq, qkv_w, qkv_b[None, :], out_w, cot)


def fast(
    n_dp,
    n_tensor,
    tokens,
    segment_ids,
    norm_gain,
    norm_bias,
    qkv_weight,
    qkv_bias,
    out_weight,
    gate_weight,
    up_weight,
    down_weight,
    cotangent,
):
    args = (tokens, segment_ids, norm_gain, norm_bias, qkv_weight, qkv_bias, out_weight, gate_weight, up_weight, down_weight, cotangent)
    row_count, width = tokens.shape
    ff = gate_weight.shape[1]
    fits = (
        (n_dp, n_tensor) == (8, 4)
        and segment_ids.shape == (1, row_count)
        and (row_count, width) == (512, 8 * W)
        and ff % W == W // 2
        and qkv_weight.shape[1] % W == 0
        and out_weight.shape[0] % W == 0
        and qkv_weight.shape[1] == 3 * out_weight.shape[0]
        and 2 * DH == QB
    )
    if not fits:
        return local(*args)
    hidden_in, context, grad_joined, bias_local = attn_call(
        tokens, segment_ids, norm_gain, norm_bias, qkv_weight, qkv_bias, out_weight, cotangent
    )
    output, grad_input, small, sums = comm_call(
        hidden_in, cotangent, tokens, context, grad_joined, norm_gain, bias_local,
        qkv_weight, out_weight, gate_weight, up_weight, down_weight,
    )
    full, tail = ff // W, ff % W
    n_out, n_qkv = out_weight.shape[0] // W, qkv_weight.shape[1] // W
    n_batch = sums.shape[0]
    b0 = n_out + full
    b1 = b0 + 1 + n_qkv
    flat = sums.reshape(n_batch, W, W)

    def side(first, count, step):
        return [flat[first + step * i] for i in range(count)]

    last = flat[n_batch - 1]
    tail_down = sums[b0, :, : tail // 2, :].reshape(tail, W)
    return (
        output,
        grad_input,
        small[0],
        small[1],
        jnp.concatenate(side(b0 + 1, n_qkv, 1), 1),
        small[2, : n_qkv * W],
        jnp.concatenate(side(0, n_out, 1), 0),
        jnp.concatenate(side(b1, full, 2) + [last[:, :tail]], 1),
        jnp.concatenate(side(b1 + 1, full, 2) + [last[:, tail:]], 1),
        jnp.concatenate(side(n_out, full, 1) + [tail_down], 0),
    )


def solution(mesh):
    body = functools.partial(fast, mesh.shape["dp"], mesh.shape["tensor"])
    return jax.shard_map(
        body,
        mesh=mesh,
        in_specs=(
            P("dp", None),
            P("dp", None),
            P(),
            P(),
            P(None, "tensor"),
            P("tensor"),
            P("tensor", None),
            P(None, "tensor"),
            P(None, "tensor"),
            P("tensor", None),
            P("dp", None),
        ),
        out_specs=(
            P("dp", None),
            P("dp", None),
            P(),
            P(),
            P("dp", "tensor"),
            P("tensor"),
            P("tensor", "dp"),
            P("dp", "tensor"),
            P("dp", "tensor"),
            P("tensor", "dp"),
        ),
        check_vma=False,
    )
```

```python
import functools

import jax
import jax.numpy as jnp
from jax import lax
from jax.experimental import pallas as pl
from jax.experimental.pallas import tpu as pltpu
from jax.sharding import PartitionSpec as P

DH = 64
ROT = 16


EPSILON = 1e-05
NEGATIVE = -1e30


def positions_of(segments):
    column = jnp.arange(segments.shape[1], dtype=jnp.int32)
    starts = jnp.concatenate(
        [jnp.ones((segments.shape[0], 1), dtype=bool), segments[:, 1:] != segments[:, :-1]], axis=1
    )
    doc_start = lax.cummax(jnp.where(starts, column[None, :], 0), axis=1)
    return column[None, :] - doc_start


def rotary_tables(positions):
    half_rot = ROT // 2
    frequency = jnp.power(10000.0, -2.0 * jnp.arange(half_rot, dtype=jnp.float32) / ROT)
    angles = positions.astype(jnp.float32)[:, None] * frequency[None, :]
    return (jnp.cos(angles)[:, None, :], jnp.sin(angles)[:, None, :])


def rotate(tensor, cosine, sine_table):
    half_rot = ROT // 2
    first_half = tensor[..., :half_rot]
    second_half = tensor[..., half_rot:ROT]
    return jnp.concatenate(
        [
            first_half * cosine - second_half * sine_table,
            second_half * cosine + first_half * sine_table,
            tensor[..., ROT:],
        ],
        axis=-1,
    )


def rotate_back(tensor, cosine, sine_table):
    half_rot = ROT // 2
    first_half = tensor[..., :half_rot]
    second_half = tensor[..., half_rot:ROT]
    return jnp.concatenate(
        [
            first_half * cosine + second_half * sine_table,
            second_half * cosine - first_half * sine_table,
            tensor[..., ROT:],
        ],
        axis=-1,
    )


def masked_scores(query_block, seq_keys, seq_segments, begin_row, block_rows):
    key_index = jnp.arange(seq_keys.shape[0], dtype=jnp.int32)
    allowed = (seq_segments[begin_row : begin_row + block_rows, None] == seq_segments[None, :]) & (
        key_index[:, None] >= key_index[None, :]
    )
    scores = jnp.einsum("qhd,khd->hqk", query_block, seq_keys, preferred_element_type=jnp.float32)
    return jnp.where(allowed[None], scores, NEGATIVE)


def attend_forward(packed):
    seq_queries, seq_keys, seq_values, seq_segments = packed
    length = seq_queries.shape[0]
    block_rows = min(512, length)
    scores = masked_scores(seq_queries, seq_keys, seq_segments, 0, block_rows)
    top_score = jnp.max(scores, -1, keepdims=True)
    weights = jnp.exp(scores - top_score)
    denominator = jnp.sum(weights, -1, keepdims=True)
    probability = (weights / denominator).astype(jnp.bfloat16)
    contexts = [
        jnp.einsum("hqk,khd->qhd", probability, seq_values, preferred_element_type=jnp.float32)
    ]
    log_totals = [top_score + jnp.log(denominator)]
    return (jnp.concatenate(contexts, 0), jnp.concatenate(log_totals, 1))


def attend_backward(packed):
    seq_queries, seq_keys, seq_values, seq_segments, seq_log_total, seq_grad_context = packed
    length = seq_queries.shape[0]
    block_rows = min(512, length)
    grad_keys = jnp.zeros(seq_keys.shape, jnp.float32)
    grad_values = jnp.zeros(seq_values.shape, jnp.float32)
    scores = masked_scores(seq_queries, seq_keys, seq_segments, 0, block_rows)
    probability = jnp.exp(scores - seq_log_total[:, 0:block_rows])
    grad_prob = jnp.einsum(
        "qhd,khd->hqk", seq_grad_context, seq_values, preferred_element_type=jnp.float32
    )
    row_dot = jnp.sum(probability * grad_prob, -1, keepdims=True)
    grad_scores = (probability * (grad_prob - row_dot)).astype(jnp.bfloat16)
    grad_queries = [
        jnp.einsum("hqk,khd->qhd", grad_scores, seq_keys, preferred_element_type=jnp.float32)
    ]
    grad_keys = grad_keys + jnp.einsum(
        "hqk,qhd->khd", grad_scores, seq_queries, preferred_element_type=jnp.float32
    )
    grad_values = grad_values + jnp.einsum(
        "hqk,qhd->khd",
        probability.astype(jnp.bfloat16),
        seq_grad_context,
        preferred_element_type=jnp.float32,
    )
    return (jnp.concatenate(grad_queries, 0), grad_keys, grad_values)


def contract_rows(left_side, right_side):
    return lax.dot_general(
        left_side, right_side, (((0,), (0,)), ((), ())), preferred_element_type=jnp.float32
    )


def contract_cols(left_side, right_side):
    return lax.dot_general(
        left_side, right_side, (((1,), (1,)), ((), ())), preferred_element_type=jnp.float32
    )


def norm_back(grad_normed_out, normed, inverse_std, gain_full):
    grad_normed = grad_normed_out * gain_full
    return inverse_std * (
        grad_normed
        - jnp.mean(grad_normed, -1, keepdims=True)
        - normed * jnp.mean(grad_normed * normed, -1, keepdims=True)
    )


def local(
    tokens,
    segment_ids,
    norm_gain,
    norm_bias,
    qkv_weight,
    qkv_bias,
    out_weight,
    gate_weight,
    up_weight,
    down_weight,
    cotangent,
):
    row_count = tokens.shape[0]
    seq_count, length = segment_ids.shape
    head_count = qkv_weight.shape[1] // (3 * DH)
    score_scale = DH ** (-0.5)
    inputs = tokens.astype(jnp.float32)
    row_mean = jnp.mean(inputs, -1, keepdims=True)
    centered = inputs - row_mean
    inverse_std = lax.rsqrt(jnp.mean(centered * centered, -1, keepdims=True) + EPSILON)
    normed = centered * inverse_std
    gain_full = norm_gain.astype(jnp.float32)
    hidden_in = (normed * gain_full + norm_bias.astype(jnp.float32)).astype(jnp.bfloat16)
    joined_qkv = (
        jnp.dot(hidden_in, qkv_weight, preferred_element_type=jnp.float32)
        + qkv_bias.astype(jnp.float32)
    ).reshape(row_count, head_count, 3, DH)
    positions = positions_of(segment_ids).reshape(row_count)
    cosine, sine_table = rotary_tables(positions)
    queries = (rotate(joined_qkv[:, :, 0], cosine, sine_table) * score_scale).astype(jnp.bfloat16)
    key_rows = rotate(joined_qkv[:, :, 1], cosine, sine_table).astype(jnp.bfloat16)
    value_rows = joined_qkv[:, :, 2].astype(jnp.bfloat16)
    seq_shape = (seq_count, length, head_count, DH)
    seq_queries = queries.reshape(seq_shape)
    seq_keys = key_rows.reshape(seq_shape)
    seq_values = value_rows.reshape(seq_shape)
    context, log_total = lax.map(attend_forward, (seq_queries, seq_keys, seq_values, segment_ids))
    context = context.reshape(row_count, head_count * DH).astype(jnp.bfloat16)
    gate_pre = jnp.dot(hidden_in, gate_weight, preferred_element_type=jnp.float32)
    up_pre = jnp.dot(hidden_in, up_weight, preferred_element_type=jnp.float32)
    sigmoid_gate = jax.nn.sigmoid(gate_pre)
    activated = gate_pre * sigmoid_gate
    mixed = (activated * up_pre).astype(jnp.bfloat16)
    partial_out = jnp.dot(context, out_weight, preferred_element_type=jnp.float32) + jnp.dot(
        mixed, down_weight, preferred_element_type=jnp.float32
    )
    summed = lax.psum(partial_out, "tensor")
    output = (inputs + summed).astype(jnp.bfloat16)
    grad_context = contract_cols(cotangent, out_weight).astype(jnp.bfloat16)
    grad_out_w = contract_rows(context, cotangent)
    grad_down_w = contract_rows(mixed, cotangent)
    grad_out_part, grad_down_part = (
        lax.psum_scatter(grad_out_w, "dp", scatter_dimension=1, tiled=True),
        lax.psum_scatter(grad_down_w, "dp", scatter_dimension=1, tiled=True),
    )
    grad_mixed = contract_cols(cotangent, down_weight)
    grad_up = (grad_mixed * activated).astype(jnp.bfloat16)
    grad_gate = (
        grad_mixed * up_pre * sigmoid_gate * (1.0 + gate_pre * (1.0 - sigmoid_gate))
    ).astype(jnp.bfloat16)
    grad_gate_w = contract_rows(hidden_in, grad_gate)
    grad_up_w = contract_rows(hidden_in, grad_up)
    grad_hidden = contract_cols(grad_gate, gate_weight) + contract_cols(grad_up, up_weight)
    grad_queries, grad_keys, grad_values = lax.map(
        attend_backward,
        (
            seq_queries,
            seq_keys,
            seq_values,
            segment_ids,
            log_total,
            grad_context.reshape(seq_shape),
        ),
    )
    flat_shape = (row_count, head_count, DH)
    grad_queries = rotate_back(grad_queries.reshape(flat_shape) * score_scale, cosine, sine_table)
    grad_keys = rotate_back(grad_keys.reshape(flat_shape), cosine, sine_table)
    grad_joined = (
        jnp.stack([grad_queries, grad_keys, grad_values.reshape(flat_shape)], axis=2)
        .reshape(row_count, head_count * 3 * DH)
        .astype(jnp.bfloat16)
    )
    bias_local = jnp.sum(grad_joined.astype(jnp.float32), 0)
    grad_qkv_w = contract_rows(hidden_in, grad_joined)
    grad_hidden = grad_hidden + contract_cols(grad_joined, qkv_weight)
    grad_qkv_part, grad_gate_part, grad_up_part = (
        lax.psum_scatter(grad_qkv_w, "dp", scatter_dimension=0, tiled=True),
        lax.psum_scatter(grad_gate_w, "dp", scatter_dimension=0, tiled=True),
        lax.psum_scatter(grad_up_w, "dp", scatter_dimension=0, tiled=True),
    )
    grad_total = lax.psum(grad_hidden, "tensor")
    grad_input = (
        cotangent.astype(jnp.float32) + norm_back(grad_total, normed, inverse_std, gain_full)
    ).astype(jnp.bfloat16)
    grad_gain, grad_shift, grad_bias = lax.psum(
        (jnp.sum(grad_total * normed, 0), jnp.sum(grad_total, 0), bias_local), "dp"
    )
    return (
        output,
        grad_input,
        grad_gain,
        grad_shift,
        grad_qkv_part,
        grad_bias,
        grad_out_part,
        grad_gate_part,
        grad_up_part,
        grad_down_part,
    )


BF = jnp.bfloat16
F32 = jnp.float32
MESH = pl.DeviceIdType.MESH
W = 256
PR = 32
SMALL_AT = 2
LATE = 4


def comm_kernel(
    dims,
    hid_h, cot_h, tok_h, ctx_h, gj_h, gain_ref, bias_ref, qkv_h, out_h, gate_h, up_h, down_h,
    out_o, gin_o, sv_o, gq_o, go_o, gg_o, gu_o, gd_o,
    hid_t, cot, cot_s, tok, ctx, gj, w_a, w_b, w_d, acc, gu, s1, own, recv1, recv2, recv3,
    zs, ze, zm, svb, svr, svq,
    ld_sem, w_sem, s1_send, s1_recv, s2_send, s2_recv, s3_send, s3_recv,
    e_send, e_recv, m_send, m_recv, o_send, o_recv, o_loc, g_sem, v_send, v_recv,
):
    rows, width, full, tail, n_out, n_qkv, n_batch = dims
    n_piece = rows // PR
    hid = zs.at[1]
    early = full // 2
    t0 = full * W
    b_tail_down = n_out + early
    b_pairs = n_out + n_qkv + 1
    b_up = b_pairs + 2 * full
    dp = lax.axis_index("dp")
    zi = lax.axis_index("tensor")
    c = lax.rem(dp, 2)
    x = lax.rem(dp // 2, 2)
    y = dp // 4
    core_dev = {"dp": dp + 1 - 2 * c}
    x_dev = {"dp": dp + 2 - 4 * x}
    y_dev = {"dp": dp + 4 - 8 * y}
    is_mid = (zi == 1) | (zi == 2)
    is_end = (zi == 0) | (zi == 3)
    end_of = jnp.where(zi == 1, 0, 3)
    mid_of_end = jnp.where(zi == 0, 1, 2)
    end_dev = {"tensor": end_of}
    mid_dev = {"tensor": mid_of_end}
    other_mid = {"tensor": 3 - zi}

    def load(src, dst, k):
        return pltpu.make_async_copy(src, dst, ld_sem.at[k])

    def w_out(j):
        return pltpu.make_async_copy(out_h.at[pl.ds(j * W, W), :], w_d, w_sem.at[2])

    def w_down(i):
        return pltpu.make_async_copy(down_h.at[pl.ds(i * W, W), :], w_d, w_sem.at[2])

    def w_gate(i):
        return pltpu.make_async_copy(gate_h.at[:, pl.ds(i * W, W)], w_a, w_sem.at[0])

    def w_up(i):
        return pltpu.make_async_copy(up_h.at[:, pl.ds(i * W, W)], w_b, w_sem.at[1])

    def w_qkv(j, side):
        return pltpu.make_async_copy(qkv_h.at[:, pl.ds(j * W, W)], (w_a, w_b)[side], w_sem.at[side])

    w_gate_t = pltpu.make_async_copy(gate_h.at[:, pl.ds(t0, tail)], w_a.at[:, 0:tail], w_sem.at[0])
    w_up_t = pltpu.make_async_copy(up_h.at[:, pl.ds(t0, tail)], w_a.at[:, tail : 2 * tail], w_sem.at[1])
    w_down_t = pltpu.make_async_copy(down_h.at[pl.ds(t0, tail), :], w_d.at[0:tail, :], w_sem.at[2])

    ctx_ld = load(ctx_h, ctx, 0)
    hid_ld = load(hid_h, hid, 1)
    cot_ld = load(cot_h, cot, 2)
    gj_ld = load(gj_h, gj, 3)
    tok_ld = load(tok_h, tok, 4)
    cs_ld = [
        load(cot_h.at[:, (2 * q + s) * W : (2 * q + s + 1) * W], cot_s.at[s, :, q * W : (q + 1) * W], 5 + 2 * q + s)
        for q in range(4)
        for s in range(2)
    ]
    ctx_ld.start()
    w_out(0).start()
    for cp in cs_ld:
        cp.start()
    hid_ld.start()
    w_gate(0).start()
    w_up(0).start()
    cot_ld.start()
    gj_ld.start()
    tok_ld.start()

    barrier = pltpu.get_barrier_semaphore()
    for dev in (core_dev, x_dev, y_dev, {"dp": dp + 2 - 4 * x + 4 - 8 * y}):
        pl.semaphore_signal(barrier, inc=1, device_id=dev, device_id_type=MESH)

    @pl.when(is_mid)
    def _():
        pl.semaphore_signal(barrier, inc=1, device_id=end_dev, device_id_type=MESH)
        pl.semaphore_signal(barrier, inc=1, device_id=other_mid, device_id_type=MESH)

    @pl.when(is_end)
    def _():
        pl.semaphore_signal(barrier, inc=1, device_id=mid_dev, device_id_type=MESH)

    pl.semaphore_wait(barrier, jnp.where(is_mid, 6, 5))

    def rdma(src, dst, send, recv, dev):
        return pltpu.make_async_remote_copy(
            src_ref=src, dst_ref=dst, send_sem=send, recv_sem=recv, device_id=dev, device_id_type=MESH
        )

    def c1(b):
        slot = lax.rem(b, 4)
        return rdma(s1.at[slot], recv1.at[b], s1_send.at[slot], s1_recv.at[b], core_dev)

    def c2(b, h):
        if h == 0:
            return rdma(recv1.at[b, :, 1 - x, 0], recv2.at[b, 0], s2_send.at[b, 0], s2_recv.at[b, 0], x_dev)
        return rdma(recv1.at[b, 1 - y, :, 1], recv2.at[b, 1], s2_send.at[b, 1], s2_recv.at[b, 1], y_dev)

    def c3(b, h):
        if h == 0:
            return rdma(recv2.at[b, 0, 1 - y], recv3.at[b, 0], s3_send.at[b, 0], s3_recv.at[b, 0], y_dev)
        return rdma(recv2.at[b, 1, 1 - x], recv3.at[b, 1], s3_send.at[b, 1], s3_recv.at[b, 1], x_dev)

    def up32(v):
        return v.astype(F32)

    def ev1(b):
        slot = lax.rem(b, 4)
        c1(b).wait_recv()
        for yy in range(2):
            for xx in range(2):
                for h in range(2):
                    recv1[b, yy, xx, h] += own[slot, yy, xx, h]
        c2(b, 0).start()
        c2(b, 1).start()

    def ev2(b):
        c2(b, 0).wait_recv()
        c2(b, 1).wait_recv()
        for k in range(2):
            recv2[b, 0, k] += recv1[b, k, x, 0]
            recv2[b, 1, k] += recv1[b, y, k, 1]
        c3(b, 0).start()
        c3(b, 1).start()

    def cut(b, h, ref, row, col, n=W // 2, lo=0, wide=W):
        if not isinstance(row, int):
            row = pl.multiple_of(row, 64)
        if not isinstance(col, int):
            col = pl.multiple_of(col, W // 2)
        return pltpu.make_async_copy(
            recv3.at[b, h, 0:n, lo : lo + wide], ref.at[pl.ds(row + h * n, n), pl.ds(col, wide)], g_sem.at[b, h]
        )

    groups = (
        (0, n_out, 1, lambda b, h, i: (cut(b, h, go_o, i * W, 0),)),
        (n_out, early, 1, lambda b, h, i: (cut(b, h, gq_o, 0, i * W),)),
        (b_tail_down, 1, 1, lambda b, h, i: (cut(b, h, gd_o, t0, 0, tail // 2),)),
        (b_tail_down + 1, n_qkv - early, 1, lambda b, h, i: (cut(b, h, gq_o, 0, (i + early) * W),)),
        (b_pairs, full, 2, lambda b, h, i: (cut(b, h, gd_o, i * W, 0),)),
        (b_pairs + 1, full, 2, lambda b, h, i: (cut(b, h, gg_o, 0, i * W),)),
        (b_up, full, 1, lambda b, h, i: (cut(b, h, gu_o, 0, i * W),)),
        (
            b_up + full, 1, 1,
            lambda b, h, i: (
                cut(b, h, gg_o, 0, t0, wide=tail), cut(b, h, gu_o, 0, t0, lo=tail, wide=tail)
            ),
        ),
    )

    def ev3(b):
        c3(b, 0).wait_recv()
        c3(b, 1).wait_recv()
        recv3[b, 0] += recv2[b, 0, y]
        recv3[b, 1] += recv2[b, 1, x]
        for first, count, step, make in groups:
            here = (b >= first) & (b < first + count * step)
            if step > 1:
                here = here & (lax.rem(b - first, step) == 0)

            @pl.when(here)
            def _(first=first, step=step, make=make):
                for h in range(2):
                    for cp in make(b, h, (b - first) // step):
                        cp.start()

    def before_put(b):
        @pl.when(b >= 4)
        def _():
            c1(b - 4).wait_send()

    def after_put(b):
        c1(b).start()

    def put_rows(b, grad):
        slot = lax.rem(b, 4)
        before_put(b)
        for part, dst in ((1 - c, s1), (c, own)):
            left = hid_t[:, part].reshape(4 * W, rows)
            res = jnp.dot(left, grad, preferred_element_type=F32).astype(BF)
            dst[slot] = res.reshape(2, 2, 2, W // 2, W)
        after_put(b)

    def put_cols(b, left_t):
        slot = lax.rem(b, 4)
        h = left_t.shape[0]
        before_put(b)
        for part, dst in ((1 - c, s1), (c, own)):
            res = jnp.dot(left_t, cot_s[part], preferred_element_type=F32).astype(BF)
            for q in range(4):
                piece = res[:, q * W : (q + 1) * W].reshape(2, h // 2, W)
                dst[slot, q // 2, q % 2, :, 0 : h // 2, :] = piece
                if h < W:
                    dst[slot, q // 2, q % 2, :, h // 2 :, :] = jnp.zeros((2, (W - h) // 2, W), BF)
        after_put(b)

    NB = 512

    def acc_cols(left, w_ref, k, first):
        for n in range(width // NB):
            cols = slice(n * NB, (n + 1) * NB)
            res = jnp.dot(left, w_ref[0:k, cols], preferred_element_type=F32)
            if first:
                acc[:, cols] = res
            else:
                acc[:, cols] += res

    def acc_rows(grad, w_ref):
        for n in range(width // NB):
            cols = slice(n * NB, (n + 1) * NB)
            acc[:, cols] += lax.dot_general(
                grad, w_ref[cols, :], (((1,), (1,)), ((), ())), preferred_element_type=F32
            )

    def z_rows(p):
        return pl.ds(pl.multiple_of(p * PR, PR), PR)

    def ce(a, p):
        i = a * n_piece + p
        return rdma(zs.at[a, z_rows(p)], ze.at[a, z_rows(p)], e_send.at[i], e_recv.at[i], mid_dev)

    def cm(a, p):
        i = a * n_piece + p
        return rdma(zs.at[a, z_rows(p)], zm.at[a, z_rows(p)], m_send.at[i], m_recv.at[i], other_mid)

    def co(a, p, ref):
        i = a * n_piece + p
        return rdma(ze.at[a, z_rows(p)], ref.at[z_rows(p)], o_send.at[i], o_recv.at[i], end_dev)

    def cl(a, p, ref):
        i = a * n_piece + p
        return pltpu.make_async_copy(ze.at[a, z_rows(p)], ref.at[z_rows(p)], o_loc.at[i])

    def ev_e(e):
        a, p = e // n_piece, lax.rem(e, n_piece)

        @pl.when(is_mid)
        def _():
            ce(a, p).wait_recv()
            r = z_rows(p)
            zs[a, r, :] += ze[a, r, :]
            cm(a, p).start()

    def norm_rows(r):
        v = up32(tok[r, :])
        mu = jnp.mean(v, -1, keepdims=True)
        v = v - mu
        inv = lax.rsqrt(jnp.mean(v * v, -1, keepdims=True) + EPSILON)
        return v * inv, inv

    def ev_m(e):
        a, p = e // n_piece, lax.rem(e, n_piece)

        @pl.when(is_mid)
        def _():
            cm(a, p).wait_recv()
            r = z_rows(p)

            @pl.when(a == 0)
            def _():
                total = up32(zs[0, r, :]) + up32(zm[0, r, :])
                ze[0, r, :] = (up32(tok[r, :]) + total).astype(BF)
                co(0, p, out_o).start()
                cl(0, p, out_o).start()

            @pl.when(a == 1)
            def _():
                total = up32(zs[1, r, :]) + up32(zm[1, r, :])
                normed, inv = norm_rows(r)
                back = norm_back(total, normed, inv, gain_ref[...].astype(F32))
                ze[1, r, :] = (up32(cot[r, :]) + back).astype(BF)
                co(1, p, gin_o).start()
                cl(1, p, gin_o).start()

    ctx_ld.wait()
    for cp in cs_ld:
        cp.wait()
    for j in range(n_out):
        left = ctx[:, j * W : (j + 1) * W]
        w_out(j).wait()
        acc_cols(left, w_d, W, j == 0)
        if j + 1 < n_out:
            w_out(j + 1).start()
        else:
            w_down(0).start()
        put_cols(jnp.int32(j), left.T)
    hid_ld.wait()
    for q in range(4):
        for s in range(2):
            lo = (2 * q + s) * W
            hid_t[q, s] = hid[:, lo : lo + W].T

    def act_of(g, u):
        return (g * jax.nn.sigmoid(g) * u).astype(BF)

    def joined_grad(j):
        return jnp.concatenate([gj[2 * j], gj[2 * j + 1]], axis=1)

    gj_ld.wait()

    def fwd(i, keep):
        w_gate(i).wait()
        g = jnp.dot(hid[...], w_a[...], preferred_element_type=F32)
        w_up(i).wait()
        u = jnp.dot(hid[...], w_b[...], preferred_element_type=F32)

        @pl.when(i + 1 < full)
        def _():
            w_gate(i + 1).start()
            w_up(i + 1).start()

        @pl.when(i + 1 == full)
        def _():
            w_gate_t.start()
            w_up_t.start()

        gu[i, 0] = g.astype(BF)
        gu[i, 1] = u.astype(BF)
        mixed = act_of(g, u)

        @pl.when(i == 0)
        def _():
            for b in range(n_out):
                ev1(jnp.int32(b))

        @pl.when((i >= 2) & (lax.rem(i, 2) == 0))
        def _():
            ev1(n_out + i // 2 - 1)
            ev2(i // 2 - 1)

        w_down(i).wait()
        acc_cols(mixed, w_d, W, False)

        @pl.when(i + 1 < full)
        def _():
            w_down(i + 1).start()

        @pl.when(i + 1 == full)
        def _():
            w_down_t.start()

        @pl.when(lax.rem(i, 2) == 1)
        def _():
            put_rows(n_out + i // 2, joined_grad(i // 2))

        return keep

    lax.fori_loop(0, full, fwd, 0)
    w_gate_t.wait()
    w_up_t.wait()
    w_qkv(1, 1).start()
    both = jnp.dot(hid[...], w_a[...], preferred_element_type=F32)
    w_qkv(0, 0).start()
    gu[full, 0] = both.astype(BF)
    mixed = act_of(both[:, 0:tail], both[:, tail:])
    w_down_t.wait()
    acc_cols(mixed, w_d, tail, False)
    w_down(0).start()

    tok_ld.wait()
    cot_ld.wait()

    def cv(k, dev):
        return rdma(svb.at[k], svr.at[k], v_send.at[k], v_recv.at[k], dev)

    def cw(k, dev):
        return rdma(svb.at[4], svq.at[y, x], v_send.at[4 + k], v_recv.at[4 + k], dev)

    square = (x_dev, y_dev, {"dp": dp + 2 - 4 * x + 4 - 8 * y})

    def small_1():
        @pl.when(is_mid)
        def _():
            cv(0, end_dev).wait_recv()
            svb[1] = svb[0] + svr[0]
            cv(1, other_mid).start()

    def small_2():
        @pl.when(is_mid)
        def _():
            cv(1, other_mid).wait_recv()
            svb[2] = svb[1] + svr[1]
            svb[3, 0:2, :] = svb[2, 0:2, :]
            cv(2, end_dev).start()

    def small_3():
        @pl.when(is_end)
        def _():
            cv(2, mid_dev).wait_recv()
            svb[3, 0:2, :] = svr[2, 0:2, :]

        svb[3, 2:8, :] = svb[0, 2:8, :]
        cv(3, core_dev).start()

    def small_4():
        cv(3, core_dev).wait_recv()
        svb[4] = svb[3] + svr[3]
        svq[y, x] = svb[4]
        for k, dev in enumerate(square):
            cw(k, dev).start()

    def small_5():
        for k, dev in enumerate(square):
            cw(k, dev).wait_recv()
        sv_o[...] = (svq[0, 0] + svq[0, 1]) + (svq[1, 0] + svq[1, 1])

    def small_sent():
        @pl.when(is_end)
        def _():
            cv(0, mid_dev).wait_send()

        @pl.when(is_mid)
        def _():
            cv(1, other_mid).wait_send()
            cv(2, end_dev).wait_send()

        cv(3, core_dev).wait_send()
        for k, dev in enumerate(square):
            cw(k, dev).wait_send()

    def to_line(a):
        def step(p, keep):
            r = z_rows(p)
            v = acc[r, :]
            zs[a, r, :] = v.astype(BF)
            if a == 0:
                acc[r, :] = jnp.zeros_like(v)
            else:
                normed, _inv = norm_rows(r)
                svb[0, 0:1, :] += jnp.sum(v * normed, 0, keepdims=True)
                svb[0, 1:2, :] += jnp.sum(v, 0, keepdims=True)

            return keep

        def send(p, keep):
            ce(a, p).start()
            return keep

        lax.fori_loop(0, n_piece, step, 0)

        @pl.when(is_end)
        def _():
            if a == 1:
                cv(0, mid_dev).start()
            lax.fori_loop(0, n_piece, send, 0)

    to_line(0)
    put_cols(jnp.int32(b_tail_down), mixed.T)

    def joined(n, keep):
        for side in range(2):
            j = 2 * n + side
            w_qkv(j, side).wait()
            acc_rows(joined_grad(j), (w_a, w_b)[side])

            @pl.when(j + 2 < n_qkv)
            def _(j=j, side=side):
                w_qkv(j + 2, side).start()

            @pl.when(j + 2 >= n_qkv)
            def _(side=side):
                (w_gate, w_up)[side](0).start()

            @pl.when(j + early < n_qkv)
            def _(j=j):
                b = b_tail_down + 1 + j
                put_rows(b, joined_grad(j + early))
                ev1(b - 1)

        ev_e(n)

        @pl.when(n == 1)
        def _():
            ev2(jnp.int32(early))

        @pl.when(n >= 2)
        def _():
            ev_m(n - 2)

        return keep

    lax.fori_loop(0, n_qkv // 2, joined, 0)

    def gate_grads(gm, g, u):
        sg = jax.nn.sigmoid(g)
        g_up = (gm * (g * sg)).astype(BF)
        g_gate = (gm * u * sg * (1.0 + g * (1.0 - sg))).astype(BF)
        return g_gate, g_up

    def cols_t(left, w_ref, k):
        return lax.dot_general(left, w_ref[0:k, :], (((1,), (1,)), ((), ())), preferred_element_type=F32)

    e0 = n_qkv // 2

    def bwd(i, keep):
        w_down(i).wait()
        gm = cols_t(cot[...], w_d, W)

        @pl.when(i + 1 < full)
        def _():
            w_down(i + 1).start()

        @pl.when(i + 1 == full)
        def _():
            w_down_t.start()

        g, u = up32(gu[i, 0]), up32(gu[i, 1])
        mixed = act_of(g, u)
        g_gate, g_up = gate_grads(gm, g, u)
        gu[i, 0] = g_gate
        gu[i, 1] = g_up
        w_gate(i).wait()
        acc_rows(g_gate, w_a)
        w_up(i).wait()
        acc_rows(g_up, w_b)

        @pl.when(i + 1 < full)
        def _():
            w_gate(i + 1).start()
            w_up(i + 1).start()

        @pl.when(i + 1 == full)
        def _():
            w_gate_t.start()
            w_up_t.start()

        b = b_pairs + 2 * i
        e = e0 + 2 * i
        put_cols(b, mixed.T)
        ev1(b - 1)
        ev2(early + 1 + 2 * i)
        ev_e(e)
        ev_m(e - 2)
        put_rows(b + 1, gu[i, 0])
        ev1(b)
        ev2(early + 2 + 2 * i)
        ev_e(e + 1)
        ev_m(e - 1)
        return keep

    lax.fori_loop(0, full, bwd, 0)
    w_down_t.wait()
    gm = cols_t(cot[...], w_d, tail)
    both = up32(gu[full, 0])
    g_gate, g_up = gate_grads(gm, both[:, 0:tail], both[:, tail:])
    both = jnp.concatenate([g_gate, g_up], axis=1)
    gu[full, 0] = both
    w_gate_t.wait()
    w_up_t.wait()
    acc_rows(both, w_a)
    svb[0] = jnp.zeros_like(svb[0])
    svb[0, 2:3, 0 : n_qkv * W] = bias_ref[...]
    to_line(1)

    e0 = e0 + 2 * full

    def left_over(i, keep):
        b = b_up + i
        at = jnp.where(i == full, 0, 1)
        put_rows(b, gu[i, at])
        ev1(b - 1)

        @pl.when(lax.rem(i, 2) == 0)
        def _():
            ev2(early + 1 + 2 * full + i // 2)
            ev_e(e0 + i // 2)
            ev_m(e0 + i // 2 - 2)

        return keep

    lax.fori_loop(0, full + 1, left_over, 0)
    ev1(jnp.int32(n_batch - 1))
    e0 = e0 + (full + 2) // 2

    n_e = 2 * n_piece
    two = early + 1 + 2 * full + (full + 2) // 2
    smalls = (small_1, small_2, small_3, small_4)

    def drain(k, keep):
        @pl.when(k + two < n_batch)
        def _():
            ev2(k + two)

        @pl.when(k + e0 < n_e)
        def _():
            ev_e(k + e0)

        @pl.when(k + e0 - 2 < n_e)
        def _():
            ev_m(k + e0 - 2)

        for i, small in enumerate(smalls):
            pl.when(k == SMALL_AT + i)(small)

        for h in range(2):
            b = 2 * (k - LATE) + h

            @pl.when((b >= 0) & (b < n_batch))
            def _():
                ev3(b)

        return keep

    lax.fori_loop(0, max(LATE + (n_batch + 1) // 2, n_e - e0 + 2), drain, 0)
    small_5()

    small_sent()

    def finish(b, keep):
        for h in range(2):
            c2(b, h).wait_send()
            c3(b, h).wait_send()
        return keep

    lax.fori_loop(0, n_batch, finish, 0)
    for k in range(4):
        c1(jnp.int32(n_batch - 4 + k)).wait_send()
    for first, count, step, make in groups:
        for i in range(count):
            for h in range(2):
                for cp in make(first + i * step, h, i):
                    cp.wait()

    def finish_line(p, keep):
        for a, ref in ((0, out_o), (1, gin_o)):
            @pl.when(is_mid)
            def _():
                cm(a, p).wait_send()
                co(a, p, ref).wait_send()
                cl(a, p, ref).wait()

            @pl.when(is_end)
            def _():
                ce(a, p).wait_send()
                co(a, p, ref).wait_recv()

        return keep

    lax.fori_loop(0, n_piece, finish_line, 0)


def comm_call(hidden, cot, tokens, ctx, gj, gain, bias_sum, qkv_w, out_w, gate_w, up_w, down_w):
    rows, width = hidden.shape
    hd = ctx.shape[1]
    ff = gate_w.shape[1]
    full, tail = ff // W, ff % W
    n_out, n_qkv = hd // W, qkv_w.shape[1] // W
    n_batch = n_out + full + 1 + n_qkv + 2 * full + 1
    n_z = 2 * (rows // PR)
    dims = (rows, width, full, tail, n_out, n_qkv, n_batch)
    piece = (W // 2, W)
    vm, dma = pltpu.VMEM, pltpu.SemaphoreType.DMA
    any_spec = pl.BlockSpec(memory_space=pl.ANY)
    vm_spec = pl.BlockSpec(memory_space=pltpu.VMEM)
    return pl.pallas_call(
        functools.partial(comm_kernel, dims),
        out_shape=(
            jax.ShapeDtypeStruct((rows, width), BF),
            jax.ShapeDtypeStruct((rows, width), BF),
            jax.ShapeDtypeStruct((8, width), F32),
            jax.ShapeDtypeStruct((W, n_qkv * W), BF),
            jax.ShapeDtypeStruct((hd, W), BF),
            jax.ShapeDtypeStruct((W, ff), BF),
            jax.ShapeDtypeStruct((W, ff), BF),
            jax.ShapeDtypeStruct((ff, W), BF),
        ),
        in_specs=[any_spec] * 5 + [vm_spec] * 2 + [any_spec] * 5,
        out_specs=(any_spec, any_spec, vm_spec) + (any_spec,) * 5,
        scratch_shapes=[
            vm((4, 2, W, rows), BF),
            vm((rows, width), BF),
            vm((2, rows, width // 2), BF),
            vm((rows, width), BF),
            vm((rows, hd), BF),
            vm((2 * n_qkv, rows, W // 2), BF),
            vm((width, W), BF),
            vm((width, W), BF),
            vm((W, width), BF),
            vm((rows, width), F32),
            vm((full + 1, 2, rows, W), BF),
            vm((4, 2, 2, 2) + piece, BF),
            vm((4, 2, 2, 2) + piece, BF),
            vm((n_batch, 2, 2, 2) + piece, BF),
            vm((n_batch, 2, 2) + piece, BF),
            vm((n_batch, 2) + piece, BF),
            vm((2, rows, width), BF),
            vm((2, rows, width), BF),
            vm((2, rows, width), BF),
            vm((5, 8, width), F32),
            vm((4, 8, width), F32),
            vm((2, 2, 8, width), F32),
            dma((13,)),
            dma((3,)),
            dma((4,)),
            dma((n_batch,)),
            dma((n_batch, 2)),
            dma((n_batch, 2)),
            dma((n_batch, 2)),
            dma((n_batch, 2)),
            dma((n_z,)),
            dma((n_z,)),
            dma((n_z,)),
            dma((n_z,)),
            dma((n_z,)),
            dma((n_z,)),
            dma((n_z,)),
            dma((n_batch, 2)),
            dma((7,)),
            dma((7,)),
        ],
        compiler_params=pltpu.CompilerParams(
            collective_id=0, has_side_effects=True, vmem_limit_bytes=67043328
        ),
        name="ffn_and_sums",
    )(hidden, cot, tokens, ctx, gj, gain[None, :], bias_sum, qkv_w, out_w, gate_w, up_w, down_w)


QB = 128
ROWS = 32


def attn_kernel(
    heads_scale, tok, seg_ref, gain_ref, shift_ref, freq_ref, w_ref, b_ref, ow_ref, cot,
    hid, ctx_o, gj_o, bias_o,
    bias_m, tab, s_m, g_m, p_m, gs_m,
):
    rows = tok.shape[0]
    nq = rows // QB
    half = ROT // 2

    @pl.when(pl.program_id(0) == 0)
    def _():
        def norm_step(n, keep):
            r = pl.ds(pl.multiple_of(n * 64, 64), 64)
            v = tok[r, :].astype(F32)
            v = v - jnp.mean(v, -1, keepdims=True)
            v = v * lax.rsqrt(jnp.mean(v * v, -1, keepdims=True) + EPSILON)
            hid[r, :] = (v * gain_ref[...].astype(F32) + shift_ref[...].astype(F32)).astype(BF)
            return keep

        lax.fori_loop(0, rows // 64, norm_step, 0)
        seg = seg_ref[...].astype(F32)
        seg_t = jnp.broadcast_to(seg, (8, rows)).T
        lane = lax.broadcasted_iota(jnp.int32, (QB, QB), 1)
        head_lane = lane % DH
        for i in range(nq):
            lo = max(0, i - 2) * QB
            n = (i + 1) * QB - lo
            q_at = lax.broadcasted_iota(jnp.int32, (QB, n), 0) + i * QB
            k_at = lax.broadcasted_iota(jnp.int32, (QB, n), 1) + lo
            same = seg_t[i * QB : (i + 1) * QB, 0:1] == seg[:, lo : lo + n]
            allowed = same & (q_at >= k_at)
            bias_m[i, :, 0:n] = jnp.where(allowed, 0.0, NEGATIVE)
            place = jnp.sum(jnp.where(allowed, 1.0, 0.0), -1, keepdims=True) - 1.0
            angle = place * freq_ref[...]
            cosine, sine = jnp.cos(angle), jnp.sin(angle)
            for blk in range(3):
                live = head_lane < ROT
                if blk == 1:
                    live = live & (lane >= DH)
                if blk == 2:
                    live = live & (lane < DH)
                scale = jnp.ones((QB, QB), F32)
                if blk == 0:
                    scale = jnp.where(lane < DH, heads_scale, 1.0)
                if blk == 1:
                    scale = jnp.where(lane >= DH, heads_scale, 1.0)
                r = slice(i * QB, (i + 1) * QB)
                tab[blk, 0, r] = jnp.where(live, cosine, 1.0) * scale
                tab[blk, 1, r] = jnp.where(live & (head_lane < half), -sine, 0.0) * scale
                tab[blk, 2, r] = jnp.where(live & (head_lane >= half), sine, 0.0) * scale

    def dot_t(a, b):
        return lax.dot_general(a, b, (((1,), (1,)), ((), ())), preferred_element_type=F32)

    def dot(a, b):
        return jnp.dot(a, b, preferred_element_type=F32)

    joined = dot(hid[...], w_ref[...]) + b_ref[...].astype(F32)
    turned = []
    for blk in range(3):
        v = joined[:, blk * QB : (blk + 1) * QB]
        v = v * tab[blk, 0] + pltpu.roll(v, QB - half, 1) * tab[blk, 1] + pltpu.roll(v, half, 1) * tab[blk, 2]
        turned.append(v.astype(BF))
    gctx = dot_t(cot[...], ow_ref[...]).astype(BF)
    lo_h, hi_h = slice(0, DH), slice(DH, 2 * DH)
    heads = (
        (turned[0][:, lo_h], turned[0][:, hi_h], turned[1][:, lo_h], gctx[:, lo_h]),
        (turned[1][:, hi_h], turned[2][:, lo_h], turned[2][:, hi_h], gctx[:, hi_h]),
    )
    spans = [(max(0, i - 2) * QB, (i + 1) * QB) for i in range(nq)]
    blocks = [(n, i) for i in range(nq) for n in range(2)]
    for n, i in blocks:
        q, k, v, gc = heads[n]
        lo, hi = spans[i]
        s_m[n, i, :, 0 : hi - lo] = dot_t(q[i * QB : hi], k[lo:hi])
        g_m[n, i, :, 0 : hi - lo] = dot_t(gc[i * QB : hi], v[lo:hi])
    for n, i in blocks:
        lo, hi = spans[i]
        for r in range(0, QB, ROWS):
            rr = slice(r, r + ROWS)
            s = s_m[n, i, rr, 0 : hi - lo] + bias_m[i, rr, 0 : hi - lo]
            e = jnp.exp(s - jnp.max(s, -1, keepdims=True))
            p = e * (1.0 / jnp.sum(e, -1, keepdims=True))
            gp = g_m[n, i, rr, 0 : hi - lo]
            p_m[n, i, rr, 0 : hi - lo] = p.astype(BF)
            gs_m[n, i, rr, 0 : hi - lo] = (p * (gp - jnp.sum(p * gp, -1, keepdims=True))).astype(BF)
    grads, contexts = [], []
    for n, (q, k, v, gc) in enumerate(heads):
        out, grad_q, grad_k, grad_v = [], [], [], []
        for i, (lo, hi) in enumerate(spans):
            out.append(dot(p_m[n, i, :, 0 : hi - lo], v[lo:hi]))
            grad_q.append(dot(gs_m[n, i, :, 0 : hi - lo], k[lo:hi]))
        for j in range(nq):
            top = min(j + 3, nq)

            def stack(part):
                cut = []
                for i in range(j, top):
                    at = j * QB - spans[i][0]
                    cut.append(part[n, i, :, at : at + QB].T)
                return jnp.concatenate(cut, 1)

            grad_k.append(dot(stack(gs_m), q[j * QB : top * QB]))
            grad_v.append(dot(stack(p_m), gc[j * QB : top * QB]))
        contexts.append(jnp.concatenate(out, 0))
        grads.append([jnp.concatenate(part, 0) for part in (grad_q, grad_k, grad_v)])
    ctx_o[...] = jnp.concatenate(contexts, 1).astype(BF)
    (q0, k0, v0), (q1, k1, v1) = grads
    for blk, pair in enumerate(((q0, k0), (v0, q1), (k1, v1))):
        g = jnp.concatenate(pair, 1)
        g = g * tab[blk, 0] - pltpu.roll(g, QB - half, 1) * tab[blk, 1] - pltpu.roll(g, half, 1) * tab[blk, 2]
        g = g.astype(BF)
        gj_o[blk] = g
        bias_o[:, blk * QB : (blk + 1) * QB] = jnp.sum(g.astype(F32), 0, keepdims=True)


def attn_call(tokens, segment_ids, gain, shift, qkv_w, qkv_b, out_w, cot):
    rows, width = tokens.shape
    hd = out_w.shape[0]
    steps = hd // (2 * DH)
    three = 3 * QB
    lane = jnp.arange(QB) % DH % (ROT // 2)
    freq = jnp.power(10000.0, -2.0 * lane.astype(F32) / ROT)[None, :]
    whole = lambda shape: pl.BlockSpec(shape, lambda i: (0,) * len(shape))
    once = lambda shape: pl.BlockSpec(shape, lambda i: (0,) * len(shape), pipeline_mode=pl.Buffered(1))
    return pl.pallas_call(
        functools.partial(attn_kernel, DH ** (-0.5)),
        grid=(steps,),
        out_shape=(
            jax.ShapeDtypeStruct((rows, width), BF),
            jax.ShapeDtypeStruct((rows, hd), BF),
            jax.ShapeDtypeStruct((3 * steps, rows, QB), BF),
            jax.ShapeDtypeStruct((1, 3 * hd), F32),
        ),
        in_specs=[
            once((rows, width)),
            whole((1, rows)),
            whole((1, width)),
            whole((1, width)),
            whole((1, QB)),
            pl.BlockSpec((width, three), lambda i: (0, i)),
            pl.BlockSpec((1, three), lambda i: (0, i)),
            pl.BlockSpec((QB, width), lambda i: (i, 0)),
            once((rows, width)),
        ],
        out_specs=(
            whole((rows, width)),
            pl.BlockSpec((rows, QB), lambda i: (0, i)),
            pl.BlockSpec((3, rows, QB), lambda i: (i, 0, 0)),
            pl.BlockSpec((1, three), lambda i: (0, i)),
        ),
        scratch_shapes=[
            pltpu.VMEM((rows // QB, QB, three), F32),
            pltpu.VMEM((3, 3, rows, QB), F32),
            pltpu.VMEM((2, rows // QB, QB, three), F32),
            pltpu.VMEM((2, rows // QB, QB, three), F32),
            pltpu.VMEM((2, rows // QB, QB, three), BF),
            pltpu.VMEM((2, rows // QB, QB, three), BF),
        ],
        compiler_params=pltpu.CompilerParams(vmem_limit_bytes=60 << 20),
        name="attention",
    )(tokens, segment_ids, gain[None, :], shift[None, :], freq, qkv_w, qkv_b[None, :], out_w, cot)


def fast(
    n_dp,
    n_tensor,
    tokens,
    segment_ids,
    norm_gain,
    norm_bias,
    qkv_weight,
    qkv_bias,
    out_weight,
    gate_weight,
    up_weight,
    down_weight,
    cotangent,
):
    args = (tokens, segment_ids, norm_gain, norm_bias, qkv_weight, qkv_bias, out_weight, gate_weight, up_weight, down_weight, cotangent)
    row_count, width = tokens.shape
    ff = gate_weight.shape[1]
    fits = (
        (n_dp, n_tensor) == (8, 4)
        and segment_ids.shape == (1, row_count)
        and (row_count, width) == (512, 8 * W)
        and ff % W == W // 2
        and qkv_weight.shape[1] % (2 * W) == 0
        and out_weight.shape[0] % W == 0
        and qkv_weight.shape[1] == 3 * out_weight.shape[0]
        and 2 * DH == QB
    )
    if not fits:
        return local(*args)
    hidden_in, context, grad_joined, bias_local = attn_call(
        tokens, segment_ids, norm_gain, norm_bias, qkv_weight, qkv_bias, out_weight, cotangent
    )
    output, grad_input, small, *sums = comm_call(
        hidden_in, cotangent, tokens, context, grad_joined, norm_gain, bias_local,
        qkv_weight, out_weight, gate_weight, up_weight, down_weight,
    )
    joined_w, out_w, gate_w, up_w, down_w = (v.astype(F32) for v in sums)
    return (
        output,
        grad_input,
        small[0],
        small[1],
        joined_w,
        small[2, : qkv_weight.shape[1]],
        out_w,
        gate_w,
        up_w,
        down_w,
    )


def solution(mesh):
    body = functools.partial(fast, mesh.shape["dp"], mesh.shape["tensor"])
    return jax.shard_map(
        body,
        mesh=mesh,
        in_specs=(
            P("dp", None),
            P("dp", None),
            P(),
            P(),
            P(None, "tensor"),
            P("tensor"),
            P("tensor", None),
            P(None, "tensor"),
            P(None, "tensor"),
            P("tensor", None),
            P("dp", None),
        ),
        out_specs=(
            P("dp", None),
            P("dp", None),
            P(),
            P(),
            P("dp", "tensor"),
            P("tensor"),
            P("tensor", "dp"),
            P("dp", "tensor"),
            P("dp", "tensor"),
            P("tensor", "dp"),
        ),
        check_vma=False,
    )
```

```python
import functools

import jax
import jax.numpy as jnp
from jax import lax
from jax.experimental import pallas as pl
from jax.experimental.pallas import tpu as pltpu
from jax.sharding import PartitionSpec as P

DH = 64
ROT = 16


EPSILON = 1e-05
NEGATIVE = -1e30


def positions_of(segments):
    column = jnp.arange(segments.shape[1], dtype=jnp.int32)
    starts = jnp.concatenate(
        [jnp.ones((segments.shape[0], 1), dtype=bool), segments[:, 1:] != segments[:, :-1]], axis=1
    )
    doc_start = lax.cummax(jnp.where(starts, column[None, :], 0), axis=1)
    return column[None, :] - doc_start


def rotary_tables(positions):
    half_rot = ROT // 2
    frequency = jnp.power(10000.0, -2.0 * jnp.arange(half_rot, dtype=jnp.float32) / ROT)
    angles = positions.astype(jnp.float32)[:, None] * frequency[None, :]
    return (jnp.cos(angles)[:, None, :], jnp.sin(angles)[:, None, :])


def rotate(tensor, cosine, sine_table):
    half_rot = ROT // 2
    first_half = tensor[..., :half_rot]
    second_half = tensor[..., half_rot:ROT]
    return jnp.concatenate(
        [
            first_half * cosine - second_half * sine_table,
            second_half * cosine + first_half * sine_table,
            tensor[..., ROT:],
        ],
        axis=-1,
    )


def rotate_back(tensor, cosine, sine_table):
    half_rot = ROT // 2
    first_half = tensor[..., :half_rot]
    second_half = tensor[..., half_rot:ROT]
    return jnp.concatenate(
        [
            first_half * cosine + second_half * sine_table,
            second_half * cosine - first_half * sine_table,
            tensor[..., ROT:],
        ],
        axis=-1,
    )


def masked_scores(query_block, seq_keys, seq_segments, begin_row, block_rows):
    key_index = jnp.arange(seq_keys.shape[0], dtype=jnp.int32)
    allowed = (seq_segments[begin_row : begin_row + block_rows, None] == seq_segments[None, :]) & (
        key_index[:, None] >= key_index[None, :]
    )
    scores = jnp.einsum("qhd,khd->hqk", query_block, seq_keys, preferred_element_type=jnp.float32)
    return jnp.where(allowed[None], scores, NEGATIVE)


def attend_forward(packed):
    seq_queries, seq_keys, seq_values, seq_segments = packed
    length = seq_queries.shape[0]
    block_rows = min(512, length)
    scores = masked_scores(seq_queries, seq_keys, seq_segments, 0, block_rows)
    top_score = jnp.max(scores, -1, keepdims=True)
    weights = jnp.exp(scores - top_score)
    denominator = jnp.sum(weights, -1, keepdims=True)
    probability = (weights / denominator).astype(jnp.bfloat16)
    contexts = [
        jnp.einsum("hqk,khd->qhd", probability, seq_values, preferred_element_type=jnp.float32)
    ]
    log_totals = [top_score + jnp.log(denominator)]
    return (jnp.concatenate(contexts, 0), jnp.concatenate(log_totals, 1))


def attend_backward(packed):
    seq_queries, seq_keys, seq_values, seq_segments, seq_log_total, seq_grad_context = packed
    length = seq_queries.shape[0]
    block_rows = min(512, length)
    grad_keys = jnp.zeros(seq_keys.shape, jnp.float32)
    grad_values = jnp.zeros(seq_values.shape, jnp.float32)
    scores = masked_scores(seq_queries, seq_keys, seq_segments, 0, block_rows)
    probability = jnp.exp(scores - seq_log_total[:, 0:block_rows])
    grad_prob = jnp.einsum(
        "qhd,khd->hqk", seq_grad_context, seq_values, preferred_element_type=jnp.float32
    )
    row_dot = jnp.sum(probability * grad_prob, -1, keepdims=True)
    grad_scores = (probability * (grad_prob - row_dot)).astype(jnp.bfloat16)
    grad_queries = [
        jnp.einsum("hqk,khd->qhd", grad_scores, seq_keys, preferred_element_type=jnp.float32)
    ]
    grad_keys = grad_keys + jnp.einsum(
        "hqk,qhd->khd", grad_scores, seq_queries, preferred_element_type=jnp.float32
    )
    grad_values = grad_values + jnp.einsum(
        "hqk,qhd->khd",
        probability.astype(jnp.bfloat16),
        seq_grad_context,
        preferred_element_type=jnp.float32,
    )
    return (jnp.concatenate(grad_queries, 0), grad_keys, grad_values)


def contract_rows(left_side, right_side):
    return lax.dot_general(
        left_side, right_side, (((0,), (0,)), ((), ())), preferred_element_type=jnp.float32
    )


def contract_cols(left_side, right_side):
    return lax.dot_general(
        left_side, right_side, (((1,), (1,)), ((), ())), preferred_element_type=jnp.float32
    )


def norm_back(grad_normed_out, normed, inverse_std, gain_full):
    grad_normed = grad_normed_out * gain_full
    return inverse_std * (
        grad_normed
        - jnp.mean(grad_normed, -1, keepdims=True)
        - normed * jnp.mean(grad_normed * normed, -1, keepdims=True)
    )


def local(
    tokens,
    segment_ids,
    norm_gain,
    norm_bias,
    qkv_weight,
    qkv_bias,
    out_weight,
    gate_weight,
    up_weight,
    down_weight,
    cotangent,
):
    row_count = tokens.shape[0]
    seq_count, length = segment_ids.shape
    head_count = qkv_weight.shape[1] // (3 * DH)
    score_scale = DH ** (-0.5)
    inputs = tokens.astype(jnp.float32)
    row_mean = jnp.mean(inputs, -1, keepdims=True)
    centered = inputs - row_mean
    inverse_std = lax.rsqrt(jnp.mean(centered * centered, -1, keepdims=True) + EPSILON)
    normed = centered * inverse_std
    gain_full = norm_gain.astype(jnp.float32)
    hidden_in = (normed * gain_full + norm_bias.astype(jnp.float32)).astype(jnp.bfloat16)
    joined_qkv = (
        jnp.dot(hidden_in, qkv_weight, preferred_element_type=jnp.float32)
        + qkv_bias.astype(jnp.float32)
    ).reshape(row_count, head_count, 3, DH)
    positions = positions_of(segment_ids).reshape(row_count)
    cosine, sine_table = rotary_tables(positions)
    queries = (rotate(joined_qkv[:, :, 0], cosine, sine_table) * score_scale).astype(jnp.bfloat16)
    key_rows = rotate(joined_qkv[:, :, 1], cosine, sine_table).astype(jnp.bfloat16)
    value_rows = joined_qkv[:, :, 2].astype(jnp.bfloat16)
    seq_shape = (seq_count, length, head_count, DH)
    seq_queries = queries.reshape(seq_shape)
    seq_keys = key_rows.reshape(seq_shape)
    seq_values = value_rows.reshape(seq_shape)
    context, log_total = lax.map(attend_forward, (seq_queries, seq_keys, seq_values, segment_ids))
    context = context.reshape(row_count, head_count * DH).astype(jnp.bfloat16)
    gate_pre = jnp.dot(hidden_in, gate_weight, preferred_element_type=jnp.float32)
    up_pre = jnp.dot(hidden_in, up_weight, preferred_element_type=jnp.float32)
    sigmoid_gate = jax.nn.sigmoid(gate_pre)
    activated = gate_pre * sigmoid_gate
    mixed = (activated * up_pre).astype(jnp.bfloat16)
    partial_out = jnp.dot(context, out_weight, preferred_element_type=jnp.float32) + jnp.dot(
        mixed, down_weight, preferred_element_type=jnp.float32
    )
    summed = lax.psum(partial_out, "tensor")
    output = (inputs + summed).astype(jnp.bfloat16)
    grad_context = contract_cols(cotangent, out_weight).astype(jnp.bfloat16)
    grad_out_w = contract_rows(context, cotangent)
    grad_down_w = contract_rows(mixed, cotangent)
    grad_out_part, grad_down_part = (
        lax.psum_scatter(grad_out_w, "dp", scatter_dimension=1, tiled=True),
        lax.psum_scatter(grad_down_w, "dp", scatter_dimension=1, tiled=True),
    )
    grad_mixed = contract_cols(cotangent, down_weight)
    grad_up = (grad_mixed * activated).astype(jnp.bfloat16)
    grad_gate = (
        grad_mixed * up_pre * sigmoid_gate * (1.0 + gate_pre * (1.0 - sigmoid_gate))
    ).astype(jnp.bfloat16)
    grad_gate_w = contract_rows(hidden_in, grad_gate)
    grad_up_w = contract_rows(hidden_in, grad_up)
    grad_hidden = contract_cols(grad_gate, gate_weight) + contract_cols(grad_up, up_weight)
    grad_queries, grad_keys, grad_values = lax.map(
        attend_backward,
        (
            seq_queries,
            seq_keys,
            seq_values,
            segment_ids,
            log_total,
            grad_context.reshape(seq_shape),
        ),
    )
    flat_shape = (row_count, head_count, DH)
    grad_queries = rotate_back(grad_queries.reshape(flat_shape) * score_scale, cosine, sine_table)
    grad_keys = rotate_back(grad_keys.reshape(flat_shape), cosine, sine_table)
    grad_joined = (
        jnp.stack([grad_queries, grad_keys, grad_values.reshape(flat_shape)], axis=2)
        .reshape(row_count, head_count * 3 * DH)
        .astype(jnp.bfloat16)
    )
    bias_local = jnp.sum(grad_joined.astype(jnp.float32), 0)
    grad_qkv_w = contract_rows(hidden_in, grad_joined)
    grad_hidden = grad_hidden + contract_cols(grad_joined, qkv_weight)
    grad_qkv_part, grad_gate_part, grad_up_part = (
        lax.psum_scatter(grad_qkv_w, "dp", scatter_dimension=0, tiled=True),
        lax.psum_scatter(grad_gate_w, "dp", scatter_dimension=0, tiled=True),
        lax.psum_scatter(grad_up_w, "dp", scatter_dimension=0, tiled=True),
    )
    grad_total = lax.psum(grad_hidden, "tensor")
    grad_input = (
        cotangent.astype(jnp.float32) + norm_back(grad_total, normed, inverse_std, gain_full)
    ).astype(jnp.bfloat16)
    grad_gain, grad_shift, grad_bias = lax.psum(
        (jnp.sum(grad_total * normed, 0), jnp.sum(grad_total, 0), bias_local), "dp"
    )
    return (
        output,
        grad_input,
        grad_gain,
        grad_shift,
        grad_qkv_part,
        grad_bias,
        grad_out_part,
        grad_gate_part,
        grad_up_part,
        grad_down_part,
    )


BF = jnp.bfloat16
F32 = jnp.float32
MESH = pl.DeviceIdType.MESH
W = 256
PR = 32
SMALL_AT = 2
LATE = 8
WAIT2 = 2


def comm_kernel(
    dims,
    hid_h, cot_h, tok_h, ctx_h, gj_h, z_h, gu_h, gain_ref, bias_ref, qkv_h, gate_h, up_h, down_h,
    out_o, gin_o, sg_o, ss_o, sb_o, gq_o, go_o, gg_o, gu_o, gd_o,
    hid_t, cot, cot_s, tok, ctx, gj, w_a, w_b, w_d, acc, gu, s1, own, recv1, recv2, recv3,
    zs, ze, zm, svb, svr, svq,
    ld_sem, w_sem, s1_send, s1_recv, s2_send, s2_recv, s3_send, s3_recv,
    e_send, e_recv, m_send, m_recv, o_send, o_recv, o_loc, g_sem, v_send, v_recv,
):
    rows, width, full, tail, n_out, n_qkv, n_batch = dims
    n_piece = rows // PR
    hid = zs.at[1]
    t0 = full * W
    b_pairs = n_out + n_qkv
    b_left = b_pairs + 2 * full
    b_up = b_left + 1
    dp = lax.axis_index("dp")
    zi = lax.axis_index("tensor")
    c = lax.rem(dp, 2)
    x = lax.rem(dp // 2, 2)
    y = dp // 4
    core_dev = {"dp": dp + 1 - 2 * c}
    x_dev = {"dp": dp + 2 - 4 * x}
    y_dev = {"dp": dp + 4 - 8 * y}
    is_mid = (zi == 1) | (zi == 2)
    is_end = (zi == 0) | (zi == 3)
    end_of = jnp.where(zi == 1, 0, 3)
    mid_of_end = jnp.where(zi == 0, 1, 2)
    end_dev = {"tensor": end_of}
    mid_dev = {"tensor": mid_of_end}
    other_mid = {"tensor": 3 - zi}

    def load(src, dst, k):
        return pltpu.make_async_copy(src, dst, ld_sem.at[k])

    def w_down(i):
        return pltpu.make_async_copy(down_h.at[pl.ds(i * W, W), :], w_d, w_sem.at[2])

    def w_gate(i):
        return pltpu.make_async_copy(gate_h.at[:, pl.ds(i * W, W)], w_a, w_sem.at[0])

    def w_up(i):
        return pltpu.make_async_copy(up_h.at[:, pl.ds(i * W, W)], w_b, w_sem.at[1])

    def w_qkv(j, side):
        return pltpu.make_async_copy(qkv_h.at[:, pl.ds(j * W, W)], (w_a, w_b)[side], w_sem.at[side])

    w_gate_t = pltpu.make_async_copy(gate_h.at[:, pl.ds(t0, tail)], w_a.at[:, 0:tail], w_sem.at[0])
    w_up_t = pltpu.make_async_copy(up_h.at[:, pl.ds(t0, tail)], w_a.at[:, tail : 2 * tail], w_sem.at[1])
    w_down_t = pltpu.make_async_copy(down_h.at[pl.ds(t0, tail), :], w_d.at[0:tail, :], w_sem.at[2])

    ctx_ld = load(ctx_h, ctx, 0)
    hid_ld = load(hid_h, hid, 1)
    cot_ld = load(cot_h, cot, 2)
    gj_ld = load(gj_h, gj, 3)
    tok_ld = load(tok_h, tok, 4)
    cs_ld = [
        load(cot_h.at[:, (2 * q + s) * W : (2 * q + s + 1) * W], cot_s.at[s, :, q * W : (q + 1) * W], 5 + 2 * q + s)
        for q in range(4)
        for s in range(2)
    ]
    z_ld = load(z_h, zs.at[0], 13)
    gu_ld = load(gu_h, gu, 14)
    z_ld.start()
    ctx_ld.start()
    for cp in cs_ld:
        cp.start()
    hid_ld.start()
    w_qkv(0, 0).start()
    gj_ld.start()
    w_qkv(1, 1).start()
    w_down(0).start()
    tok_ld.start()
    cot_ld.start()
    gu_ld.start()
    acc[...] = jnp.zeros_like(acc)

    barrier = pltpu.get_barrier_semaphore()
    for dev in (core_dev, x_dev, y_dev, {"dp": dp + 2 - 4 * x + 4 - 8 * y}):
        pl.semaphore_signal(barrier, inc=1, device_id=dev, device_id_type=MESH)

    @pl.when(is_mid)
    def _():
        pl.semaphore_signal(barrier, inc=1, device_id=end_dev, device_id_type=MESH)
        pl.semaphore_signal(barrier, inc=1, device_id=other_mid, device_id_type=MESH)

    @pl.when(is_end)
    def _():
        pl.semaphore_signal(barrier, inc=1, device_id=mid_dev, device_id_type=MESH)

    pl.semaphore_wait(barrier, jnp.where(is_mid, 6, 5))

    def rdma(src, dst, send, recv, dev):
        return pltpu.make_async_remote_copy(
            src_ref=src, dst_ref=dst, send_sem=send, recv_sem=recv, device_id=dev, device_id_type=MESH
        )

    def c1(b):
        slot = lax.rem(b, 4)
        return rdma(s1.at[slot], recv1.at[b], s1_send.at[slot], s1_recv.at[b], core_dev)

    def c2(b, h):
        if h == 0:
            return rdma(recv1.at[b, :, 1 - x, 0], recv2.at[b, 0], s2_send.at[b, 0], s2_recv.at[b, 0], x_dev)
        return rdma(recv1.at[b, 1 - y, :, 1], recv2.at[b, 1], s2_send.at[b, 1], s2_recv.at[b, 1], y_dev)

    def c3(b, h):
        if h == 0:
            return rdma(recv2.at[b, 0, 1 - y], recv3.at[b, 0], s3_send.at[b, 0], s3_recv.at[b, 0], y_dev)
        return rdma(recv2.at[b, 1, 1 - x], recv3.at[b, 1], s3_send.at[b, 1], s3_recv.at[b, 1], x_dev)

    def up32(v):
        return v.astype(F32)

    def ev1(b):
        slot = lax.rem(b, 4)
        c1(b).wait_recv()
        for yy in range(2):
            for xx in range(2):
                for h in range(2):
                    recv1[b, yy, xx, h] += own[slot, yy, xx, h]
        c2(b, 0).start()
        c2(b, 1).start()

    def ev2(b):
        c2(b, 0).wait_recv()
        c2(b, 1).wait_recv()
        for k in range(2):
            recv2[b, 0, k] += recv1[b, k, x, 0]
            recv2[b, 1, k] += recv1[b, y, k, 1]
        c3(b, 0).start()
        c3(b, 1).start()

    def cut(b, h, ref, row, col, n=W // 2, lo=0, wide=W):
        if not isinstance(row, int):
            row = pl.multiple_of(row, 64)
        if not isinstance(col, int):
            col = pl.multiple_of(col, W // 2)
        return pltpu.make_async_copy(
            recv3.at[b, h, 0:n, lo : lo + wide], ref.at[pl.ds(row + h * n, n), pl.ds(col, wide)], g_sem.at[b, h]
        )

    groups = (
        (0, n_out, 1, lambda b, h, i: (cut(b, h, go_o, i * W, 0),)),
        (n_out, n_qkv, 1, lambda b, h, i: (cut(b, h, gq_o, 0, i * W),)),
        (b_left, 1, 1, lambda b, h, i: (cut(b, h, gd_o, t0, 0, tail // 2),)),
        (b_pairs, full, 2, lambda b, h, i: (cut(b, h, gd_o, i * W, 0),)),
        (b_pairs + 1, full, 2, lambda b, h, i: (cut(b, h, gg_o, 0, i * W),)),
        (b_up, full, 1, lambda b, h, i: (cut(b, h, gu_o, 0, i * W),)),
        (
            b_up + full, 1, 1,
            lambda b, h, i: (
                cut(b, h, gg_o, 0, t0, wide=tail), cut(b, h, gu_o, 0, t0, lo=tail, wide=tail)
            ),
        ),
    )

    def ev3(b):
        c3(b, 0).wait_recv()
        c3(b, 1).wait_recv()
        recv3[b, 0] += recv2[b, 0, y]
        recv3[b, 1] += recv2[b, 1, x]
        for first, count, step, make in groups:
            here = (b >= first) & (b < first + count * step)
            if step > 1:
                here = here & (lax.rem(b - first, step) == 0)

            @pl.when(here)
            def _(first=first, step=step, make=make):
                for h in range(2):
                    for cp in make(b, h, (b - first) // step):
                        cp.start()

    def before_put(b):
        @pl.when(b >= 4)
        def _():
            c1(b - 4).wait_send()

    def after_put(b):
        c1(b).start()

    def put_rows(b, grad):
        slot = lax.rem(b, 4)
        before_put(b)
        for part, dst in ((1 - c, s1), (c, own)):
            left = hid_t[:, part].reshape(4 * W, rows)
            res = jnp.dot(left, grad, preferred_element_type=F32).astype(BF)
            dst[slot] = res.reshape(2, 2, 2, W // 2, W)
        after_put(b)

    def put_cols(b, left_t):
        slot = lax.rem(b, 4)
        h = left_t.shape[0]
        before_put(b)
        for part, dst in ((1 - c, s1), (c, own)):
            res = jnp.dot(left_t, cot_s[part], preferred_element_type=F32).astype(BF)
            for q in range(4):
                piece = res[:, q * W : (q + 1) * W].reshape(2, h // 2, W)
                dst[slot, q // 2, q % 2, :, 0 : h // 2, :] = piece
                if h < W:
                    dst[slot, q // 2, q % 2, :, h // 2 :, :] = jnp.zeros((2, (W - h) // 2, W), BF)
        after_put(b)

    NB = 512

    def acc_rows(grad, w_ref):
        for n in range(width // NB):
            cols = slice(n * NB, (n + 1) * NB)
            acc[:, cols] += lax.dot_general(
                grad, w_ref[cols, :], (((1,), (1,)), ((), ())), preferred_element_type=F32
            )

    def z_rows(p):
        return pl.ds(pl.multiple_of(p * PR, PR), PR)

    def ce(a, p):
        i = a * n_piece + p
        return rdma(zs.at[a, z_rows(p)], ze.at[a, z_rows(p)], e_send.at[i], e_recv.at[i], mid_dev)

    def cm(a, p):
        i = a * n_piece + p
        return rdma(zs.at[a, z_rows(p)], zm.at[a, z_rows(p)], m_send.at[i], m_recv.at[i], other_mid)

    def co(a, p, ref):
        i = a * n_piece + p
        return rdma(ze.at[a, z_rows(p)], ref.at[z_rows(p)], o_send.at[i], o_recv.at[i], end_dev)

    def cl(a, p, ref):
        i = a * n_piece + p
        return pltpu.make_async_copy(ze.at[a, z_rows(p)], ref.at[z_rows(p)], o_loc.at[i])

    def ev_e(e):
        a, p = e // n_piece, lax.rem(e, n_piece)

        @pl.when(is_mid)
        def _():
            ce(a, p).wait_recv()
            r = z_rows(p)
            zs[a, r, :] += ze[a, r, :]
            cm(a, p).start()

    def norm_rows(r):
        v = up32(tok[r, :])
        mu = jnp.mean(v, -1, keepdims=True)
        v = v - mu
        inv = lax.rsqrt(jnp.mean(v * v, -1, keepdims=True) + EPSILON)
        return v * inv, inv

    def ev_m(e):
        a, p = e // n_piece, lax.rem(e, n_piece)

        @pl.when(is_mid)
        def _():
            cm(a, p).wait_recv()
            r = z_rows(p)

            @pl.when(a == 0)
            def _():
                total = up32(zs[0, r, :]) + up32(zm[0, r, :])
                ze[0, r, :] = (up32(tok[r, :]) + total).astype(BF)
                co(0, p, out_o).start()
                cl(0, p, out_o).start()

            @pl.when(a == 1)
            def _():
                total = up32(zs[1, r, :]) + up32(zm[1, r, :])
                normed, inv = norm_rows(r)
                back = norm_back(total, normed, inv, gain_ref[...])
                ze[1, r, :] = (up32(cot[r, :]) + back).astype(BF)
                co(1, p, gin_o).start()
                cl(1, p, gin_o).start()

    def act_of(g, u):
        return (g * jax.nn.sigmoid(g) * u).astype(BF)

    def joined_grad(j):
        return jnp.concatenate([gj[2 * j], gj[2 * j + 1]], axis=1)

    def cv(k, dev):
        return rdma(svb.at[k], svr.at[k], v_send.at[k], v_recv.at[k], dev)

    def cw(k, dev):
        return rdma(svb.at[4], svq.at[y, x], v_send.at[4 + k], v_recv.at[4 + k], dev)

    square = (x_dev, y_dev, {"dp": dp + 2 - 4 * x + 4 - 8 * y})

    def small_1():
        @pl.when(is_mid)
        def _():
            cv(0, end_dev).wait_recv()
            svb[1] = svb[0] + svr[0]
            cv(1, other_mid).start()

    def small_2():
        @pl.when(is_mid)
        def _():
            cv(1, other_mid).wait_recv()
            svb[2] = svb[1] + svr[1]
            svb[3, 0:2, :] = svb[2, 0:2, :]
            cv(2, end_dev).start()

    def small_3():
        @pl.when(is_end)
        def _():
            cv(2, mid_dev).wait_recv()
            svb[3, 0:2, :] = svr[2, 0:2, :]

        svb[3, 2:8, :] = svb[0, 2:8, :]
        cv(3, core_dev).start()

    def small_4():
        cv(3, core_dev).wait_recv()
        svb[4] = svb[3] + svr[3]
        svq[y, x] = svb[4]
        for k, dev in enumerate(square):
            cw(k, dev).start()

    def small_5():
        for k, dev in enumerate(square):
            cw(k, dev).wait_recv()
        total = (svq[0, 0] + svq[0, 1]) + (svq[1, 0] + svq[1, 1])
        for row, ref in enumerate((sg_o, ss_o, sb_o)):
            for n in range(ref.shape[0]):
                ref[n : n + 1, :] = total[row : row + 1, n * 128 : (n + 1) * 128]

    def small_sent():
        @pl.when(is_end)
        def _():
            cv(0, mid_dev).wait_send()

        @pl.when(is_mid)
        def _():
            cv(1, other_mid).wait_send()
            cv(2, end_dev).wait_send()

        cv(3, core_dev).wait_send()
        for k, dev in enumerate(square):
            cw(k, dev).wait_send()

    def send_line(a):
        def send(p, keep):
            ce(a, p).start()
            return keep

        @pl.when(is_end)
        def _():
            if a == 1:
                cv(0, mid_dev).start()
            lax.fori_loop(0, n_piece, send, 0)

    def line_rows(p, keep):
        r = z_rows(p)
        v = acc[r, :]
        zs[1, r, :] = v.astype(BF)
        normed, _inv = norm_rows(r)
        svb[0, 0:1, :] += jnp.sum(v * normed, 0, keepdims=True)
        svb[0, 1:2, :] += jnp.sum(v, 0, keepdims=True)
        return keep

    z_ld.wait()
    send_line(0)
    ctx_ld.wait()
    for cp in cs_ld:
        cp.wait()
    for j in range(n_out):
        put_cols(jnp.int32(j), ctx[:, j * W : (j + 1) * W].T)
    hid_ld.wait()
    for q in range(4):
        for s in range(2):
            lo = (2 * q + s) * W
            hid_t[q, s] = hid[:, lo : lo + W].T
    for b in range(n_out):
        ev1(jnp.int32(b))
    gj_ld.wait()
    tok_ld.wait()
    cot_ld.wait()

    def joined(n, keep):
        for side in range(2):
            j = 2 * n + side
            w_qkv(j, side).wait()
            acc_rows(joined_grad(j), (w_a, w_b)[side])

            @pl.when(j + 2 < n_qkv)
            def _(j=j, side=side):
                w_qkv(j + 2, side).start()

            @pl.when(j + 2 >= n_qkv)
            def _(side=side):
                (w_gate, w_up)[side](0).start()

            b = n_out + j
            put_rows(b, joined_grad(j))

            @pl.when(j >= 1)
            def _(b=b):
                ev1(b - 1)

        ev_e(n)

        @pl.when(n >= 1)
        def _():
            ev2(n - 1)

        @pl.when(n >= 2)
        def _():
            ev_m(n - 2)

        return keep

    lax.fori_loop(0, n_qkv // 2, joined, 0)
    gu_ld.wait()

    def gate_grads(gm, g, u):
        sg = jax.nn.sigmoid(g)
        g_up = (gm * (g * sg)).astype(BF)
        g_gate = (gm * u * sg * (1.0 + g * (1.0 - sg))).astype(BF)
        return g_gate, g_up

    def cols_t(left, w_ref, k):
        return lax.dot_general(left, w_ref[0:k, :], (((1,), (1,)), ((), ())), preferred_element_type=F32)

    e0 = n_qkv // 2
    two = n_qkv // 2 - 1

    def bwd(i, keep):
        w_down(i).wait()
        gm = cols_t(cot[...], w_d, W)

        @pl.when(i + 1 < full)
        def _():
            w_down(i + 1).start()

        @pl.when(i + 1 == full)
        def _():
            w_down_t.start()

        g, u = up32(gu[i, 0]), up32(gu[i, 1])
        mixed = act_of(g, u)
        g_gate, g_up = gate_grads(gm, g, u)
        gu[i, 0] = g_gate
        gu[i, 1] = g_up
        w_gate(i).wait()
        acc_rows(g_gate, w_a)
        w_up(i).wait()
        acc_rows(g_up, w_b)

        @pl.when(i + 1 < full)
        def _():
            w_gate(i + 1).start()
            w_up(i + 1).start()

        @pl.when(i + 1 == full)
        def _():
            w_gate_t.start()
            w_up_t.start()

        b = b_pairs + 2 * i
        e = e0 + 2 * i
        put_cols(b, mixed.T)
        ev1(b - 1)
        ev_e(e)
        ev_m(e - 2)
        put_rows(b + 1, gu[i, 0])
        ev1(b)
        ev2(two + i)
        ev_e(e + 1)
        ev_m(e - 1)
        return keep

    lax.fori_loop(0, full, bwd, 0)
    w_down_t.wait()
    gm = cols_t(cot[...], w_d, tail)
    both = up32(gu[full, 0])
    mixed = act_of(both[:, 0:tail], both[:, tail:])
    g_gate, g_up = gate_grads(gm, both[:, 0:tail], both[:, tail:])
    both = jnp.concatenate([g_gate, g_up], axis=1)
    gu[full, 0] = both
    w_gate_t.wait()
    w_up_t.wait()
    acc_rows(both, w_a)
    svb[0] = jnp.zeros_like(svb[0])
    svb[0, 2:3, 0 : n_qkv * W] = bias_ref[...]
    lax.fori_loop(0, n_piece, line_rows, 0)
    send_line(1)

    put_cols(jnp.int32(b_left), mixed.T)
    ev1(jnp.int32(b_left - 1))
    e0 = e0 + 2 * full
    two = two + full
    ev2(jnp.int32(two))
    ev_e(jnp.int32(e0))
    ev_m(jnp.int32(e0 - 2))

    def left_over(i, keep):
        b = b_up + i
        at = jnp.where(i == full, 0, 1)
        put_rows(b, gu[i, at])
        ev1(b - 1)
        ev2(two + 1 + i)
        ev_e(e0 + 1 + i)
        ev_m(e0 - 1 + i)
        return keep

    lax.fori_loop(0, full + 1, left_over, 0)
    ev1(jnp.int32(n_batch - 1))
    e0 = e0 + full + 2
    two_left = two + full + 2

    n_e = 2 * n_piece
    smalls = (small_1, small_2, small_3, small_4)

    def drain(k, keep):
        @pl.when(k + e0 < n_e)
        def _():
            ev_e(k + e0)

        @pl.when(k + e0 - 2 < n_e)
        def _():
            ev_m(k + e0 - 2)

        @pl.when((k >= WAIT2) & (k - WAIT2 + two_left < n_batch))
        def _():
            ev2(k - WAIT2 + two_left)

        for i, small in enumerate(smalls):
            pl.when(k == SMALL_AT + i)(small)

        for h in range(2):
            b = 2 * (k - LATE) + h

            @pl.when((b >= 0) & (b < n_batch))
            def _():
                ev3(b)

        return keep

    steps = max(LATE + (n_batch + 1) // 2, n_e - e0 + 2, WAIT2 + n_batch - two_left)
    lax.fori_loop(0, steps, drain, 0)
    small_5()

    small_sent()

    def finish(b, keep):
        for h in range(2):
            c2(b, h).wait_send()
            c3(b, h).wait_send()
        return keep

    lax.fori_loop(0, n_batch, finish, 0)
    for k in range(4):
        c1(jnp.int32(n_batch - 4 + k)).wait_send()
    for first, count, step, make in groups:
        for i in range(count):
            for h in range(2):
                for cp in make(first + i * step, h, i):
                    cp.wait()

    def finish_line(p, keep):
        for a, ref in ((0, out_o), (1, gin_o)):
            @pl.when(is_mid)
            def _():
                cm(a, p).wait_send()
                co(a, p, ref).wait_send()
                cl(a, p, ref).wait()

            @pl.when(is_end)
            def _():
                ce(a, p).wait_send()
                co(a, p, ref).wait_recv()

        return keep

    lax.fori_loop(0, n_piece, finish_line, 0)


def comm_call(hidden, cot, tokens, ctx, gj, partial, gu, gain, bias_sum, qkv_w, gate_w, up_w, down_w):
    rows, width = hidden.shape
    hd = ctx.shape[1]
    ff = gate_w.shape[1]
    full, tail = ff // W, ff % W
    n_out, n_qkv = hd // W, qkv_w.shape[1] // W
    n_batch = n_out + full + 1 + n_qkv + 2 * full + 1
    n_z = 2 * (rows // PR)
    dims = (rows, width, full, tail, n_out, n_qkv, n_batch)
    piece = (W // 2, W)
    vm, dma = pltpu.VMEM, pltpu.SemaphoreType.DMA
    any_spec = pl.BlockSpec(memory_space=pl.ANY)
    vm_spec = pl.BlockSpec(memory_space=pltpu.VMEM)
    return pl.pallas_call(
        functools.partial(comm_kernel, dims),
        out_shape=(
            jax.ShapeDtypeStruct((rows, width), BF),
            jax.ShapeDtypeStruct((rows, width), BF),
            jax.ShapeDtypeStruct((width // 128, 128), F32),
            jax.ShapeDtypeStruct((width // 128, 128), F32),
            jax.ShapeDtypeStruct((n_qkv * W // 128, 128), F32),
            jax.ShapeDtypeStruct((W, n_qkv * W), BF),
            jax.ShapeDtypeStruct((hd, W), BF),
            jax.ShapeDtypeStruct((W, ff), BF),
            jax.ShapeDtypeStruct((W, ff), BF),
            jax.ShapeDtypeStruct((ff, W), BF),
        ),
        in_specs=[any_spec] * 7 + [vm_spec] * 2 + [any_spec] * 4,
        out_specs=(any_spec,) * 2 + (vm_spec,) * 3 + (any_spec,) * 5,
        scratch_shapes=[
            vm((4, 2, W, rows), BF),
            vm((rows, width), BF),
            vm((2, rows, width // 2), BF),
            vm((rows, width), BF),
            vm((rows, hd), BF),
            vm((2 * n_qkv, rows, W // 2), BF),
            vm((width, W), BF),
            vm((width, W), BF),
            vm((W, width), BF),
            vm((rows, width), F32),
            vm((full + 1, 2, rows, W), BF),
            vm((4, 2, 2, 2) + piece, BF),
            vm((4, 2, 2, 2) + piece, BF),
            vm((n_batch, 2, 2, 2) + piece, BF),
            vm((n_batch, 2, 2) + piece, BF),
            vm((n_batch, 2) + piece, BF),
            vm((2, rows, width), BF),
            vm((2, rows, width), BF),
            vm((2, rows, width), BF),
            vm((5, 8, width), F32),
            vm((4, 8, width), F32),
            vm((2, 2, 8, width), F32),
            dma((15,)),
            dma((3,)),
            dma((4,)),
            dma((n_batch,)),
            dma((n_batch, 2)),
            dma((n_batch, 2)),
            dma((n_batch, 2)),
            dma((n_batch, 2)),
            dma((n_z,)),
            dma((n_z,)),
            dma((n_z,)),
            dma((n_z,)),
            dma((n_z,)),
            dma((n_z,)),
            dma((n_z,)),
            dma((n_batch, 2)),
            dma((7,)),
            dma((7,)),
        ],
        compiler_params=pltpu.CompilerParams(
            collective_id=0, has_side_effects=True, vmem_limit_bytes=67043328
        ),
        name="ffn_and_sums",
    )(hidden, cot, tokens, ctx, gj, partial, gu, gain, bias_sum, qkv_w, gate_w, up_w, down_w)


def forward_kernel(full, tail, hid, ctx, out_w, gate_w, up_w, down_w, z_o, gu_o, acc):
    i = pl.program_id(0)
    width = acc.shape[1]
    blocks = [slice(n, n + 512) for n in range(0, width, 512)]

    def dot(a, b):
        return jnp.dot(a, b, preferred_element_type=F32)

    def act_of(g, u):
        return (g * jax.nn.sigmoid(g) * u).astype(BF)

    @pl.when(i == 0)
    def _():
        for cols in blocks:
            acc[:, cols] = dot(ctx[...], out_w[:, cols])

    @pl.when(i < full)
    def _():
        g = dot(hid[...], gate_w[...])
        u = dot(hid[...], up_w[...])
        gu_o[0, 0] = g.astype(BF)
        gu_o[0, 1] = u.astype(BF)
        mixed = act_of(g, u)
        for cols in blocks:
            acc[:, cols] += dot(mixed, down_w[:, cols])

    @pl.when(i == full)
    def _():
        both = dot(hid[...], jnp.concatenate([gate_w[:, 0:tail], up_w[:, 0:tail]], axis=1))
        gu_o[0, 0] = both.astype(BF)
        gu_o[0, 1] = jnp.zeros_like(both).astype(BF)
        mixed = act_of(both[:, 0:tail], both[:, tail:])
        for cols in blocks:
            z_o[:, cols] = (acc[:, cols] + dot(mixed, down_w[0:tail, cols])).astype(BF)


def forward_call(hidden, ctx, out_w, gate_w, up_w, down_w):
    rows, width = hidden.shape
    hd = ctx.shape[1]
    ff = gate_w.shape[1]
    full, tail = ff // W, ff % W
    once = lambda shape: pl.BlockSpec(shape, lambda i: (0,) * len(shape), pipeline_mode=pl.Buffered(1))
    return pl.pallas_call(
        functools.partial(forward_kernel, full, tail),
        grid=(full + 1,),
        out_shape=(
            jax.ShapeDtypeStruct((rows, width), BF),
            jax.ShapeDtypeStruct((full + 1, 2, rows, W), BF),
        ),
        in_specs=[
            once((rows, width)),
            once((rows, hd)),
            once((hd, width)),
            pl.BlockSpec((width, W), lambda i: (0, i)),
            pl.BlockSpec((width, W), lambda i: (0, i)),
            pl.BlockSpec((W, width), lambda i: (i, 0)),
        ],
        out_specs=(
            once((rows, width)),
            pl.BlockSpec((1, 2, rows, W), lambda i: (i, 0, 0, 0)),
        ),
        scratch_shapes=[pltpu.VMEM((rows, width), F32)],
        compiler_params=pltpu.CompilerParams(vmem_limit_bytes=60 << 20),
        name="forward",
    )(hidden, ctx, out_w, gate_w, up_w, down_w)


QB = 128
ROWS = 32


def attn_kernel(
    heads_scale, tok, seg_ref, gain_ref, shift_ref, b_ref, w_ref, ow_ref, cot,
    hid, ctx_o, gj_o, bias_o, gain_o,
    bias_m, tab, s_m, g_m, p_m, gs_m, shift_m, b_m,
):
    rows = tok.shape[0]
    nq = rows // QB
    half = ROT // 2

    step = pl.program_id(0)

    @pl.when(step == 0)
    def _():
        for n in range(gain_ref.shape[0]):
            cols = slice(n * QB, (n + 1) * QB)
            gain_o[0:1, cols] = gain_ref[n : n + 1, :].astype(F32)
            shift_m[0:1, cols] = shift_ref[n : n + 1, :].astype(F32)
        b_m[...] = b_ref[...].astype(F32)

        def norm_step(n, keep):
            r = pl.ds(pl.multiple_of(n * 64, 64), 64)
            v = tok[r, :].astype(F32)
            v = v - jnp.mean(v, -1, keepdims=True)
            v = v * lax.rsqrt(jnp.mean(v * v, -1, keepdims=True) + EPSILON)
            hid[r, :] = (v * gain_o[...] + shift_m[...]).astype(BF)
            return keep

        lax.fori_loop(0, rows // 64, norm_step, 0)
        seg = seg_ref[...].astype(F32)
        seg_t = jnp.broadcast_to(seg, (8, rows)).T
        lane = lax.broadcasted_iota(jnp.int32, (QB, QB), 1)
        head_lane = lane % DH
        freq = jnp.ones((1, QB), F32)
        for n in range(1, half):
            freq = jnp.where(head_lane[0:1] % half == n, 10000.0 ** (-2.0 * n / ROT), freq)
        for i in range(nq):
            lo = max(0, i - 2) * QB
            n = (i + 1) * QB - lo
            q_at = lax.broadcasted_iota(jnp.int32, (QB, n), 0) + i * QB
            k_at = lax.broadcasted_iota(jnp.int32, (QB, n), 1) + lo
            same = seg_t[i * QB : (i + 1) * QB, 0:1] == seg[:, lo : lo + n]
            allowed = same & (q_at >= k_at)
            bias_m[i, :, 0:n] = jnp.where(allowed, 0.0, NEGATIVE)
            place = jnp.sum(jnp.where(allowed, 1.0, 0.0), -1, keepdims=True) - 1.0
            angle = place * freq
            cosine, sine = jnp.cos(angle), jnp.sin(angle)
            for blk in range(3):
                live = head_lane < ROT
                if blk == 1:
                    live = live & (lane >= DH)
                if blk == 2:
                    live = live & (lane < DH)
                scale = jnp.ones((QB, QB), F32)
                if blk == 0:
                    scale = jnp.where(lane < DH, heads_scale, 1.0)
                if blk == 1:
                    scale = jnp.where(lane >= DH, heads_scale, 1.0)
                r = slice(i * QB, (i + 1) * QB)
                tab[blk, 0, r] = jnp.where(live, cosine, 1.0) * scale
                tab[blk, 1, r] = jnp.where(live & (head_lane < half), -sine, 0.0) * scale
                tab[blk, 2, r] = jnp.where(live & (head_lane >= half), sine, 0.0) * scale

    def dot_t(a, b):
        return lax.dot_general(a, b, (((1,), (1,)), ((), ())), preferred_element_type=F32)

    def dot(a, b):
        return jnp.dot(a, b, preferred_element_type=F32)

    joined = dot(hid[...], w_ref[...])
    turned = []
    for blk in range(3):
        v = joined[:, blk * QB : (blk + 1) * QB] + b_m[pl.ds(3 * step + blk, 1), :]
        v = v * tab[blk, 0] + pltpu.roll(v, QB - half, 1) * tab[blk, 1] + pltpu.roll(v, half, 1) * tab[blk, 2]
        turned.append(v.astype(BF))
    gctx = dot_t(cot[...], ow_ref[...]).astype(BF)
    lo_h, hi_h = slice(0, DH), slice(DH, 2 * DH)
    heads = (
        (turned[0][:, lo_h], turned[0][:, hi_h], turned[1][:, lo_h], gctx[:, lo_h]),
        (turned[1][:, hi_h], turned[2][:, lo_h], turned[2][:, hi_h], gctx[:, hi_h]),
    )
    spans = [(max(0, i - 2) * QB, (i + 1) * QB) for i in range(nq)]
    blocks = [(n, i) for i in range(nq) for n in range(2)]
    for n, i in blocks:
        q, k, v, gc = heads[n]
        lo, hi = spans[i]
        s_m[n, i, :, 0 : hi - lo] = dot_t(q[i * QB : hi], k[lo:hi])
        g_m[n, i, :, 0 : hi - lo] = dot_t(gc[i * QB : hi], v[lo:hi])
    for n, i in blocks:
        lo, hi = spans[i]
        for r in range(0, QB, ROWS):
            rr = slice(r, r + ROWS)
            s = s_m[n, i, rr, 0 : hi - lo] + bias_m[i, rr, 0 : hi - lo]
            e = jnp.exp(s - jnp.max(s, -1, keepdims=True))
            p = e * (1.0 / jnp.sum(e, -1, keepdims=True))
            gp = g_m[n, i, rr, 0 : hi - lo]
            p_m[n, i, rr, 0 : hi - lo] = p.astype(BF)
            gs_m[n, i, rr, 0 : hi - lo] = (p * (gp - jnp.sum(p * gp, -1, keepdims=True))).astype(BF)
    grads, contexts = [], []
    for n, (q, k, v, gc) in enumerate(heads):
        out, grad_q, grad_k, grad_v = [], [], [], []
        for i, (lo, hi) in enumerate(spans):
            out.append(dot(p_m[n, i, :, 0 : hi - lo], v[lo:hi]))
            grad_q.append(dot(gs_m[n, i, :, 0 : hi - lo], k[lo:hi]))
        for j in range(nq):
            top = min(j + 3, nq)

            def stack(part):
                cut = []
                for i in range(j, top):
                    at = j * QB - spans[i][0]
                    cut.append(part[n, i, :, at : at + QB].T)
                return jnp.concatenate(cut, 1)

            grad_k.append(dot(stack(gs_m), q[j * QB : top * QB]))
            grad_v.append(dot(stack(p_m), gc[j * QB : top * QB]))
        contexts.append(jnp.concatenate(out, 0))
        grads.append([jnp.concatenate(part, 0) for part in (grad_q, grad_k, grad_v)])
    ctx_o[...] = jnp.concatenate(contexts, 1).astype(BF)
    (q0, k0, v0), (q1, k1, v1) = grads
    for blk, pair in enumerate(((q0, k0), (v0, q1), (k1, v1))):
        g = jnp.concatenate(pair, 1)
        g = g * tab[blk, 0] - pltpu.roll(g, QB - half, 1) * tab[blk, 1] - pltpu.roll(g, half, 1) * tab[blk, 2]
        g = g.astype(BF)
        gj_o[blk] = g
        bias_o[:, blk * QB : (blk + 1) * QB] = jnp.sum(g.astype(F32), 0, keepdims=True)


def attn_call(tokens, segment_ids, gain, shift, qkv_w, qkv_b, out_w, cot):
    rows, width = tokens.shape
    hd = out_w.shape[0]
    steps = hd // (2 * DH)
    three = 3 * QB
    whole = lambda shape: pl.BlockSpec(shape, lambda i: (0,) * len(shape))
    once = lambda shape: pl.BlockSpec(shape, lambda i: (0,) * len(shape), pipeline_mode=pl.Buffered(1))
    return pl.pallas_call(
        functools.partial(attn_kernel, DH ** (-0.5)),
        grid=(steps,),
        out_shape=(
            jax.ShapeDtypeStruct((rows, width), BF),
            jax.ShapeDtypeStruct((rows, hd), BF),
            jax.ShapeDtypeStruct((3 * steps, rows, QB), BF),
            jax.ShapeDtypeStruct((1, 3 * hd), F32),
            jax.ShapeDtypeStruct((1, width), F32),
        ),
        in_specs=[
            once((rows, width)),
            whole((1, rows)),
            whole((width // QB, QB)),
            whole((width // QB, QB)),
            whole((3 * hd // QB, QB)),
            pl.BlockSpec((width, three), lambda i: (0, i)),
            pl.BlockSpec((QB, width), lambda i: (i, 0)),
            once((rows, width)),
        ],
        out_specs=(
            whole((rows, width)),
            pl.BlockSpec((rows, QB), lambda i: (0, i)),
            pl.BlockSpec((3, rows, QB), lambda i: (i, 0, 0)),
            pl.BlockSpec((1, three), lambda i: (0, i)),
            whole((1, width)),
        ),
        scratch_shapes=[
            pltpu.VMEM((rows // QB, QB, three), F32),
            pltpu.VMEM((3, 3, rows, QB), F32),
            pltpu.VMEM((2, rows // QB, QB, three), F32),
            pltpu.VMEM((2, rows // QB, QB, three), F32),
            pltpu.VMEM((2, rows // QB, QB, three), BF),
            pltpu.VMEM((2, rows // QB, QB, three), BF),
            pltpu.VMEM((1, width), F32),
            pltpu.VMEM((3 * hd // QB, QB), F32),
        ],
        compiler_params=pltpu.CompilerParams(vmem_limit_bytes=60 << 20),
        name="attention",
    )(
        tokens, segment_ids, gain.reshape(-1, QB), shift.reshape(-1, QB), qkv_b.reshape(-1, QB), qkv_w, out_w, cot
    )


def fast(
    n_dp,
    n_tensor,
    tokens,
    segment_ids,
    norm_gain,
    norm_bias,
    qkv_weight,
    qkv_bias,
    out_weight,
    gate_weight,
    up_weight,
    down_weight,
    cotangent,
):
    args = (tokens, segment_ids, norm_gain, norm_bias, qkv_weight, qkv_bias, out_weight, gate_weight, up_weight, down_weight, cotangent)
    row_count, width = tokens.shape
    ff = gate_weight.shape[1]
    fits = (
        (n_dp, n_tensor) == (8, 4)
        and segment_ids.shape == (1, row_count)
        and (row_count, width) == (512, 8 * W)
        and ff % W == W // 2
        and qkv_weight.shape[1] % (2 * W) == 0
        and out_weight.shape[0] % W == 0
        and qkv_weight.shape[1] == 3 * out_weight.shape[0]
        and 2 * DH == QB
    )
    if not fits:
        return local(*args)
    hidden_in, context, grad_joined, bias_local, gain_row = attn_call(
        tokens, segment_ids, norm_gain, norm_bias, qkv_weight, qkv_bias, out_weight, cotangent
    )
    partial, gate_up = forward_call(hidden_in, context, out_weight, gate_weight, up_weight, down_weight)
    output, grad_input, gain_sum, shift_sum, bias_sum, *sums = comm_call(
        hidden_in, cotangent, tokens, context, grad_joined, partial, gate_up, gain_row, bias_local,
        qkv_weight, gate_weight, up_weight, down_weight,
    )
    joined_w, out_w, gate_w, up_w, down_w = (v.astype(F32) for v in sums)
    return (
        output,
        grad_input,
        gain_sum.reshape(width),
        shift_sum.reshape(width),
        joined_w,
        bias_sum.reshape(qkv_weight.shape[1]),
        out_w,
        gate_w,
        up_w,
        down_w,
    )


def solution(mesh):
    body = functools.partial(fast, mesh.shape["dp"], mesh.shape["tensor"])
    return jax.shard_map(
        body,
        mesh=mesh,
        in_specs=(
            P("dp", None),
            P("dp", None),
            P(),
            P(),
            P(None, "tensor"),
            P("tensor"),
            P("tensor", None),
            P(None, "tensor"),
            P(None, "tensor"),
            P("tensor", None),
            P("dp", None),
        ),
        out_specs=(
            P("dp", None),
            P("dp", None),
            P(),
            P(),
            P("dp", "tensor"),
            P("tensor"),
            P("tensor", "dp"),
            P("dp", "tensor"),
            P("dp", "tensor"),
            P("tensor", "dp"),
        ),
        check_vma=False,
    )
```

```python
import functools

import jax
import jax.numpy as jnp
from jax import lax
from jax.experimental import pallas as pl
from jax.experimental.pallas import tpu as pltpu
from jax.sharding import PartitionSpec as P

DH = 64
ROT = 16


EPSILON = 1e-05
NEGATIVE = -1e30


def positions_of(segments):
    column = jnp.arange(segments.shape[1], dtype=jnp.int32)
    starts = jnp.concatenate(
        [jnp.ones((segments.shape[0], 1), dtype=bool), segments[:, 1:] != segments[:, :-1]], axis=1
    )
    doc_start = lax.cummax(jnp.where(starts, column[None, :], 0), axis=1)
    return column[None, :] - doc_start


def rotary_tables(positions):
    half_rot = ROT // 2
    frequency = jnp.power(10000.0, -2.0 * jnp.arange(half_rot, dtype=jnp.float32) / ROT)
    angles = positions.astype(jnp.float32)[:, None] * frequency[None, :]
    return (jnp.cos(angles)[:, None, :], jnp.sin(angles)[:, None, :])


def rotate(tensor, cosine, sine_table):
    half_rot = ROT // 2
    first_half = tensor[..., :half_rot]
    second_half = tensor[..., half_rot:ROT]
    return jnp.concatenate(
        [
            first_half * cosine - second_half * sine_table,
            second_half * cosine + first_half * sine_table,
            tensor[..., ROT:],
        ],
        axis=-1,
    )


def rotate_back(tensor, cosine, sine_table):
    half_rot = ROT // 2
    first_half = tensor[..., :half_rot]
    second_half = tensor[..., half_rot:ROT]
    return jnp.concatenate(
        [
            first_half * cosine + second_half * sine_table,
            second_half * cosine - first_half * sine_table,
            tensor[..., ROT:],
        ],
        axis=-1,
    )


def masked_scores(query_block, seq_keys, seq_segments, begin_row, block_rows):
    key_index = jnp.arange(seq_keys.shape[0], dtype=jnp.int32)
    allowed = (seq_segments[begin_row : begin_row + block_rows, None] == seq_segments[None, :]) & (
        key_index[:, None] >= key_index[None, :]
    )
    scores = jnp.einsum("qhd,khd->hqk", query_block, seq_keys, preferred_element_type=jnp.float32)
    return jnp.where(allowed[None], scores, NEGATIVE)


def attend_forward(packed):
    seq_queries, seq_keys, seq_values, seq_segments = packed
    length = seq_queries.shape[0]
    block_rows = min(512, length)
    scores = masked_scores(seq_queries, seq_keys, seq_segments, 0, block_rows)
    top_score = jnp.max(scores, -1, keepdims=True)
    weights = jnp.exp(scores - top_score)
    denominator = jnp.sum(weights, -1, keepdims=True)
    probability = (weights / denominator).astype(jnp.bfloat16)
    contexts = [
        jnp.einsum("hqk,khd->qhd", probability, seq_values, preferred_element_type=jnp.float32)
    ]
    log_totals = [top_score + jnp.log(denominator)]
    return (jnp.concatenate(contexts, 0), jnp.concatenate(log_totals, 1))


def attend_backward(packed):
    seq_queries, seq_keys, seq_values, seq_segments, seq_log_total, seq_grad_context = packed
    length = seq_queries.shape[0]
    block_rows = min(512, length)
    grad_keys = jnp.zeros(seq_keys.shape, jnp.float32)
    grad_values = jnp.zeros(seq_values.shape, jnp.float32)
    scores = masked_scores(seq_queries, seq_keys, seq_segments, 0, block_rows)
    probability = jnp.exp(scores - seq_log_total[:, 0:block_rows])
    grad_prob = jnp.einsum(
        "qhd,khd->hqk", seq_grad_context, seq_values, preferred_element_type=jnp.float32
    )
    row_dot = jnp.sum(probability * grad_prob, -1, keepdims=True)
    grad_scores = (probability * (grad_prob - row_dot)).astype(jnp.bfloat16)
    grad_queries = [
        jnp.einsum("hqk,khd->qhd", grad_scores, seq_keys, preferred_element_type=jnp.float32)
    ]
    grad_keys = grad_keys + jnp.einsum(
        "hqk,qhd->khd", grad_scores, seq_queries, preferred_element_type=jnp.float32
    )
    grad_values = grad_values + jnp.einsum(
        "hqk,qhd->khd",
        probability.astype(jnp.bfloat16),
        seq_grad_context,
        preferred_element_type=jnp.float32,
    )
    return (jnp.concatenate(grad_queries, 0), grad_keys, grad_values)


def contract_rows(left_side, right_side):
    return lax.dot_general(
        left_side, right_side, (((0,), (0,)), ((), ())), preferred_element_type=jnp.float32
    )


def contract_cols(left_side, right_side):
    return lax.dot_general(
        left_side, right_side, (((1,), (1,)), ((), ())), preferred_element_type=jnp.float32
    )


def norm_back(grad_normed_out, normed, inverse_std, gain_full):
    grad_normed = grad_normed_out * gain_full
    return inverse_std * (
        grad_normed
        - jnp.mean(grad_normed, -1, keepdims=True)
        - normed * jnp.mean(grad_normed * normed, -1, keepdims=True)
    )


def local(
    tokens,
    segment_ids,
    norm_gain,
    norm_bias,
    qkv_weight,
    qkv_bias,
    out_weight,
    gate_weight,
    up_weight,
    down_weight,
    cotangent,
):
    row_count = tokens.shape[0]
    seq_count, length = segment_ids.shape
    head_count = qkv_weight.shape[1] // (3 * DH)
    score_scale = DH ** (-0.5)
    inputs = tokens.astype(jnp.float32)
    row_mean = jnp.mean(inputs, -1, keepdims=True)
    centered = inputs - row_mean
    inverse_std = lax.rsqrt(jnp.mean(centered * centered, -1, keepdims=True) + EPSILON)
    normed = centered * inverse_std
    gain_full = norm_gain.astype(jnp.float32)
    hidden_in = (normed * gain_full + norm_bias.astype(jnp.float32)).astype(jnp.bfloat16)
    joined_qkv = (
        jnp.dot(hidden_in, qkv_weight, preferred_element_type=jnp.float32)
        + qkv_bias.astype(jnp.float32)
    ).reshape(row_count, head_count, 3, DH)
    positions = positions_of(segment_ids).reshape(row_count)
    cosine, sine_table = rotary_tables(positions)
    queries = (rotate(joined_qkv[:, :, 0], cosine, sine_table) * score_scale).astype(jnp.bfloat16)
    key_rows = rotate(joined_qkv[:, :, 1], cosine, sine_table).astype(jnp.bfloat16)
    value_rows = joined_qkv[:, :, 2].astype(jnp.bfloat16)
    seq_shape = (seq_count, length, head_count, DH)
    seq_queries = queries.reshape(seq_shape)
    seq_keys = key_rows.reshape(seq_shape)
    seq_values = value_rows.reshape(seq_shape)
    context, log_total = lax.map(attend_forward, (seq_queries, seq_keys, seq_values, segment_ids))
    context = context.reshape(row_count, head_count * DH).astype(jnp.bfloat16)
    gate_pre = jnp.dot(hidden_in, gate_weight, preferred_element_type=jnp.float32)
    up_pre = jnp.dot(hidden_in, up_weight, preferred_element_type=jnp.float32)
    sigmoid_gate = jax.nn.sigmoid(gate_pre)
    activated = gate_pre * sigmoid_gate
    mixed = (activated * up_pre).astype(jnp.bfloat16)
    partial_out = jnp.dot(context, out_weight, preferred_element_type=jnp.float32) + jnp.dot(
        mixed, down_weight, preferred_element_type=jnp.float32
    )
    summed = lax.psum(partial_out, "tensor")
    output = (inputs + summed).astype(jnp.bfloat16)
    grad_context = contract_cols(cotangent, out_weight).astype(jnp.bfloat16)
    grad_out_w = contract_rows(context, cotangent)
    grad_down_w = contract_rows(mixed, cotangent)
    grad_out_part, grad_down_part = (
        lax.psum_scatter(grad_out_w, "dp", scatter_dimension=1, tiled=True),
        lax.psum_scatter(grad_down_w, "dp", scatter_dimension=1, tiled=True),
    )
    grad_mixed = contract_cols(cotangent, down_weight)
    grad_up = (grad_mixed * activated).astype(jnp.bfloat16)
    grad_gate = (
        grad_mixed * up_pre * sigmoid_gate * (1.0 + gate_pre * (1.0 - sigmoid_gate))
    ).astype(jnp.bfloat16)
    grad_gate_w = contract_rows(hidden_in, grad_gate)
    grad_up_w = contract_rows(hidden_in, grad_up)
    grad_hidden = contract_cols(grad_gate, gate_weight) + contract_cols(grad_up, up_weight)
    grad_queries, grad_keys, grad_values = lax.map(
        attend_backward,
        (
            seq_queries,
            seq_keys,
            seq_values,
            segment_ids,
            log_total,
            grad_context.reshape(seq_shape),
        ),
    )
    flat_shape = (row_count, head_count, DH)
    grad_queries = rotate_back(grad_queries.reshape(flat_shape) * score_scale, cosine, sine_table)
    grad_keys = rotate_back(grad_keys.reshape(flat_shape), cosine, sine_table)
    grad_joined = (
        jnp.stack([grad_queries, grad_keys, grad_values.reshape(flat_shape)], axis=2)
        .reshape(row_count, head_count * 3 * DH)
        .astype(jnp.bfloat16)
    )
    bias_local = jnp.sum(grad_joined.astype(jnp.float32), 0)
    grad_qkv_w = contract_rows(hidden_in, grad_joined)
    grad_hidden = grad_hidden + contract_cols(grad_joined, qkv_weight)
    grad_qkv_part, grad_gate_part, grad_up_part = (
        lax.psum_scatter(grad_qkv_w, "dp", scatter_dimension=0, tiled=True),
        lax.psum_scatter(grad_gate_w, "dp", scatter_dimension=0, tiled=True),
        lax.psum_scatter(grad_up_w, "dp", scatter_dimension=0, tiled=True),
    )
    grad_total = lax.psum(grad_hidden, "tensor")
    grad_input = (
        cotangent.astype(jnp.float32) + norm_back(grad_total, normed, inverse_std, gain_full)
    ).astype(jnp.bfloat16)
    grad_gain, grad_shift, grad_bias = lax.psum(
        (jnp.sum(grad_total * normed, 0), jnp.sum(grad_total, 0), bias_local), "dp"
    )
    return (
        output,
        grad_input,
        grad_gain,
        grad_shift,
        grad_qkv_part,
        grad_bias,
        grad_out_part,
        grad_gate_part,
        grad_up_part,
        grad_down_part,
    )


BF = jnp.bfloat16
F32 = jnp.float32
MESH = pl.DeviceIdType.MESH
W = 256
PR = 32
SMALL_AT = 2
LATE = 8
WAIT2 = 2


def comm_kernel(
    dims,
    hid_h, cot_h, tok_h, ctx_h, gj_h, z_h, gu_h, gain_ref, bias_ref, qkv_h, gate_h, up_h, down_h,
    out_o, gin_o, sg_o, ss_o, sb_o, gq_o, go_o, gg_o, gu_o, gd_o,
    hid_t, cot, cot_s, tok, ctx, gj, w_a, w_b, w_d, acc, gu, s1, own, recv1, recv2, recv3,
    zs, ze, zm, svb, svr, svq,
    ld_sem, w_sem, s1_send, s1_recv, s2_send, s2_recv, s3_send, s3_recv,
    e_send, e_recv, m_send, m_recv, o_send, o_recv, o_loc, g_sem, v_send, v_recv,
):
    rows, width, full, tail, n_out, n_qkv, n_batch = dims
    n_piece = rows // PR
    hid = zs.at[1]
    t0 = full * W
    b_pairs = n_out + n_qkv
    b_left = b_pairs + 2 * full
    b_up = b_left + 1
    dp = lax.axis_index("dp")
    zi = lax.axis_index("tensor")
    c = lax.rem(dp, 2)
    x = lax.rem(dp // 2, 2)
    y = dp // 4
    core_dev = {"dp": dp + 1 - 2 * c}
    x_dev = {"dp": dp + 2 - 4 * x}
    y_dev = {"dp": dp + 4 - 8 * y}
    is_mid = (zi == 1) | (zi == 2)
    is_end = (zi == 0) | (zi == 3)
    end_of = jnp.where(zi == 1, 0, 3)
    mid_of_end = jnp.where(zi == 0, 1, 2)
    end_dev = {"tensor": end_of}
    mid_dev = {"tensor": mid_of_end}
    other_mid = {"tensor": 3 - zi}

    def load(src, dst, k):
        return pltpu.make_async_copy(src, dst, ld_sem.at[k])

    def w_down(i):
        return pltpu.make_async_copy(down_h.at[pl.ds(i * W, W), :], w_d, w_sem.at[2])

    def w_gate(i):
        return pltpu.make_async_copy(gate_h.at[:, pl.ds(i * W, W)], w_a, w_sem.at[0])

    def w_up(i):
        return pltpu.make_async_copy(up_h.at[:, pl.ds(i * W, W)], w_b, w_sem.at[1])

    def w_qkv(j, side):
        return pltpu.make_async_copy(qkv_h.at[:, pl.ds(j * W, W)], (w_a, w_b)[side], w_sem.at[side])

    w_gate_t = pltpu.make_async_copy(gate_h.at[:, pl.ds(t0, tail)], w_a.at[:, 0:tail], w_sem.at[0])
    w_up_t = pltpu.make_async_copy(up_h.at[:, pl.ds(t0, tail)], w_a.at[:, tail : 2 * tail], w_sem.at[1])
    w_down_t = pltpu.make_async_copy(down_h.at[pl.ds(t0, tail), :], w_d.at[0:tail, :], w_sem.at[2])

    ctx_ld = load(ctx_h, ctx, 0)
    hid_ld = load(hid_h, hid, 1)
    cot_ld = load(cot_h, cot, 2)
    gj_ld = load(gj_h, gj, 3)
    tok_ld = load(tok_h, tok, 4)
    cs_ld = [
        load(cot_h.at[:, (2 * q + s) * W : (2 * q + s + 1) * W], cot_s.at[s, :, q * W : (q + 1) * W], 5 + 2 * q + s)
        for q in range(4)
        for s in range(2)
    ]
    z_ld = load(z_h, zs.at[0], 13)
    gu_ld = load(gu_h, gu, 14)
    z_ld.start()
    ctx_ld.start()
    for cp in cs_ld:
        cp.start()
    hid_ld.start()
    w_qkv(0, 0).start()
    gj_ld.start()
    w_qkv(1, 1).start()
    w_down(0).start()
    tok_ld.start()
    cot_ld.start()
    gu_ld.start()
    acc[...] = jnp.zeros_like(acc)

    barrier = pltpu.get_barrier_semaphore()
    for dev in (core_dev, x_dev, y_dev, {"dp": dp + 2 - 4 * x + 4 - 8 * y}):
        pl.semaphore_signal(barrier, inc=1, device_id=dev, device_id_type=MESH)

    @pl.when(is_mid)
    def _():
        pl.semaphore_signal(barrier, inc=1, device_id=end_dev, device_id_type=MESH)
        pl.semaphore_signal(barrier, inc=1, device_id=other_mid, device_id_type=MESH)

    @pl.when(is_end)
    def _():
        pl.semaphore_signal(barrier, inc=1, device_id=mid_dev, device_id_type=MESH)

    pl.semaphore_wait(barrier, jnp.where(is_mid, 6, 5))

    def rdma(src, dst, send, recv, dev):
        return pltpu.make_async_remote_copy(
            src_ref=src, dst_ref=dst, send_sem=send, recv_sem=recv, device_id=dev, device_id_type=MESH
        )

    def c1(b):
        slot = lax.rem(b, 4)
        return rdma(s1.at[slot], recv1.at[b], s1_send.at[slot], s1_recv.at[b], core_dev)

    def c2(b, h):
        if h == 0:
            return rdma(recv1.at[b, :, 1 - x, 0], recv2.at[b, 0], s2_send.at[b, 0], s2_recv.at[b, 0], x_dev)
        return rdma(recv1.at[b, 1 - y, :, 1], recv2.at[b, 1], s2_send.at[b, 1], s2_recv.at[b, 1], y_dev)

    def c3(b, h):
        if h == 0:
            return rdma(recv2.at[b, 0, 1 - y], recv3.at[b, 0], s3_send.at[b, 0], s3_recv.at[b, 0], y_dev)
        return rdma(recv2.at[b, 1, 1 - x], recv3.at[b, 1], s3_send.at[b, 1], s3_recv.at[b, 1], x_dev)

    def up32(v):
        return v.astype(F32)

    def ev1(b):
        slot = lax.rem(b, 4)
        c1(b).wait_recv()
        for yy in range(2):
            for xx in range(2):
                for h in range(2):
                    recv1[b, yy, xx, h] += own[slot, yy, xx, h]
        c2(b, 0).start()
        c2(b, 1).start()

    def ev2(b):
        c2(b, 0).wait_recv()
        c2(b, 1).wait_recv()
        for k in range(2):
            recv2[b, 0, k] += recv1[b, k, x, 0]
            recv2[b, 1, k] += recv1[b, y, k, 1]
        c3(b, 0).start()
        c3(b, 1).start()

    def cut(b, h, ref, row, col, n=W // 2, lo=0, wide=W):
        if not isinstance(row, int):
            row = pl.multiple_of(row, 64)
        if not isinstance(col, int):
            col = pl.multiple_of(col, W // 2)
        return pltpu.make_async_copy(
            recv3.at[b, h, 0:n, lo : lo + wide], ref.at[pl.ds(row + h * n, n), pl.ds(col, wide)], g_sem.at[b, h]
        )

    groups = (
        (0, n_out, 1, lambda b, h, i: (cut(b, h, go_o, i * W, 0),)),
        (n_out, n_qkv, 1, lambda b, h, i: (cut(b, h, gq_o, 0, i * W),)),
        (b_left, 1, 1, lambda b, h, i: (cut(b, h, gd_o, t0, 0, tail // 2),)),
        (b_pairs, full, 2, lambda b, h, i: (cut(b, h, gd_o, i * W, 0),)),
        (b_pairs + 1, full, 2, lambda b, h, i: (cut(b, h, gg_o, 0, i * W),)),
        (b_up, full, 1, lambda b, h, i: (cut(b, h, gu_o, 0, i * W),)),
        (
            b_up + full, 1, 1,
            lambda b, h, i: (
                cut(b, h, gg_o, 0, t0, wide=tail), cut(b, h, gu_o, 0, t0, lo=tail, wide=tail)
            ),
        ),
    )

    def ev3(b):
        c3(b, 0).wait_recv()
        c3(b, 1).wait_recv()
        recv3[b, 0] += recv2[b, 0, y]
        recv3[b, 1] += recv2[b, 1, x]
        for first, count, step, make in groups:
            here = (b >= first) & (b < first + count * step)
            if step > 1:
                here = here & (lax.rem(b - first, step) == 0)

            @pl.when(here)
            def _(first=first, step=step, make=make):
                for h in range(2):
                    for cp in make(b, h, (b - first) // step):
                        cp.start()

    def before_put(b):
        @pl.when(b >= 4)
        def _():
            c1(b - 4).wait_send()

    def after_put(b):
        c1(b).start()

    def put_rows(b, grad):
        slot = lax.rem(b, 4)
        before_put(b)
        for part, dst in ((1 - c, s1), (c, own)):
            left = hid_t[:, part].reshape(4 * W, rows)
            res = jnp.dot(left, grad, preferred_element_type=F32).astype(BF)
            dst[slot] = res.reshape(2, 2, 2, W // 2, W)
        after_put(b)

    def put_cols(b, left_t):
        slot = lax.rem(b, 4)
        h = left_t.shape[0]
        before_put(b)
        for part, dst in ((1 - c, s1), (c, own)):
            res = jnp.dot(left_t, cot_s[part], preferred_element_type=F32).astype(BF)
            for q in range(4):
                piece = res[:, q * W : (q + 1) * W].reshape(2, h // 2, W)
                dst[slot, q // 2, q % 2, :, 0 : h // 2, :] = piece
                if h < W:
                    dst[slot, q // 2, q % 2, :, h // 2 :, :] = jnp.zeros((2, (W - h) // 2, W), BF)
        after_put(b)

    NB = 512

    def acc_rows(grad, w_ref):
        for n in range(width // NB):
            cols = slice(n * NB, (n + 1) * NB)
            acc[:, cols] += lax.dot_general(
                grad, w_ref[cols, :], (((1,), (1,)), ((), ())), preferred_element_type=F32
            )

    def z_rows(p):
        return pl.ds(pl.multiple_of(p * PR, PR), PR)

    def ce(a, p):
        i = a * n_piece + p
        return rdma(zs.at[a, z_rows(p)], ze.at[a, z_rows(p)], e_send.at[i], e_recv.at[i], mid_dev)

    def cm(a, p):
        i = a * n_piece + p
        return rdma(zs.at[a, z_rows(p)], zm.at[a, z_rows(p)], m_send.at[i], m_recv.at[i], other_mid)

    def co(a, p, ref):
        i = a * n_piece + p
        return rdma(ze.at[a, z_rows(p)], ref.at[z_rows(p)], o_send.at[i], o_recv.at[i], end_dev)

    def cl(a, p, ref):
        i = a * n_piece + p
        return pltpu.make_async_copy(ze.at[a, z_rows(p)], ref.at[z_rows(p)], o_loc.at[i])

    def ev_e(e):
        a, p = e // n_piece, lax.rem(e, n_piece)

        @pl.when(is_mid)
        def _():
            ce(a, p).wait_recv()
            r = z_rows(p)
            zs[a, r, :] += ze[a, r, :]
            cm(a, p).start()

    def norm_rows(r):
        v = up32(tok[r, :])
        mu = jnp.mean(v, -1, keepdims=True)
        v = v - mu
        inv = lax.rsqrt(jnp.mean(v * v, -1, keepdims=True) + EPSILON)
        return v * inv, inv

    def ev_m(e):
        a, p = e // n_piece, lax.rem(e, n_piece)

        @pl.when(is_mid)
        def _():
            cm(a, p).wait_recv()
            r = z_rows(p)

            @pl.when(a == 0)
            def _():
                total = up32(zs[0, r, :]) + up32(zm[0, r, :])
                ze[0, r, :] = (up32(tok[r, :]) + total).astype(BF)
                co(0, p, out_o).start()
                cl(0, p, out_o).start()

            @pl.when(a == 1)
            def _():
                total = up32(zs[1, r, :]) + up32(zm[1, r, :])
                normed, inv = norm_rows(r)
                back = norm_back(total, normed, inv, gain_ref[...])
                ze[1, r, :] = (up32(cot[r, :]) + back).astype(BF)
                co(1, p, gin_o).start()
                cl(1, p, gin_o).start()

    def act_of(g, u):
        return (g * jax.nn.sigmoid(g) * u).astype(BF)

    def joined_grad(j):
        return jnp.concatenate([gj[2 * j], gj[2 * j + 1]], axis=1)

    def cv(k, dev):
        return rdma(svb.at[k], svr.at[k], v_send.at[k], v_recv.at[k], dev)

    def cw(k, dev):
        return rdma(svb.at[4], svq.at[y, x], v_send.at[4 + k], v_recv.at[4 + k], dev)

    square = (x_dev, y_dev, {"dp": dp + 2 - 4 * x + 4 - 8 * y})

    def small_1():
        @pl.when(is_mid)
        def _():
            cv(0, end_dev).wait_recv()
            svb[1] = svb[0] + svr[0]
            cv(1, other_mid).start()

    def small_2():
        @pl.when(is_mid)
        def _():
            cv(1, other_mid).wait_recv()
            svb[2] = svb[1] + svr[1]
            svb[3, 0:2, :] = svb[2, 0:2, :]
            cv(2, end_dev).start()

    def small_3():
        @pl.when(is_end)
        def _():
            cv(2, mid_dev).wait_recv()
            svb[3, 0:2, :] = svr[2, 0:2, :]

        svb[3, 2:8, :] = svb[0, 2:8, :]
        cv(3, core_dev).start()

    def small_4():
        cv(3, core_dev).wait_recv()
        svb[4] = svb[3] + svr[3]
        svq[y, x] = svb[4]
        for k, dev in enumerate(square):
            cw(k, dev).start()

    def small_5():
        for k, dev in enumerate(square):
            cw(k, dev).wait_recv()
        total = (svq[0, 0] + svq[0, 1]) + (svq[1, 0] + svq[1, 1])
        for row, ref in enumerate((sg_o, ss_o, sb_o)):
            for n in range(ref.shape[0]):
                ref[n : n + 1, :] = total[row : row + 1, n * 128 : (n + 1) * 128]

    def small_sent():
        @pl.when(is_end)
        def _():
            cv(0, mid_dev).wait_send()

        @pl.when(is_mid)
        def _():
            cv(1, other_mid).wait_send()
            cv(2, end_dev).wait_send()

        cv(3, core_dev).wait_send()
        for k, dev in enumerate(square):
            cw(k, dev).wait_send()

    def send_line(a):
        def send(p, keep):
            ce(a, p).start()
            return keep

        @pl.when(is_end)
        def _():
            if a == 1:
                cv(0, mid_dev).start()
            lax.fori_loop(0, n_piece, send, 0)

    def line_rows(p, keep):
        r = z_rows(p)
        v = acc[r, :]
        zs[1, r, :] = v.astype(BF)
        normed, _inv = norm_rows(r)
        svb[0, 0:1, :] += jnp.sum(v * normed, 0, keepdims=True)
        svb[0, 1:2, :] += jnp.sum(v, 0, keepdims=True)
        return keep

    z_ld.wait()
    send_line(0)
    ctx_ld.wait()
    for cp in cs_ld:
        cp.wait()
    for j in range(n_out):
        put_cols(jnp.int32(j), ctx[:, j * W : (j + 1) * W].T)
    hid_ld.wait()
    for q in range(4):
        for s in range(2):
            lo = (2 * q + s) * W
            hid_t[q, s] = hid[:, lo : lo + W].T
    for b in range(n_out):
        ev1(jnp.int32(b))
    gj_ld.wait()
    tok_ld.wait()
    cot_ld.wait()

    def joined(n, keep):
        for side in range(2):
            j = 2 * n + side
            w_qkv(j, side).wait()
            acc_rows(joined_grad(j), (w_a, w_b)[side])

            @pl.when(j + 2 < n_qkv)
            def _(j=j, side=side):
                w_qkv(j + 2, side).start()

            @pl.when(j + 2 >= n_qkv)
            def _(side=side):
                (w_gate, w_up)[side](0).start()

            b = n_out + j
            put_rows(b, joined_grad(j))

            @pl.when(j >= 1)
            def _(b=b):
                ev1(b - 1)

        ev_e(n)

        @pl.when(n >= 1)
        def _():
            ev2(n - 1)

        @pl.when(n >= 2)
        def _():
            ev_m(n - 2)

        return keep

    lax.fori_loop(0, n_qkv // 2, joined, 0)
    gu_ld.wait()

    def gate_grads(gm, g, u):
        sg = jax.nn.sigmoid(g)
        g_up = (gm * (g * sg)).astype(BF)
        g_gate = (gm * u * sg * (1.0 + g * (1.0 - sg))).astype(BF)
        return g_gate, g_up

    def cols_t(left, w_ref, k):
        return lax.dot_general(left, w_ref[0:k, :], (((1,), (1,)), ((), ())), preferred_element_type=F32)

    e0 = n_qkv // 2
    two = n_qkv // 2 - 1

    def bwd(i, keep):
        w_down(i).wait()
        gm = cols_t(cot[...], w_d, W)

        @pl.when(i + 1 < full)
        def _():
            w_down(i + 1).start()

        @pl.when(i + 1 == full)
        def _():
            w_down_t.start()

        g, u = up32(gu[i, 0]), up32(gu[i, 1])
        mixed = act_of(g, u)
        g_gate, g_up = gate_grads(gm, g, u)
        gu[i, 0] = g_gate
        gu[i, 1] = g_up
        w_gate(i).wait()
        acc_rows(g_gate, w_a)
        w_up(i).wait()
        acc_rows(g_up, w_b)

        @pl.when(i + 1 < full)
        def _():
            w_gate(i + 1).start()
            w_up(i + 1).start()

        @pl.when(i + 1 == full)
        def _():
            w_gate_t.start()
            w_up_t.start()

        b = b_pairs + 2 * i
        e = e0 + 2 * i
        put_cols(b, mixed.T)
        ev1(b - 1)
        ev_e(e)
        ev_m(e - 2)
        put_rows(b + 1, gu[i, 0])
        ev1(b)
        ev2(two + i)
        ev_e(e + 1)
        ev_m(e - 1)
        return keep

    lax.fori_loop(0, full, bwd, 0)
    w_down_t.wait()
    gm = cols_t(cot[...], w_d, tail)
    both = up32(gu[full, 0])
    mixed = act_of(both[:, 0:tail], both[:, tail:])
    g_gate, g_up = gate_grads(gm, both[:, 0:tail], both[:, tail:])
    both = jnp.concatenate([g_gate, g_up], axis=1)
    gu[full, 0] = both
    w_gate_t.wait()
    w_up_t.wait()
    acc_rows(both, w_a)
    svb[0] = jnp.zeros_like(svb[0])
    svb[0, 2:3, 0 : n_qkv * W] = bias_ref[...]
    lax.fori_loop(0, n_piece, line_rows, 0)
    send_line(1)

    put_cols(jnp.int32(b_left), mixed.T)
    ev1(jnp.int32(b_left - 1))
    e0 = e0 + 2 * full
    two = two + full
    ev2(jnp.int32(two))
    ev_e(jnp.int32(e0))
    ev_m(jnp.int32(e0 - 2))

    def left_over(i, keep):
        b = b_up + i
        at = jnp.where(i == full, 0, 1)
        put_rows(b, gu[i, at])
        ev1(b - 1)
        ev2(two + 1 + i)
        ev_e(e0 + 1 + i)
        ev_m(e0 - 1 + i)
        return keep

    lax.fori_loop(0, full + 1, left_over, 0)
    ev1(jnp.int32(n_batch - 1))
    e0 = e0 + full + 2
    two_left = two + full + 2

    n_e = 2 * n_piece
    smalls = (small_1, small_2, small_3, small_4)

    def drain(k, keep):
        @pl.when(k + e0 < n_e)
        def _():
            ev_e(k + e0)

        @pl.when(k + e0 - 2 < n_e)
        def _():
            ev_m(k + e0 - 2)

        @pl.when((k >= WAIT2) & (k - WAIT2 + two_left < n_batch))
        def _():
            ev2(k - WAIT2 + two_left)

        for i, small in enumerate(smalls):
            pl.when(k == SMALL_AT + i)(small)

        for h in range(2):
            b = 2 * (k - LATE) + h

            @pl.when((b >= 0) & (b < n_batch))
            def _():
                ev3(b)

        return keep

    steps = max(LATE + (n_batch + 1) // 2, n_e - e0 + 2, WAIT2 + n_batch - two_left)
    lax.fori_loop(0, steps, drain, 0)
    small_5()

    small_sent()

    def finish(b, keep):
        for h in range(2):
            c2(b, h).wait_send()
            c3(b, h).wait_send()
        return keep

    lax.fori_loop(0, n_batch, finish, 0)
    for k in range(4):
        c1(jnp.int32(n_batch - 4 + k)).wait_send()
    for first, count, step, make in groups:
        for i in range(count):
            for h in range(2):
                for cp in make(first + i * step, h, i):
                    cp.wait()

    def finish_line(p, keep):
        for a, ref in ((0, out_o), (1, gin_o)):
            @pl.when(is_mid)
            def _():
                cm(a, p).wait_send()
                co(a, p, ref).wait_send()
                cl(a, p, ref).wait()

            @pl.when(is_end)
            def _():
                ce(a, p).wait_send()
                co(a, p, ref).wait_recv()

        return keep

    lax.fori_loop(0, n_piece, finish_line, 0)


def comm_call(hidden, cot, tokens, ctx, gj, partial, gu, gain, bias_sum, qkv_w, gate_w, up_w, down_w):
    rows, width = hidden.shape
    hd = ctx.shape[1]
    ff = gate_w.shape[1]
    full, tail = ff // W, ff % W
    n_out, n_qkv = hd // W, qkv_w.shape[1] // W
    n_batch = n_out + full + 1 + n_qkv + 2 * full + 1
    n_z = 2 * (rows // PR)
    dims = (rows, width, full, tail, n_out, n_qkv, n_batch)
    piece = (W // 2, W)
    vm, dma = pltpu.VMEM, pltpu.SemaphoreType.DMA
    any_spec = pl.BlockSpec(memory_space=pl.ANY)
    vm_spec = pl.BlockSpec(memory_space=pltpu.VMEM)
    return pl.pallas_call(
        functools.partial(comm_kernel, dims),
        out_shape=(
            jax.ShapeDtypeStruct((rows, width), BF),
            jax.ShapeDtypeStruct((rows, width), BF),
            jax.ShapeDtypeStruct((width // 128, 128), F32),
            jax.ShapeDtypeStruct((width // 128, 128), F32),
            jax.ShapeDtypeStruct((n_qkv * W // 128, 128), F32),
            jax.ShapeDtypeStruct((W, n_qkv * W), BF),
            jax.ShapeDtypeStruct((hd, W), BF),
            jax.ShapeDtypeStruct((W, ff), BF),
            jax.ShapeDtypeStruct((W, ff), BF),
            jax.ShapeDtypeStruct((ff, W), BF),
        ),
        in_specs=[any_spec] * 7 + [vm_spec] * 2 + [any_spec] * 4,
        out_specs=(any_spec,) * 2 + (vm_spec,) * 3 + (any_spec,) * 5,
        scratch_shapes=[
            vm((4, 2, W, rows), BF),
            vm((rows, width), BF),
            vm((2, rows, width // 2), BF),
            vm((rows, width), BF),
            vm((rows, hd), BF),
            vm((2 * n_qkv, rows, W // 2), BF),
            vm((width, W), BF),
            vm((width, W), BF),
            vm((W, width), BF),
            vm((rows, width), F32),
            vm((full + 1, 2, rows, W), BF),
            vm((4, 2, 2, 2) + piece, BF),
            vm((4, 2, 2, 2) + piece, BF),
            vm((n_batch, 2, 2, 2) + piece, BF),
            vm((n_batch, 2, 2) + piece, BF),
            vm((n_batch, 2) + piece, BF),
            vm((2, rows, width), BF),
            vm((2, rows, width), BF),
            vm((2, rows, width), BF),
            vm((5, 8, width), F32),
            vm((4, 8, width), F32),
            vm((2, 2, 8, width), F32),
            dma((15,)),
            dma((3,)),
            dma((4,)),
            dma((n_batch,)),
            dma((n_batch, 2)),
            dma((n_batch, 2)),
            dma((n_batch, 2)),
            dma((n_batch, 2)),
            dma((n_z,)),
            dma((n_z,)),
            dma((n_z,)),
            dma((n_z,)),
            dma((n_z,)),
            dma((n_z,)),
            dma((n_z,)),
            dma((n_batch, 2)),
            dma((7,)),
            dma((7,)),
        ],
        compiler_params=pltpu.CompilerParams(
            collective_id=0, has_side_effects=True, vmem_limit_bytes=67043328
        ),
        name="ffn_and_sums",
    )(hidden, cot, tokens, ctx, gj, partial, gu, gain, bias_sum, qkv_w, gate_w, up_w, down_w)


def forward_kernel(full, tail, hid, ctx, out_w, gate_w, up_w, down_w, z_o, gu_o, acc):
    i = pl.program_id(0)
    width = acc.shape[1]
    blocks = [slice(n, n + 512) for n in range(0, width, 512)]

    def dot(a, b):
        return jnp.dot(a, b, preferred_element_type=F32)

    def act_of(g, u):
        return (g * jax.nn.sigmoid(g) * u).astype(BF)

    @pl.when(i == 0)
    def _():
        for cols in blocks:
            acc[:, cols] = dot(ctx[...], out_w[:, cols])

    @pl.when(i < full)
    def _():
        g = dot(hid[...], gate_w[...])
        u = dot(hid[...], up_w[...])
        gu_o[0, 0] = g.astype(BF)
        gu_o[0, 1] = u.astype(BF)
        mixed = act_of(g, u)
        for cols in blocks:
            acc[:, cols] += dot(mixed, down_w[:, cols])

    @pl.when(i == full)
    def _():
        both = dot(hid[...], jnp.concatenate([gate_w[:, 0:tail], up_w[:, 0:tail]], axis=1))
        gu_o[0, 0] = both.astype(BF)
        gu_o[0, 1] = jnp.zeros_like(both).astype(BF)
        mixed = act_of(both[:, 0:tail], both[:, tail:])
        for cols in blocks:
            z_o[:, cols] = (acc[:, cols] + dot(mixed, down_w[0:tail, cols])).astype(BF)


def forward_call(hidden, ctx, out_w, gate_w, up_w, down_w):
    rows, width = hidden.shape
    hd = ctx.shape[1]
    ff = gate_w.shape[1]
    full, tail = ff // W, ff % W
    once = lambda shape: pl.BlockSpec(shape, lambda i: (0,) * len(shape), pipeline_mode=pl.Buffered(1))
    return pl.pallas_call(
        functools.partial(forward_kernel, full, tail),
        grid=(full + 1,),
        out_shape=(
            jax.ShapeDtypeStruct((rows, width), BF),
            jax.ShapeDtypeStruct((full + 1, 2, rows, W), BF),
        ),
        in_specs=[
            once((rows, width)),
            once((rows, hd)),
            once((hd, width)),
            pl.BlockSpec((width, W), lambda i: (0, i)),
            pl.BlockSpec((width, W), lambda i: (0, i)),
            pl.BlockSpec((W, width), lambda i: (i, 0)),
        ],
        out_specs=(
            once((rows, width)),
            pl.BlockSpec((1, 2, rows, W), lambda i: (i, 0, 0, 0)),
        ),
        scratch_shapes=[pltpu.VMEM((rows, width), F32)],
        compiler_params=pltpu.CompilerParams(vmem_limit_bytes=60 << 20),
        name="forward",
    )(hidden, ctx, out_w, gate_w, up_w, down_w)


PARTS = 4


def finish_kernel(*refs):
    n = len(refs) // 2
    for src, dst in zip(refs[:n], refs[n:]):
        dst[...] = src[...].astype(dst.dtype)


def finish_call(values, types):
    def spec(v):
        if v.shape[0] < 16 * PARTS:
            return pl.BlockSpec(v.shape, lambda i: (0, 0))
        return pl.BlockSpec((v.shape[0] // PARTS, v.shape[1]), lambda i: (i, 0))

    return pl.pallas_call(
        finish_kernel,
        grid=(PARTS,),
        out_shape=tuple(jax.ShapeDtypeStruct(v.shape, t) for v, t in zip(values, types)),
        in_specs=[spec(v) for v in values],
        out_specs=tuple(spec(v) for v in values),
        compiler_params=pltpu.CompilerParams(vmem_limit_bytes=60 << 20),
        name="finish",
    )(*values)


QB = 128
ROWS = 32


def attn_kernel(
    heads_scale, tok, seg_ref, gain_ref, shift_ref, b_ref, w_ref, ow_ref, cot,
    hid, ctx_o, gj_o, bias_o, gain_o,
    bias_m, tab, s_m, g_m, p_m, gs_m, shift_m, b_m,
):
    rows = tok.shape[0]
    nq = rows // QB
    half = ROT // 2

    step = pl.program_id(0)

    @pl.when(step == 0)
    def _():
        for n in range(gain_ref.shape[0]):
            cols = slice(n * QB, (n + 1) * QB)
            gain_o[0:1, cols] = gain_ref[n : n + 1, :].astype(F32)
            shift_m[0:1, cols] = shift_ref[n : n + 1, :].astype(F32)
        b_m[...] = b_ref[...].astype(F32)

        def norm_step(n, keep):
            r = pl.ds(pl.multiple_of(n * 64, 64), 64)
            v = tok[r, :].astype(F32)
            v = v - jnp.mean(v, -1, keepdims=True)
            v = v * lax.rsqrt(jnp.mean(v * v, -1, keepdims=True) + EPSILON)
            hid[r, :] = (v * gain_o[...] + shift_m[...]).astype(BF)
            return keep

        lax.fori_loop(0, rows // 64, norm_step, 0)
        seg = seg_ref[...].astype(F32)
        seg_t = jnp.broadcast_to(seg, (8, rows)).T
        lane = lax.broadcasted_iota(jnp.int32, (QB, QB), 1)
        head_lane = lane % DH
        freq = jnp.ones((1, QB), F32)
        for n in range(1, half):
            freq = jnp.where(head_lane[0:1] % half == n, 10000.0 ** (-2.0 * n / ROT), freq)
        for i in range(nq):
            lo = max(0, i - 2) * QB
            n = (i + 1) * QB - lo
            q_at = lax.broadcasted_iota(jnp.int32, (QB, n), 0) + i * QB
            k_at = lax.broadcasted_iota(jnp.int32, (QB, n), 1) + lo
            same = seg_t[i * QB : (i + 1) * QB, 0:1] == seg[:, lo : lo + n]
            allowed = same & (q_at >= k_at)
            bias_m[i, :, 0:n] = jnp.where(allowed, 0.0, NEGATIVE)
            place = jnp.sum(jnp.where(allowed, 1.0, 0.0), -1, keepdims=True) - 1.0
            angle = place * freq
            cosine, sine = jnp.cos(angle), jnp.sin(angle)
            for blk in range(3):
                live = head_lane < ROT
                if blk == 1:
                    live = live & (lane >= DH)
                if blk == 2:
                    live = live & (lane < DH)
                scale = jnp.ones((QB, QB), F32)
                if blk == 0:
                    scale = jnp.where(lane < DH, heads_scale, 1.0)
                if blk == 1:
                    scale = jnp.where(lane >= DH, heads_scale, 1.0)
                r = slice(i * QB, (i + 1) * QB)
                tab[blk, 0, r] = jnp.where(live, cosine, 1.0) * scale
                tab[blk, 1, r] = jnp.where(live & (head_lane < half), -sine, 0.0) * scale
                tab[blk, 2, r] = jnp.where(live & (head_lane >= half), sine, 0.0) * scale

    def dot_t(a, b):
        return lax.dot_general(a, b, (((1,), (1,)), ((), ())), preferred_element_type=F32)

    def dot(a, b):
        return jnp.dot(a, b, preferred_element_type=F32)

    joined = dot(hid[...], w_ref[...])
    turned = []
    for blk in range(3):
        v = joined[:, blk * QB : (blk + 1) * QB] + b_m[pl.ds(3 * step + blk, 1), :]
        v = v * tab[blk, 0] + pltpu.roll(v, QB - half, 1) * tab[blk, 1] + pltpu.roll(v, half, 1) * tab[blk, 2]
        turned.append(v.astype(BF))
    gctx = dot_t(cot[...], ow_ref[...]).astype(BF)
    lo_h, hi_h = slice(0, DH), slice(DH, 2 * DH)
    heads = (
        (turned[0][:, lo_h], turned[0][:, hi_h], turned[1][:, lo_h], gctx[:, lo_h]),
        (turned[1][:, hi_h], turned[2][:, lo_h], turned[2][:, hi_h], gctx[:, hi_h]),
    )
    spans = [(max(0, i - 2) * QB, (i + 1) * QB) for i in range(nq)]
    blocks = [(n, i) for i in range(nq) for n in range(2)]
    for n, i in blocks:
        q, k, v, gc = heads[n]
        lo, hi = spans[i]
        s_m[n, i, :, 0 : hi - lo] = dot_t(q[i * QB : hi], k[lo:hi])
        g_m[n, i, :, 0 : hi - lo] = dot_t(gc[i * QB : hi], v[lo:hi])
    for n, i in blocks:
        lo, hi = spans[i]
        for r in range(0, QB, ROWS):
            rr = slice(r, r + ROWS)
            s = s_m[n, i, rr, 0 : hi - lo] + bias_m[i, rr, 0 : hi - lo]
            e = jnp.exp(s - jnp.max(s, -1, keepdims=True))
            p = e * (1.0 / jnp.sum(e, -1, keepdims=True))
            gp = g_m[n, i, rr, 0 : hi - lo]
            p_m[n, i, rr, 0 : hi - lo] = p.astype(BF)
            gs_m[n, i, rr, 0 : hi - lo] = (p * (gp - jnp.sum(p * gp, -1, keepdims=True))).astype(BF)
    grads, contexts = [], []
    for n, (q, k, v, gc) in enumerate(heads):
        out, grad_q, grad_k, grad_v = [], [], [], []
        for i, (lo, hi) in enumerate(spans):
            out.append(dot(p_m[n, i, :, 0 : hi - lo], v[lo:hi]))
            grad_q.append(dot(gs_m[n, i, :, 0 : hi - lo], k[lo:hi]))
        for j in range(nq):
            top = min(j + 3, nq)

            def stack(part):
                cut = []
                for i in range(j, top):
                    at = j * QB - spans[i][0]
                    cut.append(part[n, i, :, at : at + QB].T)
                return jnp.concatenate(cut, 1)

            grad_k.append(dot(stack(gs_m), q[j * QB : top * QB]))
            grad_v.append(dot(stack(p_m), gc[j * QB : top * QB]))
        contexts.append(jnp.concatenate(out, 0))
        grads.append([jnp.concatenate(part, 0) for part in (grad_q, grad_k, grad_v)])
    ctx_o[...] = jnp.concatenate(contexts, 1).astype(BF)
    (q0, k0, v0), (q1, k1, v1) = grads
    for blk, pair in enumerate(((q0, k0), (v0, q1), (k1, v1))):
        g = jnp.concatenate(pair, 1)
        g = g * tab[blk, 0] - pltpu.roll(g, QB - half, 1) * tab[blk, 1] - pltpu.roll(g, half, 1) * tab[blk, 2]
        g = g.astype(BF)
        gj_o[blk] = g
        bias_o[:, blk * QB : (blk + 1) * QB] = jnp.sum(g.astype(F32), 0, keepdims=True)


def attn_call(tokens, segment_ids, gain, shift, qkv_w, qkv_b, out_w, cot):
    rows, width = tokens.shape
    hd = out_w.shape[0]
    steps = hd // (2 * DH)
    three = 3 * QB
    whole = lambda shape: pl.BlockSpec(shape, lambda i: (0,) * len(shape))
    once = lambda shape: pl.BlockSpec(shape, lambda i: (0,) * len(shape), pipeline_mode=pl.Buffered(1))
    return pl.pallas_call(
        functools.partial(attn_kernel, DH ** (-0.5)),
        grid=(steps,),
        out_shape=(
            jax.ShapeDtypeStruct((rows, width), BF),
            jax.ShapeDtypeStruct((rows, hd), BF),
            jax.ShapeDtypeStruct((3 * steps, rows, QB), BF),
            jax.ShapeDtypeStruct((1, 3 * hd), F32),
            jax.ShapeDtypeStruct((1, width), F32),
        ),
        in_specs=[
            once((rows, width)),
            whole((1, rows)),
            whole((width // QB, QB)),
            whole((width // QB, QB)),
            whole((3 * hd // QB, QB)),
            pl.BlockSpec((width, three), lambda i: (0, i)),
            pl.BlockSpec((QB, width), lambda i: (i, 0)),
            once((rows, width)),
        ],
        out_specs=(
            whole((rows, width)),
            pl.BlockSpec((rows, QB), lambda i: (0, i)),
            pl.BlockSpec((3, rows, QB), lambda i: (i, 0, 0)),
            pl.BlockSpec((1, three), lambda i: (0, i)),
            whole((1, width)),
        ),
        scratch_shapes=[
            pltpu.VMEM((rows // QB, QB, three), F32),
            pltpu.VMEM((3, 3, rows, QB), F32),
            pltpu.VMEM((2, rows // QB, QB, three), F32),
            pltpu.VMEM((2, rows // QB, QB, three), F32),
            pltpu.VMEM((2, rows // QB, QB, three), BF),
            pltpu.VMEM((2, rows // QB, QB, three), BF),
            pltpu.VMEM((1, width), F32),
            pltpu.VMEM((3 * hd // QB, QB), F32),
        ],
        compiler_params=pltpu.CompilerParams(vmem_limit_bytes=60 << 20),
        name="attention",
    )(
        tokens, segment_ids, gain.reshape(-1, QB), shift.reshape(-1, QB), qkv_b.reshape(-1, QB), qkv_w, out_w, cot
    )


def fast(
    n_dp,
    n_tensor,
    tokens,
    segment_ids,
    norm_gain,
    norm_bias,
    qkv_weight,
    qkv_bias,
    out_weight,
    gate_weight,
    up_weight,
    down_weight,
    cotangent,
):
    args = (tokens, segment_ids, norm_gain, norm_bias, qkv_weight, qkv_bias, out_weight, gate_weight, up_weight, down_weight, cotangent)
    row_count, width = tokens.shape
    ff = gate_weight.shape[1]
    fits = (
        (n_dp, n_tensor) == (8, 4)
        and segment_ids.shape == (1, row_count)
        and (row_count, width) == (512, 8 * W)
        and ff % W == W // 2
        and qkv_weight.shape[1] % (2 * W) == 0
        and out_weight.shape[0] % W == 0
        and qkv_weight.shape[1] == 3 * out_weight.shape[0]
        and 2 * DH == QB
    )
    if not fits:
        return local(*args)
    hidden_in, context, grad_joined, bias_local, gain_row = attn_call(
        tokens, segment_ids, norm_gain, norm_bias, qkv_weight, qkv_bias, out_weight, cotangent
    )
    partial, gate_up = forward_call(hidden_in, context, out_weight, gate_weight, up_weight, down_weight)
    results = comm_call(
        hidden_in, cotangent, tokens, context, grad_joined, partial, gate_up, gain_row, bias_local,
        qkv_weight, gate_weight, up_weight, down_weight,
    )
    output, grad_input, gain_sum, shift_sum, bias_sum, joined_w, out_w, gate_w, up_w, down_w = finish_call(
        results, (BF,) * 2 + (F32,) * 8
    )
    return (
        output,
        grad_input,
        gain_sum.reshape(width),
        shift_sum.reshape(width),
        joined_w,
        bias_sum.reshape(qkv_weight.shape[1]),
        out_w,
        gate_w,
        up_w,
        down_w,
    )


def solution(mesh):
    body = functools.partial(fast, mesh.shape["dp"], mesh.shape["tensor"])
    return jax.shard_map(
        body,
        mesh=mesh,
        in_specs=(
            P("dp", None),
            P("dp", None),
            P(),
            P(),
            P(None, "tensor"),
            P("tensor"),
            P("tensor", None),
            P(None, "tensor"),
            P(None, "tensor"),
            P("tensor", None),
            P("dp", None),
        ),
        out_specs=(
            P("dp", None),
            P("dp", None),
            P(),
            P(),
            P("dp", "tensor"),
            P("tensor"),
            P("tensor", "dp"),
            P("dp", "tensor"),
            P("dp", "tensor"),
            P("tensor", "dp"),
        ),
        check_vma=False,
    )
```

```python
import functools

import jax
import jax.numpy as jnp
from jax import lax
from jax.experimental import pallas as pl
from jax.experimental.pallas import tpu as pltpu
from jax.sharding import PartitionSpec as P

DH = 64
ROT = 16


EPSILON = 1e-05
NEGATIVE = -1e30


def positions_of(segments):
    column = jnp.arange(segments.shape[1], dtype=jnp.int32)
    starts = jnp.concatenate(
        [jnp.ones((segments.shape[0], 1), dtype=bool), segments[:, 1:] != segments[:, :-1]], axis=1
    )
    doc_start = lax.cummax(jnp.where(starts, column[None, :], 0), axis=1)
    return column[None, :] - doc_start


def rotary_tables(positions):
    half_rot = ROT // 2
    frequency = jnp.power(10000.0, -2.0 * jnp.arange(half_rot, dtype=jnp.float32) / ROT)
    angles = positions.astype(jnp.float32)[:, None] * frequency[None, :]
    return (jnp.cos(angles)[:, None, :], jnp.sin(angles)[:, None, :])


def rotate(tensor, cosine, sine_table):
    half_rot = ROT // 2
    first_half = tensor[..., :half_rot]
    second_half = tensor[..., half_rot:ROT]
    return jnp.concatenate(
        [
            first_half * cosine - second_half * sine_table,
            second_half * cosine + first_half * sine_table,
            tensor[..., ROT:],
        ],
        axis=-1,
    )


def rotate_back(tensor, cosine, sine_table):
    half_rot = ROT // 2
    first_half = tensor[..., :half_rot]
    second_half = tensor[..., half_rot:ROT]
    return jnp.concatenate(
        [
            first_half * cosine + second_half * sine_table,
            second_half * cosine - first_half * sine_table,
            tensor[..., ROT:],
        ],
        axis=-1,
    )


def masked_scores(query_block, seq_keys, seq_segments, begin_row, block_rows):
    key_index = jnp.arange(seq_keys.shape[0], dtype=jnp.int32)
    allowed = (seq_segments[begin_row : begin_row + block_rows, None] == seq_segments[None, :]) & (
        key_index[:, None] >= key_index[None, :]
    )
    scores = jnp.einsum("qhd,khd->hqk", query_block, seq_keys, preferred_element_type=jnp.float32)
    return jnp.where(allowed[None], scores, NEGATIVE)


def attend_forward(packed):
    seq_queries, seq_keys, seq_values, seq_segments = packed
    length = seq_queries.shape[0]
    block_rows = min(512, length)
    scores = masked_scores(seq_queries, seq_keys, seq_segments, 0, block_rows)
    top_score = jnp.max(scores, -1, keepdims=True)
    weights = jnp.exp(scores - top_score)
    denominator = jnp.sum(weights, -1, keepdims=True)
    probability = (weights / denominator).astype(jnp.bfloat16)
    contexts = [
        jnp.einsum("hqk,khd->qhd", probability, seq_values, preferred_element_type=jnp.float32)
    ]
    log_totals = [top_score + jnp.log(denominator)]
    return (jnp.concatenate(contexts, 0), jnp.concatenate(log_totals, 1))


def attend_backward(packed):
    seq_queries, seq_keys, seq_values, seq_segments, seq_log_total, seq_grad_context = packed
    length = seq_queries.shape[0]
    block_rows = min(512, length)
    grad_keys = jnp.zeros(seq_keys.shape, jnp.float32)
    grad_values = jnp.zeros(seq_values.shape, jnp.float32)
    scores = masked_scores(seq_queries, seq_keys, seq_segments, 0, block_rows)
    probability = jnp.exp(scores - seq_log_total[:, 0:block_rows])
    grad_prob = jnp.einsum(
        "qhd,khd->hqk", seq_grad_context, seq_values, preferred_element_type=jnp.float32
    )
    row_dot = jnp.sum(probability * grad_prob, -1, keepdims=True)
    grad_scores = (probability * (grad_prob - row_dot)).astype(jnp.bfloat16)
    grad_queries = [
        jnp.einsum("hqk,khd->qhd", grad_scores, seq_keys, preferred_element_type=jnp.float32)
    ]
    grad_keys = grad_keys + jnp.einsum(
        "hqk,qhd->khd", grad_scores, seq_queries, preferred_element_type=jnp.float32
    )
    grad_values = grad_values + jnp.einsum(
        "hqk,qhd->khd",
        probability.astype(jnp.bfloat16),
        seq_grad_context,
        preferred_element_type=jnp.float32,
    )
    return (jnp.concatenate(grad_queries, 0), grad_keys, grad_values)


def contract_rows(left_side, right_side):
    return lax.dot_general(
        left_side, right_side, (((0,), (0,)), ((), ())), preferred_element_type=jnp.float32
    )


def contract_cols(left_side, right_side):
    return lax.dot_general(
        left_side, right_side, (((1,), (1,)), ((), ())), preferred_element_type=jnp.float32
    )


def norm_back(grad_normed_out, normed, inverse_std, gain_full):
    grad_normed = grad_normed_out * gain_full
    return inverse_std * (
        grad_normed
        - jnp.mean(grad_normed, -1, keepdims=True)
        - normed * jnp.mean(grad_normed * normed, -1, keepdims=True)
    )


def local(
    tokens,
    segment_ids,
    norm_gain,
    norm_bias,
    qkv_weight,
    qkv_bias,
    out_weight,
    gate_weight,
    up_weight,
    down_weight,
    cotangent,
):
    row_count = tokens.shape[0]
    seq_count, length = segment_ids.shape
    head_count = qkv_weight.shape[1] // (3 * DH)
    score_scale = DH ** (-0.5)
    inputs = tokens.astype(jnp.float32)
    row_mean = jnp.mean(inputs, -1, keepdims=True)
    centered = inputs - row_mean
    inverse_std = lax.rsqrt(jnp.mean(centered * centered, -1, keepdims=True) + EPSILON)
    normed = centered * inverse_std
    gain_full = norm_gain.astype(jnp.float32)
    hidden_in = (normed * gain_full + norm_bias.astype(jnp.float32)).astype(jnp.bfloat16)
    joined_qkv = (
        jnp.dot(hidden_in, qkv_weight, preferred_element_type=jnp.float32)
        + qkv_bias.astype(jnp.float32)
    ).reshape(row_count, head_count, 3, DH)
    positions = positions_of(segment_ids).reshape(row_count)
    cosine, sine_table = rotary_tables(positions)
    queries = (rotate(joined_qkv[:, :, 0], cosine, sine_table) * score_scale).astype(jnp.bfloat16)
    key_rows = rotate(joined_qkv[:, :, 1], cosine, sine_table).astype(jnp.bfloat16)
    value_rows = joined_qkv[:, :, 2].astype(jnp.bfloat16)
    seq_shape = (seq_count, length, head_count, DH)
    seq_queries = queries.reshape(seq_shape)
    seq_keys = key_rows.reshape(seq_shape)
    seq_values = value_rows.reshape(seq_shape)
    context, log_total = lax.map(attend_forward, (seq_queries, seq_keys, seq_values, segment_ids))
    context = context.reshape(row_count, head_count * DH).astype(jnp.bfloat16)
    gate_pre = jnp.dot(hidden_in, gate_weight, preferred_element_type=jnp.float32)
    up_pre = jnp.dot(hidden_in, up_weight, preferred_element_type=jnp.float32)
    sigmoid_gate = jax.nn.sigmoid(gate_pre)
    activated = gate_pre * sigmoid_gate
    mixed = (activated * up_pre).astype(jnp.bfloat16)
    partial_out = jnp.dot(context, out_weight, preferred_element_type=jnp.float32) + jnp.dot(
        mixed, down_weight, preferred_element_type=jnp.float32
    )
    summed = lax.psum(partial_out, "tensor")
    output = (inputs + summed).astype(jnp.bfloat16)
    grad_context = contract_cols(cotangent, out_weight).astype(jnp.bfloat16)
    grad_out_w = contract_rows(context, cotangent)
    grad_down_w = contract_rows(mixed, cotangent)
    grad_out_part, grad_down_part = (
        lax.psum_scatter(grad_out_w, "dp", scatter_dimension=1, tiled=True),
        lax.psum_scatter(grad_down_w, "dp", scatter_dimension=1, tiled=True),
    )
    grad_mixed = contract_cols(cotangent, down_weight)
    grad_up = (grad_mixed * activated).astype(jnp.bfloat16)
    grad_gate = (
        grad_mixed * up_pre * sigmoid_gate * (1.0 + gate_pre * (1.0 - sigmoid_gate))
    ).astype(jnp.bfloat16)
    grad_gate_w = contract_rows(hidden_in, grad_gate)
    grad_up_w = contract_rows(hidden_in, grad_up)
    grad_hidden = contract_cols(grad_gate, gate_weight) + contract_cols(grad_up, up_weight)
    grad_queries, grad_keys, grad_values = lax.map(
        attend_backward,
        (
            seq_queries,
            seq_keys,
            seq_values,
            segment_ids,
            log_total,
            grad_context.reshape(seq_shape),
        ),
    )
    flat_shape = (row_count, head_count, DH)
    grad_queries = rotate_back(grad_queries.reshape(flat_shape) * score_scale, cosine, sine_table)
    grad_keys = rotate_back(grad_keys.reshape(flat_shape), cosine, sine_table)
    grad_joined = (
        jnp.stack([grad_queries, grad_keys, grad_values.reshape(flat_shape)], axis=2)
        .reshape(row_count, head_count * 3 * DH)
        .astype(jnp.bfloat16)
    )
    bias_local = jnp.sum(grad_joined.astype(jnp.float32), 0)
    grad_qkv_w = contract_rows(hidden_in, grad_joined)
    grad_hidden = grad_hidden + contract_cols(grad_joined, qkv_weight)
    grad_qkv_part, grad_gate_part, grad_up_part = (
        lax.psum_scatter(grad_qkv_w, "dp", scatter_dimension=0, tiled=True),
        lax.psum_scatter(grad_gate_w, "dp", scatter_dimension=0, tiled=True),
        lax.psum_scatter(grad_up_w, "dp", scatter_dimension=0, tiled=True),
    )
    grad_total = lax.psum(grad_hidden, "tensor")
    grad_input = (
        cotangent.astype(jnp.float32) + norm_back(grad_total, normed, inverse_std, gain_full)
    ).astype(jnp.bfloat16)
    grad_gain, grad_shift, grad_bias = lax.psum(
        (jnp.sum(grad_total * normed, 0), jnp.sum(grad_total, 0), bias_local), "dp"
    )
    return (
        output,
        grad_input,
        grad_gain,
        grad_shift,
        grad_qkv_part,
        grad_bias,
        grad_out_part,
        grad_gate_part,
        grad_up_part,
        grad_down_part,
    )


BF = jnp.bfloat16
F32 = jnp.float32
MESH = pl.DeviceIdType.MESH
W = 256
PR = 32
SMALL_AT = 2
LATE = 8
WAIT2 = 2


def comm_kernel(
    dims,
    hid_h, cot_h, tok_h, ctx_h, gj_h, z_h, gu_h, gain_ref, bias_ref, qkv_h, gate_h, up_h, down_h,
    out_o, gin_o, sg_o, ss_o, sb_o, gq_o, go_o, gg_o, gu_o, gd_o,
    hid_t, cot, cot_s, tok, ctx, gj, w_a, w_b, w_d, acc, gu, s1, own, recv1, recv2, recv3,
    zs, ze, zm, svb, svr, svq,
    ld_sem, w_sem, s1_send, s1_recv, s2_send, s2_recv, s3_send, s3_recv,
    e_send, e_recv, m_send, m_recv, o_send, o_recv, o_loc, g_sem, v_send, v_recv,
):
    rows, width, full, tail, n_out, n_qkv, n_batch = dims
    n_piece = rows // PR
    hid = zs.at[1]
    t0 = full * W
    b_pairs = n_out + n_qkv
    b_left = b_pairs + 2 * full
    b_up = b_left + 1
    dp = lax.axis_index("dp")
    zi = lax.axis_index("tensor")
    c = lax.rem(dp, 2)
    x = lax.rem(dp // 2, 2)
    y = dp // 4
    core_dev = {"dp": dp + 1 - 2 * c}
    x_dev = {"dp": dp + 2 - 4 * x}
    y_dev = {"dp": dp + 4 - 8 * y}
    is_mid = (zi == 1) | (zi == 2)
    is_end = (zi == 0) | (zi == 3)
    end_of = jnp.where(zi == 1, 0, 3)
    mid_of_end = jnp.where(zi == 0, 1, 2)
    end_dev = {"tensor": end_of}
    mid_dev = {"tensor": mid_of_end}
    other_mid = {"tensor": 3 - zi}

    def load(src, dst, k):
        return pltpu.make_async_copy(src, dst, ld_sem.at[k])

    def w_down(i):
        return pltpu.make_async_copy(down_h.at[pl.ds(i * W, W), :], w_d, w_sem.at[2])

    def w_gate(i):
        return pltpu.make_async_copy(gate_h.at[:, pl.ds(i * W, W)], w_a, w_sem.at[0])

    def w_up(i):
        return pltpu.make_async_copy(up_h.at[:, pl.ds(i * W, W)], w_b, w_sem.at[1])

    def w_qkv(j, side):
        return pltpu.make_async_copy(qkv_h.at[:, pl.ds(j * W, W)], (w_a, w_b)[side], w_sem.at[side])

    w_gate_t = pltpu.make_async_copy(gate_h.at[:, pl.ds(t0, tail)], w_a.at[:, 0:tail], w_sem.at[0])
    w_up_t = pltpu.make_async_copy(up_h.at[:, pl.ds(t0, tail)], w_a.at[:, tail : 2 * tail], w_sem.at[1])
    w_down_t = pltpu.make_async_copy(down_h.at[pl.ds(t0, tail), :], w_d.at[0:tail, :], w_sem.at[2])

    ctx_ld = load(ctx_h, ctx, 0)
    hid_ld = load(hid_h, hid, 1)
    cot_ld = load(cot_h, cot, 2)
    gj_ld = load(gj_h, gj, 3)
    tok_ld = load(tok_h, tok, 4)
    cs_ld = [
        load(cot_h.at[:, (2 * q + s) * W : (2 * q + s + 1) * W], cot_s.at[s, :, q * W : (q + 1) * W], 5 + 2 * q + s)
        for q in range(4)
        for s in range(2)
    ]
    z_ld = load(z_h, zs.at[0], 13)
    gu_ld = load(gu_h, gu, 14)
    z_ld.start()
    ctx_ld.start()
    for cp in cs_ld:
        cp.start()
    hid_ld.start()
    w_qkv(0, 0).start()
    gj_ld.start()
    w_qkv(1, 1).start()
    w_down(0).start()
    tok_ld.start()
    cot_ld.start()
    gu_ld.start()
    acc[...] = jnp.zeros_like(acc)

    barrier = pltpu.get_barrier_semaphore()
    for dev in (core_dev, x_dev, y_dev, {"dp": dp + 2 - 4 * x + 4 - 8 * y}):
        pl.semaphore_signal(barrier, inc=1, device_id=dev, device_id_type=MESH)

    @pl.when(is_mid)
    def _():
        pl.semaphore_signal(barrier, inc=1, device_id=end_dev, device_id_type=MESH)
        pl.semaphore_signal(barrier, inc=1, device_id=other_mid, device_id_type=MESH)

    @pl.when(is_end)
    def _():
        pl.semaphore_signal(barrier, inc=1, device_id=mid_dev, device_id_type=MESH)

    pl.semaphore_wait(barrier, jnp.where(is_mid, 6, 5))

    def rdma(src, dst, send, recv, dev):
        return pltpu.make_async_remote_copy(
            src_ref=src, dst_ref=dst, send_sem=send, recv_sem=recv, device_id=dev, device_id_type=MESH
        )

    def c1(b):
        slot = lax.rem(b, 4)
        return rdma(s1.at[slot], recv1.at[b], s1_send.at[slot], s1_recv.at[b], core_dev)

    def c2(b, h):
        if h == 0:
            return rdma(recv1.at[b, :, 1 - x, 0], recv2.at[b, 0], s2_send.at[b, 0], s2_recv.at[b, 0], x_dev)
        return rdma(recv1.at[b, 1 - y, :, 1], recv2.at[b, 1], s2_send.at[b, 1], s2_recv.at[b, 1], y_dev)

    def c3(b, h):
        if h == 0:
            return rdma(recv2.at[b, 0, 1 - y], recv3.at[b, 0], s3_send.at[b, 0], s3_recv.at[b, 0], y_dev)
        return rdma(recv2.at[b, 1, 1 - x], recv3.at[b, 1], s3_send.at[b, 1], s3_recv.at[b, 1], x_dev)

    def up32(v):
        return v.astype(F32)

    def ev1(b):
        slot = lax.rem(b, 4)
        c1(b).wait_recv()
        for yy in range(2):
            for xx in range(2):
                for h in range(2):
                    recv1[b, yy, xx, h] += own[slot, yy, xx, h]
        c2(b, 0).start()
        c2(b, 1).start()

    def ev2(b):
        c2(b, 0).wait_recv()
        c2(b, 1).wait_recv()
        for k in range(2):
            recv2[b, 0, k] += recv1[b, k, x, 0]
            recv2[b, 1, k] += recv1[b, y, k, 1]
        c3(b, 0).start()
        c3(b, 1).start()

    def cut(b, h, ref, row, col, n=W // 2, lo=0, wide=W):
        if not isinstance(row, int):
            row = pl.multiple_of(row, 64)
        if not isinstance(col, int):
            col = pl.multiple_of(col, W // 2)
        return pltpu.make_async_copy(
            recv3.at[b, h, 0:n, lo : lo + wide], ref.at[pl.ds(row + h * n, n), pl.ds(col, wide)], g_sem.at[b, h]
        )

    groups = (
        (0, n_out, 1, lambda b, h, i: (cut(b, h, go_o, i * W, 0),)),
        (n_out, n_qkv, 1, lambda b, h, i: (cut(b, h, gq_o, 0, i * W),)),
        (b_left, 1, 1, lambda b, h, i: (cut(b, h, gd_o, t0, 0, tail // 2),)),
        (b_pairs, full, 2, lambda b, h, i: (cut(b, h, gd_o, i * W, 0),)),
        (b_pairs + 1, full, 2, lambda b, h, i: (cut(b, h, gg_o, 0, i * W),)),
        (b_up, full, 1, lambda b, h, i: (cut(b, h, gu_o, 0, i * W),)),
        (
            b_up + full, 1, 1,
            lambda b, h, i: (
                cut(b, h, gg_o, 0, t0, wide=tail), cut(b, h, gu_o, 0, t0, lo=tail, wide=tail)
            ),
        ),
    )

    def ev3(b):
        c3(b, 0).wait_recv()
        c3(b, 1).wait_recv()
        recv3[b, 0] += recv2[b, 0, y]
        recv3[b, 1] += recv2[b, 1, x]
        for first, count, step, make in groups:
            here = (b >= first) & (b < first + count * step)
            if step > 1:
                here = here & (lax.rem(b - first, step) == 0)

            @pl.when(here)
            def _(first=first, step=step, make=make):
                for h in range(2):
                    for cp in make(b, h, (b - first) // step):
                        cp.start()

    def before_put(b):
        @pl.when(b >= 4)
        def _():
            c1(b - 4).wait_send()

    def after_put(b):
        c1(b).start()

    def put_rows(b, grad):
        slot = lax.rem(b, 4)
        before_put(b)
        for part, dst in ((1 - c, s1), (c, own)):
            left = hid_t[:, part].reshape(4 * W, rows)
            res = jnp.dot(left, grad, preferred_element_type=F32).astype(BF)
            dst[slot] = res.reshape(2, 2, 2, W // 2, W)
        after_put(b)

    def put_cols(b, left_t):
        slot = lax.rem(b, 4)
        h = left_t.shape[0]
        before_put(b)
        for part, dst in ((1 - c, s1), (c, own)):
            res = jnp.dot(left_t, cot_s[part], preferred_element_type=F32).astype(BF)
            for q in range(4):
                piece = res[:, q * W : (q + 1) * W].reshape(2, h // 2, W)
                dst[slot, q // 2, q % 2, :, 0 : h // 2, :] = piece
                if h < W:
                    dst[slot, q // 2, q % 2, :, h // 2 :, :] = jnp.zeros((2, (W - h) // 2, W), BF)
        after_put(b)

    NB = 512

    def acc_rows(grad, w_ref):
        for n in range(width // NB):
            cols = slice(n * NB, (n + 1) * NB)
            acc[:, cols] += lax.dot_general(
                grad, w_ref[cols, :], (((1,), (1,)), ((), ())), preferred_element_type=F32
            )

    def z_rows(p):
        return pl.ds(pl.multiple_of(p * PR, PR), PR)

    def ce(a, p):
        i = a * n_piece + p
        return rdma(zs.at[a, z_rows(p)], ze.at[a, z_rows(p)], e_send.at[i], e_recv.at[i], mid_dev)

    def cm(a, p):
        i = a * n_piece + p
        return rdma(zs.at[a, z_rows(p)], zm.at[a, z_rows(p)], m_send.at[i], m_recv.at[i], other_mid)

    def co(a, p, ref):
        i = a * n_piece + p
        return rdma(ze.at[a, z_rows(p)], ref.at[z_rows(p)], o_send.at[i], o_recv.at[i], end_dev)

    def cl(a, p, ref):
        i = a * n_piece + p
        return pltpu.make_async_copy(ze.at[a, z_rows(p)], ref.at[z_rows(p)], o_loc.at[i])

    def ev_e(e):
        a, p = e // n_piece, lax.rem(e, n_piece)

        @pl.when(is_mid)
        def _():
            ce(a, p).wait_recv()
            r = z_rows(p)
            zs[a, r, :] += ze[a, r, :]
            cm(a, p).start()

    def norm_rows(r):
        v = up32(tok[r, :])
        mu = jnp.mean(v, -1, keepdims=True)
        v = v - mu
        inv = lax.rsqrt(jnp.mean(v * v, -1, keepdims=True) + EPSILON)
        return v * inv, inv

    def ev_m(e):
        a, p = e // n_piece, lax.rem(e, n_piece)

        @pl.when(is_mid)
        def _():
            cm(a, p).wait_recv()
            r = z_rows(p)

            @pl.when(a == 0)
            def _():
                total = up32(zs[0, r, :]) + up32(zm[0, r, :])
                ze[0, r, :] = (up32(tok[r, :]) + total).astype(BF)
                co(0, p, out_o).start()
                cl(0, p, out_o).start()

            @pl.when(a == 1)
            def _():
                total = up32(zs[1, r, :]) + up32(zm[1, r, :])
                normed, inv = norm_rows(r)
                back = norm_back(total, normed, inv, gain_ref[...])
                ze[1, r, :] = (up32(cot[r, :]) + back).astype(BF)
                co(1, p, gin_o).start()
                cl(1, p, gin_o).start()

    def act_of(g, u):
        return (g * jax.nn.sigmoid(g) * u).astype(BF)

    def joined_grad(j):
        return jnp.concatenate([gj[2 * j], gj[2 * j + 1]], axis=1)

    def cv(k, dev):
        return rdma(svb.at[k], svr.at[k], v_send.at[k], v_recv.at[k], dev)

    def cw(k, dev):
        return rdma(svb.at[4], svq.at[y, x], v_send.at[4 + k], v_recv.at[4 + k], dev)

    square = (x_dev, y_dev, {"dp": dp + 2 - 4 * x + 4 - 8 * y})

    def small_1():
        @pl.when(is_mid)
        def _():
            cv(0, end_dev).wait_recv()
            svb[1] = svb[0] + svr[0]
            cv(1, other_mid).start()

    def small_2():
        @pl.when(is_mid)
        def _():
            cv(1, other_mid).wait_recv()
            svb[2] = svb[1] + svr[1]
            svb[3, 0:2, :] = svb[2, 0:2, :]
            cv(2, end_dev).start()

    def small_3():
        @pl.when(is_end)
        def _():
            cv(2, mid_dev).wait_recv()
            svb[3, 0:2, :] = svr[2, 0:2, :]

        svb[3, 2:8, :] = svb[0, 2:8, :]
        cv(3, core_dev).start()

    def small_4():
        cv(3, core_dev).wait_recv()
        svb[4] = svb[3] + svr[3]
        svq[y, x] = svb[4]
        for k, dev in enumerate(square):
            cw(k, dev).start()

    def small_5():
        for k, dev in enumerate(square):
            cw(k, dev).wait_recv()
        total = (svq[0, 0] + svq[0, 1]) + (svq[1, 0] + svq[1, 1])
        for row, ref in enumerate((sg_o, ss_o, sb_o)):
            for n in range(ref.shape[0]):
                ref[n : n + 1, :] = total[row : row + 1, n * 128 : (n + 1) * 128]

    def small_sent():
        @pl.when(is_end)
        def _():
            cv(0, mid_dev).wait_send()

        @pl.when(is_mid)
        def _():
            cv(1, other_mid).wait_send()
            cv(2, end_dev).wait_send()

        cv(3, core_dev).wait_send()
        for k, dev in enumerate(square):
            cw(k, dev).wait_send()

    def send_line(a):
        def send(p, keep):
            ce(a, p).start()
            return keep

        @pl.when(is_end)
        def _():
            if a == 1:
                cv(0, mid_dev).start()
            lax.fori_loop(0, n_piece, send, 0)

    def line_rows(p, keep):
        r = z_rows(p)
        v = acc[r, :]
        zs[1, r, :] = v.astype(BF)
        normed, _inv = norm_rows(r)
        svb[0, 0:1, :] += jnp.sum(v * normed, 0, keepdims=True)
        svb[0, 1:2, :] += jnp.sum(v, 0, keepdims=True)
        return keep

    z_ld.wait()
    send_line(0)
    ctx_ld.wait()
    for cp in cs_ld:
        cp.wait()
    for j in range(n_out):
        put_cols(jnp.int32(j), ctx[:, j * W : (j + 1) * W].T)
    hid_ld.wait()
    for q in range(4):
        for s in range(2):
            lo = (2 * q + s) * W
            hid_t[q, s] = hid[:, lo : lo + W].T
    for b in range(n_out):
        ev1(jnp.int32(b))
    gj_ld.wait()
    tok_ld.wait()
    cot_ld.wait()

    def joined(n, keep):
        for side in range(2):
            j = 2 * n + side
            w_qkv(j, side).wait()
            acc_rows(joined_grad(j), (w_a, w_b)[side])

            @pl.when(j + 2 < n_qkv)
            def _(j=j, side=side):
                w_qkv(j + 2, side).start()

            @pl.when(j + 2 >= n_qkv)
            def _(side=side):
                (w_gate, w_up)[side](0).start()

            b = n_out + j
            put_rows(b, joined_grad(j))

            @pl.when(j >= 1)
            def _(b=b):
                ev1(b - 1)

        ev_e(n)

        @pl.when(n >= 1)
        def _():
            ev2(n - 1)

        @pl.when(n >= 2)
        def _():
            ev_m(n - 2)

        return keep

    lax.fori_loop(0, n_qkv // 2, joined, 0)
    gu_ld.wait()

    def gate_grads(gm, g, u):
        sg = jax.nn.sigmoid(g)
        g_up = (gm * (g * sg)).astype(BF)
        g_gate = (gm * u * sg * (1.0 + g * (1.0 - sg))).astype(BF)
        return g_gate, g_up

    def cols_t(left, w_ref, k):
        return lax.dot_general(left, w_ref[0:k, :], (((1,), (1,)), ((), ())), preferred_element_type=F32)

    e0 = n_qkv // 2
    two = n_qkv // 2 - 1

    def bwd(i, keep):
        w_down(i).wait()
        gm = cols_t(cot[...], w_d, W)

        @pl.when(i + 1 < full)
        def _():
            w_down(i + 1).start()

        @pl.when(i + 1 == full)
        def _():
            w_down_t.start()

        g, u = up32(gu[i, 0]), up32(gu[i, 1])
        mixed = act_of(g, u)
        g_gate, g_up = gate_grads(gm, g, u)
        gu[i, 0] = g_gate
        gu[i, 1] = g_up
        w_gate(i).wait()
        acc_rows(g_gate, w_a)
        w_up(i).wait()
        acc_rows(g_up, w_b)

        @pl.when(i + 1 < full)
        def _():
            w_gate(i + 1).start()
            w_up(i + 1).start()

        @pl.when(i + 1 == full)
        def _():
            w_gate_t.start()
            w_up_t.start()

        b = b_pairs + 2 * i
        e = e0 + 2 * i
        put_cols(b, mixed.T)
        ev1(b - 1)
        ev_e(e)
        ev_m(e - 2)
        put_rows(b + 1, gu[i, 0])
        ev1(b)
        ev2(two + i)
        ev_e(e + 1)
        ev_m(e - 1)
        return keep

    lax.fori_loop(0, full, bwd, 0)
    w_down_t.wait()
    gm = cols_t(cot[...], w_d, tail)
    both = up32(gu[full, 0])
    mixed = act_of(both[:, 0:tail], both[:, tail:])
    g_gate, g_up = gate_grads(gm, both[:, 0:tail], both[:, tail:])
    both = jnp.concatenate([g_gate, g_up], axis=1)
    gu[full, 0] = both
    w_gate_t.wait()
    w_up_t.wait()
    acc_rows(both, w_a)
    svb[0] = jnp.zeros_like(svb[0])
    svb[0, 2:3, 0 : n_qkv * W] = bias_ref[...]
    lax.fori_loop(0, n_piece, line_rows, 0)
    send_line(1)

    put_cols(jnp.int32(b_left), mixed.T)
    ev1(jnp.int32(b_left - 1))
    e0 = e0 + 2 * full
    two = two + full
    ev2(jnp.int32(two))
    ev_e(jnp.int32(e0))
    ev_m(jnp.int32(e0 - 2))

    def left_over(i, keep):
        b = b_up + i
        at = jnp.where(i == full, 0, 1)
        put_rows(b, gu[i, at])
        ev1(b - 1)
        ev2(two + 1 + i)
        ev_e(e0 + 1 + i)
        ev_m(e0 - 1 + i)
        return keep

    lax.fori_loop(0, full + 1, left_over, 0)
    ev1(jnp.int32(n_batch - 1))
    e0 = e0 + full + 2
    two_left = two + full + 2

    n_e = 2 * n_piece
    smalls = (small_1, small_2, small_3, small_4)

    def drain(k, keep):
        @pl.when(k + e0 < n_e)
        def _():
            ev_e(k + e0)

        @pl.when(k + e0 - 2 < n_e)
        def _():
            ev_m(k + e0 - 2)

        @pl.when((k >= WAIT2) & (k - WAIT2 + two_left < n_batch))
        def _():
            ev2(k - WAIT2 + two_left)

        for i, small in enumerate(smalls):
            pl.when(k == SMALL_AT + i)(small)

        for h in range(2):
            b = 2 * (k - LATE) + h

            @pl.when((b >= 0) & (b < n_batch))
            def _():
                ev3(b)

        return keep

    steps = max(LATE + (n_batch + 1) // 2, n_e - e0 + 2, WAIT2 + n_batch - two_left)
    lax.fori_loop(0, steps, drain, 0)
    small_5()

    small_sent()

    def finish(b, keep):
        for h in range(2):
            c2(b, h).wait_send()
            c3(b, h).wait_send()
        return keep

    lax.fori_loop(0, n_batch, finish, 0)
    for k in range(4):
        c1(jnp.int32(n_batch - 4 + k)).wait_send()
    for first, count, step, make in groups:
        for i in range(count):
            for h in range(2):
                for cp in make(first + i * step, h, i):
                    cp.wait()

    def finish_line(p, keep):
        for a, ref in ((0, out_o), (1, gin_o)):
            @pl.when(is_mid)
            def _():
                cm(a, p).wait_send()
                co(a, p, ref).wait_send()
                cl(a, p, ref).wait()

            @pl.when(is_end)
            def _():
                ce(a, p).wait_send()
                co(a, p, ref).wait_recv()

        return keep

    lax.fori_loop(0, n_piece, finish_line, 0)


def comm_call(hidden, cot, tokens, ctx, gj, partial, gu, gain, bias_sum, qkv_w, gate_w, up_w, down_w):
    rows, width = hidden.shape
    hd = ctx.shape[1]
    ff = gate_w.shape[1]
    full, tail = ff // W, ff % W
    n_out, n_qkv = hd // W, qkv_w.shape[1] // W
    n_batch = n_out + full + 1 + n_qkv + 2 * full + 1
    n_z = 2 * (rows // PR)
    dims = (rows, width, full, tail, n_out, n_qkv, n_batch)
    piece = (W // 2, W)
    vm, dma = pltpu.VMEM, pltpu.SemaphoreType.DMA
    any_spec = pl.BlockSpec(memory_space=pl.ANY)
    vm_spec = pl.BlockSpec(memory_space=pltpu.VMEM)
    return pl.pallas_call(
        functools.partial(comm_kernel, dims),
        out_shape=(
            jax.ShapeDtypeStruct((rows, width), BF),
            jax.ShapeDtypeStruct((rows, width), BF),
            jax.ShapeDtypeStruct((width // 128, 128), F32),
            jax.ShapeDtypeStruct((width // 128, 128), F32),
            jax.ShapeDtypeStruct((n_qkv * W // 128, 128), F32),
            jax.ShapeDtypeStruct((W, n_qkv * W), BF),
            jax.ShapeDtypeStruct((hd, W), BF),
            jax.ShapeDtypeStruct((W, ff), BF),
            jax.ShapeDtypeStruct((W, ff), BF),
            jax.ShapeDtypeStruct((ff, W), BF),
        ),
        in_specs=[any_spec] * 7 + [vm_spec] * 2 + [any_spec] * 4,
        out_specs=(any_spec,) * 2 + (vm_spec,) * 3 + (any_spec,) * 5,
        scratch_shapes=[
            vm((4, 2, W, rows), BF),
            vm((rows, width), BF),
            vm((2, rows, width // 2), BF),
            vm((rows, width), BF),
            vm((rows, hd), BF),
            vm((2 * n_qkv, rows, W // 2), BF),
            vm((width, W), BF),
            vm((width, W), BF),
            vm((W, width), BF),
            vm((rows, width), F32),
            vm((full + 1, 2, rows, W), BF),
            vm((4, 2, 2, 2) + piece, BF),
            vm((4, 2, 2, 2) + piece, BF),
            vm((n_batch, 2, 2, 2) + piece, BF),
            vm((n_batch, 2, 2) + piece, BF),
            vm((n_batch, 2) + piece, BF),
            vm((2, rows, width), BF),
            vm((2, rows, width), BF),
            vm((2, rows, width), BF),
            vm((5, 8, width), F32),
            vm((4, 8, width), F32),
            vm((2, 2, 8, width), F32),
            dma((15,)),
            dma((3,)),
            dma((4,)),
            dma((n_batch,)),
            dma((n_batch, 2)),
            dma((n_batch, 2)),
            dma((n_batch, 2)),
            dma((n_batch, 2)),
            dma((n_z,)),
            dma((n_z,)),
            dma((n_z,)),
            dma((n_z,)),
            dma((n_z,)),
            dma((n_z,)),
            dma((n_z,)),
            dma((n_batch, 2)),
            dma((7,)),
            dma((7,)),
        ],
        compiler_params=pltpu.CompilerParams(
            collective_id=0, has_side_effects=True, vmem_limit_bytes=67043328
        ),
        name="ffn_and_sums",
    )(hidden, cot, tokens, ctx, gj, partial, gu, gain, bias_sum, qkv_w, gate_w, up_w, down_w)


def forward_kernel(full, tail, hid, ctx, out_w, gate_w, up_w, down_w, z_o, gu_o, acc):
    i = pl.program_id(0)
    width = acc.shape[1]
    blocks = [slice(n, n + 512) for n in range(0, width, 512)]

    def dot(a, b):
        return jnp.dot(a, b, preferred_element_type=F32)

    def act_of(g, u):
        return (g * jax.nn.sigmoid(g) * u).astype(BF)

    @pl.when(i == 0)
    def _():
        for cols in blocks:
            acc[:, cols] = dot(ctx[...], out_w[:, cols])

    @pl.when(i < full)
    def _():
        g = dot(hid[...], gate_w[...])
        u = dot(hid[...], up_w[...])
        gu_o[0, 0] = g.astype(BF)
        gu_o[0, 1] = u.astype(BF)
        mixed = act_of(g, u)
        for cols in blocks:
            acc[:, cols] += dot(mixed, down_w[:, cols])

    @pl.when(i == full)
    def _():
        both = dot(hid[...], jnp.concatenate([gate_w[:, 0:tail], up_w[:, 0:tail]], axis=1))
        gu_o[0, 0] = both.astype(BF)
        gu_o[0, 1] = jnp.zeros_like(both).astype(BF)
        mixed = act_of(both[:, 0:tail], both[:, tail:])
        for cols in blocks:
            z_o[:, cols] = (acc[:, cols] + dot(mixed, down_w[0:tail, cols])).astype(BF)


def forward_call(hidden, ctx, out_w, gate_w, up_w, down_w):
    rows, width = hidden.shape
    hd = ctx.shape[1]
    ff = gate_w.shape[1]
    full, tail = ff // W, ff % W
    once = lambda shape: pl.BlockSpec(shape, lambda i: (0,) * len(shape), pipeline_mode=pl.Buffered(1))
    return pl.pallas_call(
        functools.partial(forward_kernel, full, tail),
        grid=(full + 1,),
        out_shape=(
            jax.ShapeDtypeStruct((rows, width), BF),
            jax.ShapeDtypeStruct((full + 1, 2, rows, W), BF),
        ),
        in_specs=[
            once((rows, width)),
            once((rows, hd)),
            once((hd, width)),
            pl.BlockSpec((width, W), lambda i: (0, i)),
            pl.BlockSpec((width, W), lambda i: (0, i)),
            pl.BlockSpec((W, width), lambda i: (i, 0)),
        ],
        out_specs=(
            once((rows, width)),
            pl.BlockSpec((1, 2, rows, W), lambda i: (i, 0, 0, 0)),
        ),
        scratch_shapes=[pltpu.VMEM((rows, width), F32)],
        compiler_params=pltpu.CompilerParams(vmem_limit_bytes=60 << 20),
        name="forward",
    )(hidden, ctx, out_w, gate_w, up_w, down_w)


PARTS = 4


def finish_kernel(*refs):
    n = len(refs) // 2
    for src, dst in zip(refs[:n], refs[n:]):
        dst[...] = src[...].astype(dst.dtype)


def finish_call(values, types):
    def spec(v):
        if v.shape[0] < 16 * PARTS:
            return pl.BlockSpec(v.shape, lambda i: (0, 0))
        return pl.BlockSpec((v.shape[0] // PARTS, v.shape[1]), lambda i: (i, 0))

    return pl.pallas_call(
        finish_kernel,
        grid=(PARTS,),
        out_shape=tuple(jax.ShapeDtypeStruct(v.shape, t) for v, t in zip(values, types)),
        in_specs=[spec(v) for v in values],
        out_specs=tuple(spec(v) for v in values),
        compiler_params=pltpu.CompilerParams(vmem_limit_bytes=60 << 20),
        name="finish",
    )(*values)


QB = 128
ROWS = 32


def attn_kernel(
    heads_scale, tok, seg_ref, gain_ref, shift_ref, b_ref, w_ref, ow_ref, cot,
    hid, ctx_o, gj_o, bias_o, gain_o,
    bias_m, tab, s_m, g_m, p_m, gs_m, shift_m, b_m,
):
    rows = tok.shape[0]
    nq = rows // QB
    half = ROT // 2

    step = pl.program_id(0)

    @pl.when(step == 0)
    def _():
        for n in range(gain_ref.shape[0]):
            cols = slice(n * QB, (n + 1) * QB)
            gain_o[0:1, cols] = gain_ref[n : n + 1, :].astype(F32)
            shift_m[0:1, cols] = shift_ref[n : n + 1, :].astype(F32)
        b_m[...] = b_ref[...].astype(F32)

        def norm_step(n, keep):
            r = pl.ds(pl.multiple_of(n * 64, 64), 64)
            v = tok[r, :].astype(F32)
            v = v - jnp.mean(v, -1, keepdims=True)
            v = v * lax.rsqrt(jnp.mean(v * v, -1, keepdims=True) + EPSILON)
            hid[r, :] = (v * gain_o[...] + shift_m[...]).astype(BF)
            return keep

        lax.fori_loop(0, rows // 64, norm_step, 0)
        seg = seg_ref[...].astype(F32)
        seg_t = jnp.broadcast_to(seg, (8, rows)).T
        lane = lax.broadcasted_iota(jnp.int32, (QB, QB), 1)
        head_lane = lane % DH
        freq = jnp.ones((1, QB), F32)
        for n in range(1, half):
            freq = jnp.where(head_lane[0:1] % half == n, 10000.0 ** (-2.0 * n / ROT), freq)
        group = QB // nq
        packed = jnp.zeros((QB, QB), F32)
        for i in range(nq):
            lo = max(0, i - 2) * QB
            n = (i + 1) * QB - lo
            q_at = lax.broadcasted_iota(jnp.int32, (QB, n), 0) + i * QB
            k_at = lax.broadcasted_iota(jnp.int32, (QB, n), 1) + lo
            same = seg_t[i * QB : (i + 1) * QB, 0:1] == seg[:, lo : lo + n]
            allowed = same & (q_at >= k_at)
            bias_m[i, :, 0:n] = jnp.where(allowed, 0.0, NEGATIVE)
            place = jnp.sum(jnp.where(allowed, 1.0, 0.0), -1, keepdims=True) - 1.0
            packed = jnp.where(lane // group == i, place, packed)
        angle = packed * freq
        tables = jnp.cos(angle), jnp.sin(angle)
        for i in range(nq):
            cosine, sine = (
                jnp.where(
                    lane < DH,
                    pltpu.roll(t, (QB - group * i) % QB, 1) if i else t,
                    pltpu.roll(t, (QB + DH - group * i) % QB, 1) if DH != group * i else t,
                )
                for t in tables
            )
            for blk in range(3):
                live = head_lane < ROT
                if blk == 1:
                    live = live & (lane >= DH)
                if blk == 2:
                    live = live & (lane < DH)
                scale = jnp.ones((QB, QB), F32)
                if blk == 0:
                    scale = jnp.where(lane < DH, heads_scale, 1.0)
                if blk == 1:
                    scale = jnp.where(lane >= DH, heads_scale, 1.0)
                r = slice(i * QB, (i + 1) * QB)
                tab[blk, 0, r] = jnp.where(live, cosine, 1.0) * scale
                tab[blk, 1, r] = jnp.where(live & (head_lane < half), -sine, 0.0) * scale
                tab[blk, 2, r] = jnp.where(live & (head_lane >= half), sine, 0.0) * scale

    def dot_t(a, b):
        return lax.dot_general(a, b, (((1,), (1,)), ((), ())), preferred_element_type=F32)

    def dot(a, b):
        return jnp.dot(a, b, preferred_element_type=F32)

    joined = dot(hid[...], w_ref[...])
    turned = []
    for blk in range(3):
        v = joined[:, blk * QB : (blk + 1) * QB] + b_m[pl.ds(3 * step + blk, 1), :]
        v = v * tab[blk, 0] + pltpu.roll(v, QB - half, 1) * tab[blk, 1] + pltpu.roll(v, half, 1) * tab[blk, 2]
        turned.append(v.astype(BF))
    gctx = dot_t(cot[...], ow_ref[...]).astype(BF)
    lo_h, hi_h = slice(0, DH), slice(DH, 2 * DH)
    heads = (
        (turned[0][:, lo_h], turned[0][:, hi_h], turned[1][:, lo_h], gctx[:, lo_h]),
        (turned[1][:, hi_h], turned[2][:, lo_h], turned[2][:, hi_h], gctx[:, hi_h]),
    )
    spans = [(max(0, i - 2) * QB, (i + 1) * QB) for i in range(nq)]
    blocks = [(n, i) for i in range(nq) for n in range(2)]
    for n, i in blocks:
        q, k, v, gc = heads[n]
        lo, hi = spans[i]
        s_m[n, i, :, 0 : hi - lo] = dot_t(q[i * QB : hi], k[lo:hi])
        g_m[n, i, :, 0 : hi - lo] = dot_t(gc[i * QB : hi], v[lo:hi])
    for n, i in blocks:
        lo, hi = spans[i]
        for r in range(0, QB, ROWS):
            rr = slice(r, r + ROWS)
            s = s_m[n, i, rr, 0 : hi - lo] + bias_m[i, rr, 0 : hi - lo]
            e = jnp.exp(s - jnp.max(s, -1, keepdims=True))
            p = e * (1.0 / jnp.sum(e, -1, keepdims=True))
            gp = g_m[n, i, rr, 0 : hi - lo]
            p_m[n, i, rr, 0 : hi - lo] = p.astype(BF)
            gs_m[n, i, rr, 0 : hi - lo] = (p * (gp - jnp.sum(p * gp, -1, keepdims=True))).astype(BF)
    grads, contexts = [], []
    for n, (q, k, v, gc) in enumerate(heads):
        out, grad_q, grad_k, grad_v = [], [], [], []
        for i, (lo, hi) in enumerate(spans):
            out.append(dot(p_m[n, i, :, 0 : hi - lo], v[lo:hi]))
            grad_q.append(dot(gs_m[n, i, :, 0 : hi - lo], k[lo:hi]))
        for j in range(nq):
            top = min(j + 3, nq)

            def stack(part):
                cut = []
                for i in range(j, top):
                    at = j * QB - spans[i][0]
                    cut.append(part[n, i, :, at : at + QB].T)
                return jnp.concatenate(cut, 1)

            grad_k.append(dot(stack(gs_m), q[j * QB : top * QB]))
            grad_v.append(dot(stack(p_m), gc[j * QB : top * QB]))
        contexts.append(jnp.concatenate(out, 0))
        grads.append([jnp.concatenate(part, 0) for part in (grad_q, grad_k, grad_v)])
    ctx_o[...] = jnp.concatenate(contexts, 1).astype(BF)
    (q0, k0, v0), (q1, k1, v1) = grads
    for blk, pair in enumerate(((q0, k0), (v0, q1), (k1, v1))):
        g = jnp.concatenate(pair, 1)
        g = g * tab[blk, 0] - pltpu.roll(g, QB - half, 1) * tab[blk, 1] - pltpu.roll(g, half, 1) * tab[blk, 2]
        g = g.astype(BF)
        gj_o[blk] = g
        bias_o[:, blk * QB : (blk + 1) * QB] = jnp.sum(g.astype(F32), 0, keepdims=True)


def attn_call(tokens, segment_ids, gain, shift, qkv_w, qkv_b, out_w, cot):
    rows, width = tokens.shape
    hd = out_w.shape[0]
    steps = hd // (2 * DH)
    three = 3 * QB
    whole = lambda shape: pl.BlockSpec(shape, lambda i: (0,) * len(shape))
    once = lambda shape: pl.BlockSpec(shape, lambda i: (0,) * len(shape), pipeline_mode=pl.Buffered(1))
    return pl.pallas_call(
        functools.partial(attn_kernel, DH ** (-0.5)),
        grid=(steps,),
        out_shape=(
            jax.ShapeDtypeStruct((rows, width), BF),
            jax.ShapeDtypeStruct((rows, hd), BF),
            jax.ShapeDtypeStruct((3 * steps, rows, QB), BF),
            jax.ShapeDtypeStruct((1, 3 * hd), F32),
            jax.ShapeDtypeStruct((1, width), F32),
        ),
        in_specs=[
            once((rows, width)),
            whole((1, rows)),
            whole((width // QB, QB)),
            whole((width // QB, QB)),
            whole((3 * hd // QB, QB)),
            pl.BlockSpec((width, three), lambda i: (0, i)),
            pl.BlockSpec((QB, width), lambda i: (i, 0)),
            once((rows, width)),
        ],
        out_specs=(
            whole((rows, width)),
            pl.BlockSpec((rows, QB), lambda i: (0, i)),
            pl.BlockSpec((3, rows, QB), lambda i: (i, 0, 0)),
            pl.BlockSpec((1, three), lambda i: (0, i)),
            whole((1, width)),
        ),
        scratch_shapes=[
            pltpu.VMEM((rows // QB, QB, three), F32),
            pltpu.VMEM((3, 3, rows, QB), F32),
            pltpu.VMEM((2, rows // QB, QB, three), F32),
            pltpu.VMEM((2, rows // QB, QB, three), F32),
            pltpu.VMEM((2, rows // QB, QB, three), BF),
            pltpu.VMEM((2, rows // QB, QB, three), BF),
            pltpu.VMEM((1, width), F32),
            pltpu.VMEM((3 * hd // QB, QB), F32),
        ],
        compiler_params=pltpu.CompilerParams(vmem_limit_bytes=60 << 20),
        name="attention",
    )(
        tokens, segment_ids, gain.reshape(-1, QB), shift.reshape(-1, QB), qkv_b.reshape(-1, QB), qkv_w, out_w, cot
    )


def fast(
    n_dp,
    n_tensor,
    tokens,
    segment_ids,
    norm_gain,
    norm_bias,
    qkv_weight,
    qkv_bias,
    out_weight,
    gate_weight,
    up_weight,
    down_weight,
    cotangent,
):
    args = (tokens, segment_ids, norm_gain, norm_bias, qkv_weight, qkv_bias, out_weight, gate_weight, up_weight, down_weight, cotangent)
    row_count, width = tokens.shape
    ff = gate_weight.shape[1]
    fits = (
        (n_dp, n_tensor) == (8, 4)
        and segment_ids.shape == (1, row_count)
        and (row_count, width) == (512, 8 * W)
        and ff % W == W // 2
        and qkv_weight.shape[1] % (2 * W) == 0
        and out_weight.shape[0] % W == 0
        and qkv_weight.shape[1] == 3 * out_weight.shape[0]
        and 2 * DH == QB
        and 4 * ROT <= QB
    )
    if not fits:
        return local(*args)
    hidden_in, context, grad_joined, bias_local, gain_row = attn_call(
        tokens, segment_ids, norm_gain, norm_bias, qkv_weight, qkv_bias, out_weight, cotangent
    )
    partial, gate_up = forward_call(hidden_in, context, out_weight, gate_weight, up_weight, down_weight)
    results = comm_call(
        hidden_in, cotangent, tokens, context, grad_joined, partial, gate_up, gain_row, bias_local,
        qkv_weight, gate_weight, up_weight, down_weight,
    )
    output, grad_input, gain_sum, shift_sum, bias_sum, joined_w, out_w, gate_w, up_w, down_w = finish_call(
        results, (BF,) * 2 + (F32,) * 8
    )
    return (
        output,
        grad_input,
        gain_sum.reshape(width),
        shift_sum.reshape(width),
        joined_w,
        bias_sum.reshape(qkv_weight.shape[1]),
        out_w,
        gate_w,
        up_w,
        down_w,
    )


def solution(mesh):
    body = functools.partial(fast, mesh.shape["dp"], mesh.shape["tensor"])
    return jax.shard_map(
        body,
        mesh=mesh,
        in_specs=(
            P("dp", None),
            P("dp", None),
            P(),
            P(),
            P(None, "tensor"),
            P("tensor"),
            P("tensor", None),
            P(None, "tensor"),
            P(None, "tensor"),
            P("tensor", None),
            P("dp", None),
        ),
        out_specs=(
            P("dp", None),
            P("dp", None),
            P(),
            P(),
            P("dp", "tensor"),
            P("tensor"),
            P("tensor", "dp"),
            P("dp", "tensor"),
            P("dp", "tensor"),
            P("tensor", "dp"),
        ),
        check_vma=False,
    )
```

```python
import functools

import jax
import jax.numpy as jnp
from jax import lax
from jax.experimental import pallas as pl
from jax.experimental.pallas import tpu as pltpu
from jax.sharding import PartitionSpec as P

DH = 64
ROT = 16


EPSILON = 1e-05
NEGATIVE = -1e30


def positions_of(segments):
    column = jnp.arange(segments.shape[1], dtype=jnp.int32)
    starts = jnp.concatenate(
        [jnp.ones((segments.shape[0], 1), dtype=bool), segments[:, 1:] != segments[:, :-1]], axis=1
    )
    doc_start = lax.cummax(jnp.where(starts, column[None, :], 0), axis=1)
    return column[None, :] - doc_start


def rotary_tables(positions):
    half_rot = ROT // 2
    frequency = jnp.power(10000.0, -2.0 * jnp.arange(half_rot, dtype=jnp.float32) / ROT)
    angles = positions.astype(jnp.float32)[:, None] * frequency[None, :]
    return (jnp.cos(angles)[:, None, :], jnp.sin(angles)[:, None, :])


def rotate(tensor, cosine, sine_table):
    half_rot = ROT // 2
    first_half = tensor[..., :half_rot]
    second_half = tensor[..., half_rot:ROT]
    return jnp.concatenate(
        [
            first_half * cosine - second_half * sine_table,
            second_half * cosine + first_half * sine_table,
            tensor[..., ROT:],
        ],
        axis=-1,
    )


def rotate_back(tensor, cosine, sine_table):
    half_rot = ROT // 2
    first_half = tensor[..., :half_rot]
    second_half = tensor[..., half_rot:ROT]
    return jnp.concatenate(
        [
            first_half * cosine + second_half * sine_table,
            second_half * cosine - first_half * sine_table,
            tensor[..., ROT:],
        ],
        axis=-1,
    )


def masked_scores(query_block, seq_keys, seq_segments, begin_row, block_rows):
    key_index = jnp.arange(seq_keys.shape[0], dtype=jnp.int32)
    allowed = (seq_segments[begin_row : begin_row + block_rows, None] == seq_segments[None, :]) & (
        key_index[:, None] >= key_index[None, :]
    )
    scores = jnp.einsum("qhd,khd->hqk", query_block, seq_keys, preferred_element_type=jnp.float32)
    return jnp.where(allowed[None], scores, NEGATIVE)


def attend_forward(packed):
    seq_queries, seq_keys, seq_values, seq_segments = packed
    length = seq_queries.shape[0]
    block_rows = min(512, length)
    scores = masked_scores(seq_queries, seq_keys, seq_segments, 0, block_rows)
    top_score = jnp.max(scores, -1, keepdims=True)
    weights = jnp.exp(scores - top_score)
    denominator = jnp.sum(weights, -1, keepdims=True)
    probability = (weights / denominator).astype(jnp.bfloat16)
    contexts = [
        jnp.einsum("hqk,khd->qhd", probability, seq_values, preferred_element_type=jnp.float32)
    ]
    log_totals = [top_score + jnp.log(denominator)]
    return (jnp.concatenate(contexts, 0), jnp.concatenate(log_totals, 1))


def attend_backward(packed):
    seq_queries, seq_keys, seq_values, seq_segments, seq_log_total, seq_grad_context = packed
    length = seq_queries.shape[0]
    block_rows = min(512, length)
    grad_keys = jnp.zeros(seq_keys.shape, jnp.float32)
    grad_values = jnp.zeros(seq_values.shape, jnp.float32)
    scores = masked_scores(seq_queries, seq_keys, seq_segments, 0, block_rows)
    probability = jnp.exp(scores - seq_log_total[:, 0:block_rows])
    grad_prob = jnp.einsum(
        "qhd,khd->hqk", seq_grad_context, seq_values, preferred_element_type=jnp.float32
    )
    row_dot = jnp.sum(probability * grad_prob, -1, keepdims=True)
    grad_scores = (probability * (grad_prob - row_dot)).astype(jnp.bfloat16)
    grad_queries = [
        jnp.einsum("hqk,khd->qhd", grad_scores, seq_keys, preferred_element_type=jnp.float32)
    ]
    grad_keys = grad_keys + jnp.einsum(
        "hqk,qhd->khd", grad_scores, seq_queries, preferred_element_type=jnp.float32
    )
    grad_values = grad_values + jnp.einsum(
        "hqk,qhd->khd",
        probability.astype(jnp.bfloat16),
        seq_grad_context,
        preferred_element_type=jnp.float32,
    )
    return (jnp.concatenate(grad_queries, 0), grad_keys, grad_values)


def contract_rows(left_side, right_side):
    return lax.dot_general(
        left_side, right_side, (((0,), (0,)), ((), ())), preferred_element_type=jnp.float32
    )


def contract_cols(left_side, right_side):
    return lax.dot_general(
        left_side, right_side, (((1,), (1,)), ((), ())), preferred_element_type=jnp.float32
    )


def norm_back(grad_normed_out, normed, inverse_std, gain_full):
    grad_normed = grad_normed_out * gain_full
    return inverse_std * (
        grad_normed
        - jnp.mean(grad_normed, -1, keepdims=True)
        - normed * jnp.mean(grad_normed * normed, -1, keepdims=True)
    )


def local(
    tokens,
    segment_ids,
    norm_gain,
    norm_bias,
    qkv_weight,
    qkv_bias,
    out_weight,
    gate_weight,
    up_weight,
    down_weight,
    cotangent,
):
    row_count = tokens.shape[0]
    seq_count, length = segment_ids.shape
    head_count = qkv_weight.shape[1] // (3 * DH)
    score_scale = DH ** (-0.5)
    inputs = tokens.astype(jnp.float32)
    row_mean = jnp.mean(inputs, -1, keepdims=True)
    centered = inputs - row_mean
    inverse_std = lax.rsqrt(jnp.mean(centered * centered, -1, keepdims=True) + EPSILON)
    normed = centered * inverse_std
    gain_full = norm_gain.astype(jnp.float32)
    hidden_in = (normed * gain_full + norm_bias.astype(jnp.float32)).astype(jnp.bfloat16)
    joined_qkv = (
        jnp.dot(hidden_in, qkv_weight, preferred_element_type=jnp.float32)
        + qkv_bias.astype(jnp.float32)
    ).reshape(row_count, head_count, 3, DH)
    positions = positions_of(segment_ids).reshape(row_count)
    cosine, sine_table = rotary_tables(positions)
    queries = (rotate(joined_qkv[:, :, 0], cosine, sine_table) * score_scale).astype(jnp.bfloat16)
    key_rows = rotate(joined_qkv[:, :, 1], cosine, sine_table).astype(jnp.bfloat16)
    value_rows = joined_qkv[:, :, 2].astype(jnp.bfloat16)
    seq_shape = (seq_count, length, head_count, DH)
    seq_queries = queries.reshape(seq_shape)
    seq_keys = key_rows.reshape(seq_shape)
    seq_values = value_rows.reshape(seq_shape)
    context, log_total = lax.map(attend_forward, (seq_queries, seq_keys, seq_values, segment_ids))
    context = context.reshape(row_count, head_count * DH).astype(jnp.bfloat16)
    gate_pre = jnp.dot(hidden_in, gate_weight, preferred_element_type=jnp.float32)
    up_pre = jnp.dot(hidden_in, up_weight, preferred_element_type=jnp.float32)
    sigmoid_gate = jax.nn.sigmoid(gate_pre)
    activated = gate_pre * sigmoid_gate
    mixed = (activated * up_pre).astype(jnp.bfloat16)
    partial_out = jnp.dot(context, out_weight, preferred_element_type=jnp.float32) + jnp.dot(
        mixed, down_weight, preferred_element_type=jnp.float32
    )
    summed = lax.psum(partial_out, "tensor")
    output = (inputs + summed).astype(jnp.bfloat16)
    grad_context = contract_cols(cotangent, out_weight).astype(jnp.bfloat16)
    grad_out_w = contract_rows(context, cotangent)
    grad_down_w = contract_rows(mixed, cotangent)
    grad_out_part, grad_down_part = (
        lax.psum_scatter(grad_out_w, "dp", scatter_dimension=1, tiled=True),
        lax.psum_scatter(grad_down_w, "dp", scatter_dimension=1, tiled=True),
    )
    grad_mixed = contract_cols(cotangent, down_weight)
    grad_up = (grad_mixed * activated).astype(jnp.bfloat16)
    grad_gate = (
        grad_mixed * up_pre * sigmoid_gate * (1.0 + gate_pre * (1.0 - sigmoid_gate))
    ).astype(jnp.bfloat16)
    grad_gate_w = contract_rows(hidden_in, grad_gate)
    grad_up_w = contract_rows(hidden_in, grad_up)
    grad_hidden = contract_cols(grad_gate, gate_weight) + contract_cols(grad_up, up_weight)
    grad_queries, grad_keys, grad_values = lax.map(
        attend_backward,
        (
            seq_queries,
            seq_keys,
            seq_values,
            segment_ids,
            log_total,
            grad_context.reshape(seq_shape),
        ),
    )
    flat_shape = (row_count, head_count, DH)
    grad_queries = rotate_back(grad_queries.reshape(flat_shape) * score_scale, cosine, sine_table)
    grad_keys = rotate_back(grad_keys.reshape(flat_shape), cosine, sine_table)
    grad_joined = (
        jnp.stack([grad_queries, grad_keys, grad_values.reshape(flat_shape)], axis=2)
        .reshape(row_count, head_count * 3 * DH)
        .astype(jnp.bfloat16)
    )
    bias_local = jnp.sum(grad_joined.astype(jnp.float32), 0)
    grad_qkv_w = contract_rows(hidden_in, grad_joined)
    grad_hidden = grad_hidden + contract_cols(grad_joined, qkv_weight)
    grad_qkv_part, grad_gate_part, grad_up_part = (
        lax.psum_scatter(grad_qkv_w, "dp", scatter_dimension=0, tiled=True),
        lax.psum_scatter(grad_gate_w, "dp", scatter_dimension=0, tiled=True),
        lax.psum_scatter(grad_up_w, "dp", scatter_dimension=0, tiled=True),
    )
    grad_total = lax.psum(grad_hidden, "tensor")
    grad_input = (
        cotangent.astype(jnp.float32) + norm_back(grad_total, normed, inverse_std, gain_full)
    ).astype(jnp.bfloat16)
    grad_gain, grad_shift, grad_bias = lax.psum(
        (jnp.sum(grad_total * normed, 0), jnp.sum(grad_total, 0), bias_local), "dp"
    )
    return (
        output,
        grad_input,
        grad_gain,
        grad_shift,
        grad_qkv_part,
        grad_bias,
        grad_out_part,
        grad_gate_part,
        grad_up_part,
        grad_down_part,
    )


BF = jnp.bfloat16
F32 = jnp.float32
MESH = pl.DeviceIdType.MESH
W = 256
PR = 32
SMALL_AT = 2
LATE = 8
WAIT2 = 4


def comm_kernel(
    dims,
    hid_h, cot_h, tok_h, ctx_h, gj_h, z_h, gu_h, gain_ref, bias_ref, qkv_h, gate_h, up_h, down_h,
    out_o, gin_o, sg_o, ss_o, sb_o, gq_o, go_o, gg_o, gu_o, gd_o,
    hid_t, cot, cot_s, tok, ctx, gj, w_a, w_b, w_d, acc, gu, s1, own, recv1, recv2, recv3,
    zs, ze, zm, svb, svr, svq,
    ld_sem, w_sem, s1_send, s1_recv, s2_send, s2_recv, s3_send, s3_recv,
    e_send, e_recv, m_send, m_recv, o_send, o_recv, o_loc, g_sem, v_send, v_recv,
):
    rows, width, full, tail, n_out, n_qkv, n_batch = dims
    n_piece = rows // PR
    hid = zs.at[1]
    t0 = full * W
    b_pairs = n_out + n_qkv
    b_left = b_pairs + 2 * full
    b_up = b_left + 1
    dp = lax.axis_index("dp")
    zi = lax.axis_index("tensor")
    c = lax.rem(dp, 2)
    x = lax.rem(dp // 2, 2)
    y = dp // 4
    core_dev = {"dp": dp + 1 - 2 * c}
    x_dev = {"dp": dp + 2 - 4 * x}
    y_dev = {"dp": dp + 4 - 8 * y}
    is_mid = (zi == 1) | (zi == 2)
    is_end = (zi == 0) | (zi == 3)
    end_of = jnp.where(zi == 1, 0, 3)
    mid_of_end = jnp.where(zi == 0, 1, 2)
    end_dev = {"tensor": end_of}
    mid_dev = {"tensor": mid_of_end}
    other_mid = {"tensor": 3 - zi}

    def load(src, dst, k):
        return pltpu.make_async_copy(src, dst, ld_sem.at[k])

    def w_down(i):
        return pltpu.make_async_copy(down_h.at[pl.ds(i * W, W), :], w_d, w_sem.at[2])

    def w_gate(i):
        return pltpu.make_async_copy(gate_h.at[:, pl.ds(i * W, W)], w_a, w_sem.at[0])

    def w_up(i):
        return pltpu.make_async_copy(up_h.at[:, pl.ds(i * W, W)], w_b, w_sem.at[1])

    def w_qkv(j, side):
        return pltpu.make_async_copy(qkv_h.at[:, pl.ds(j * W, W)], (w_a, w_b)[side], w_sem.at[side])

    w_gate_t = pltpu.make_async_copy(gate_h.at[:, pl.ds(t0, tail)], w_a.at[:, 0:tail], w_sem.at[0])
    w_up_t = pltpu.make_async_copy(up_h.at[:, pl.ds(t0, tail)], w_a.at[:, tail : 2 * tail], w_sem.at[1])
    w_down_t = pltpu.make_async_copy(down_h.at[pl.ds(t0, tail), :], w_d.at[0:tail, :], w_sem.at[2])

    ctx_ld = load(ctx_h, ctx, 0)
    hid_ld = load(hid_h, hid, 1)
    cot_ld = load(cot_h, cot, 2)
    gj_ld = load(gj_h, gj, 3)
    tok_ld = load(tok_h, tok, 4)
    cs_ld = [
        load(cot_h.at[:, (2 * q + s) * W : (2 * q + s + 1) * W], cot_s.at[s, :, q * W : (q + 1) * W], 5 + 2 * q + s)
        for q in range(4)
        for s in range(2)
    ]
    z_ld = load(z_h, zs.at[0], 13)
    gu_ld = load(gu_h, gu, 14)
    z_ld.start()
    ctx_ld.start()
    for cp in cs_ld:
        cp.start()
    hid_ld.start()
    w_qkv(0, 0).start()
    gj_ld.start()
    w_qkv(1, 1).start()
    w_down(0).start()
    tok_ld.start()
    cot_ld.start()
    gu_ld.start()
    acc[...] = jnp.zeros_like(acc)

    barrier = pltpu.get_barrier_semaphore()
    for dev in (core_dev, x_dev, y_dev, {"dp": dp + 2 - 4 * x + 4 - 8 * y}):
        pl.semaphore_signal(barrier, inc=1, device_id=dev, device_id_type=MESH)

    @pl.when(is_mid)
    def _():
        pl.semaphore_signal(barrier, inc=1, device_id=end_dev, device_id_type=MESH)
        pl.semaphore_signal(barrier, inc=1, device_id=other_mid, device_id_type=MESH)

    @pl.when(is_end)
    def _():
        pl.semaphore_signal(barrier, inc=1, device_id=mid_dev, device_id_type=MESH)

    pl.semaphore_wait(barrier, jnp.where(is_mid, 6, 5))

    def rdma(src, dst, send, recv, dev):
        return pltpu.make_async_remote_copy(
            src_ref=src, dst_ref=dst, send_sem=send, recv_sem=recv, device_id=dev, device_id_type=MESH
        )

    def c1(b):
        slot = lax.rem(b, 4)
        return rdma(s1.at[slot], recv1.at[b], s1_send.at[slot], s1_recv.at[b], core_dev)

    def c2(b, h):
        if h == 0:
            return rdma(recv1.at[b, :, 1 - x, 0], recv2.at[b, 0], s2_send.at[b, 0], s2_recv.at[b, 0], x_dev)
        return rdma(recv1.at[b, 1 - y, :, 1], recv2.at[b, 1], s2_send.at[b, 1], s2_recv.at[b, 1], y_dev)

    def c3(b, h):
        if h == 0:
            return rdma(recv2.at[b, 0, 1 - y], recv3.at[b, 0], s3_send.at[b, 0], s3_recv.at[b, 0], y_dev)
        return rdma(recv2.at[b, 1, 1 - x], recv3.at[b, 1], s3_send.at[b, 1], s3_recv.at[b, 1], x_dev)

    def up32(v):
        return v.astype(F32)

    def ev1(b):
        slot = lax.rem(b, 4)
        c1(b).wait_recv()
        for yy in range(2):
            for xx in range(2):
                for h in range(2):
                    recv1[b, yy, xx, h] += own[slot, yy, xx, h]
        c2(b, 0).start()
        c2(b, 1).start()

    def ev2(b):
        c2(b, 0).wait_recv()
        c2(b, 1).wait_recv()
        for k in range(2):
            recv2[b, 0, k] += recv1[b, k, x, 0]
            recv2[b, 1, k] += recv1[b, y, k, 1]
        c3(b, 0).start()
        c3(b, 1).start()

    def cut(b, h, ref, row, col, n=W // 2, lo=0, wide=W):
        if not isinstance(row, int):
            row = pl.multiple_of(row, 64)
        if not isinstance(col, int):
            col = pl.multiple_of(col, W // 2)
        return pltpu.make_async_copy(
            recv3.at[b, h, 0:n, lo : lo + wide], ref.at[pl.ds(row + h * n, n), pl.ds(col, wide)], g_sem.at[b, h]
        )

    groups = (
        (0, n_out, 1, lambda b, h, i: (cut(b, h, go_o, i * W, 0),)),
        (n_out, n_qkv, 1, lambda b, h, i: (cut(b, h, gq_o, 0, i * W),)),
        (b_left, 1, 1, lambda b, h, i: (cut(b, h, gd_o, t0, 0, tail // 2),)),
        (b_pairs, full, 2, lambda b, h, i: (cut(b, h, gd_o, i * W, 0),)),
        (b_pairs + 1, full, 2, lambda b, h, i: (cut(b, h, gg_o, 0, i * W),)),
        (b_up, full, 1, lambda b, h, i: (cut(b, h, gu_o, 0, i * W),)),
        (
            b_up + full, 1, 1,
            lambda b, h, i: (
                cut(b, h, gg_o, 0, t0, wide=tail), cut(b, h, gu_o, 0, t0, lo=tail, wide=tail)
            ),
        ),
    )

    def ev3(b):
        c3(b, 0).wait_recv()
        c3(b, 1).wait_recv()
        recv3[b, 0] += recv2[b, 0, y]
        recv3[b, 1] += recv2[b, 1, x]
        for first, count, step, make in groups:
            here = (b >= first) & (b < first + count * step)
            if step > 1:
                here = here & (lax.rem(b - first, step) == 0)

            @pl.when(here)
            def _(first=first, step=step, make=make):
                for h in range(2):
                    for cp in make(b, h, (b - first) // step):
                        cp.start()

    def before_put(b):
        @pl.when(b >= 4)
        def _():
            c1(b - 4).wait_send()

    def after_put(b):
        c1(b).start()

    def put_rows(b, grad):
        slot = lax.rem(b, 4)
        before_put(b)
        for part, dst in ((1 - c, s1), (c, own)):
            left = hid_t[:, part].reshape(4 * W, rows)
            res = jnp.dot(left, grad, preferred_element_type=F32).astype(BF)
            dst[slot] = res.reshape(2, 2, 2, W // 2, W)
        after_put(b)

    def put_cols(b, left_t):
        slot = lax.rem(b, 4)
        h = left_t.shape[0]
        before_put(b)
        for part, dst in ((1 - c, s1), (c, own)):
            res = jnp.dot(left_t, cot_s[part], preferred_element_type=F32).astype(BF)
            for q in range(4):
                piece = res[:, q * W : (q + 1) * W].reshape(2, h // 2, W)
                dst[slot, q // 2, q % 2, :, 0 : h // 2, :] = piece
                if h < W:
                    dst[slot, q // 2, q % 2, :, h // 2 :, :] = jnp.zeros((2, (W - h) // 2, W), BF)
        after_put(b)

    NB = 512

    def acc_rows(grad, w_ref):
        for n in range(width // NB):
            cols = slice(n * NB, (n + 1) * NB)
            acc[:, cols] += lax.dot_general(
                grad, w_ref[cols, :], (((1,), (1,)), ((), ())), preferred_element_type=F32
            )

    def z_rows(p):
        return pl.ds(pl.multiple_of(p * PR, PR), PR)

    def ce(a, p):
        i = a * n_piece + p
        return rdma(zs.at[a, z_rows(p)], ze.at[a, z_rows(p)], e_send.at[i], e_recv.at[i], mid_dev)

    def cm(a, p):
        i = a * n_piece + p
        return rdma(zs.at[a, z_rows(p)], zm.at[a, z_rows(p)], m_send.at[i], m_recv.at[i], other_mid)

    def co(a, p, ref):
        i = a * n_piece + p
        return rdma(ze.at[a, z_rows(p)], ref.at[z_rows(p)], o_send.at[i], o_recv.at[i], end_dev)

    def cl(a, p, ref):
        i = a * n_piece + p
        return pltpu.make_async_copy(ze.at[a, z_rows(p)], ref.at[z_rows(p)], o_loc.at[i])

    def ev_e(e):
        a, p = e // n_piece, lax.rem(e, n_piece)

        @pl.when(is_mid)
        def _():
            ce(a, p).wait_recv()
            r = z_rows(p)
            zs[a, r, :] += ze[a, r, :]
            cm(a, p).start()

    def norm_rows(r):
        v = up32(tok[r, :])
        mu = jnp.mean(v, -1, keepdims=True)
        v = v - mu
        inv = lax.rsqrt(jnp.mean(v * v, -1, keepdims=True) + EPSILON)
        return v * inv, inv

    def ev_m(e):
        a, p = e // n_piece, lax.rem(e, n_piece)

        @pl.when(is_mid)
        def _():
            cm(a, p).wait_recv()
            r = z_rows(p)

            @pl.when(a == 0)
            def _():
                total = up32(zs[0, r, :]) + up32(zm[0, r, :])
                ze[0, r, :] = (up32(tok[r, :]) + total).astype(BF)
                co(0, p, out_o).start()
                cl(0, p, out_o).start()

            @pl.when(a == 1)
            def _():
                total = up32(zs[1, r, :]) + up32(zm[1, r, :])
                normed, inv = norm_rows(r)
                back = norm_back(total, normed, inv, gain_ref[...])
                ze[1, r, :] = (up32(cot[r, :]) + back).astype(BF)
                co(1, p, gin_o).start()
                cl(1, p, gin_o).start()

    def act_of(g, u):
        return (g * jax.nn.sigmoid(g) * u).astype(BF)

    def joined_grad(j):
        return jnp.concatenate([gj[2 * j], gj[2 * j + 1]], axis=1)

    def cv(k, dev):
        return rdma(svb.at[k], svr.at[k], v_send.at[k], v_recv.at[k], dev)

    def cw(k, dev):
        return rdma(svb.at[4], svq.at[y, x], v_send.at[4 + k], v_recv.at[4 + k], dev)

    square = (x_dev, y_dev, {"dp": dp + 2 - 4 * x + 4 - 8 * y})

    def small_1():
        @pl.when(is_mid)
        def _():
            cv(0, end_dev).wait_recv()
            svb[1] = svb[0] + svr[0]
            cv(1, other_mid).start()

    def small_2():
        @pl.when(is_mid)
        def _():
            cv(1, other_mid).wait_recv()
            svb[2] = svb[1] + svr[1]
            svb[3, 0:2, :] = svb[2, 0:2, :]
            cv(2, end_dev).start()

    def small_3():
        @pl.when(is_end)
        def _():
            cv(2, mid_dev).wait_recv()
            svb[3, 0:2, :] = svr[2, 0:2, :]

        svb[3, 2:8, :] = svb[0, 2:8, :]
        cv(3, core_dev).start()

    def small_4():
        cv(3, core_dev).wait_recv()
        svb[4] = svb[3] + svr[3]
        svq[y, x] = svb[4]
        for k, dev in enumerate(square):
            cw(k, dev).start()

    def small_5():
        for k, dev in enumerate(square):
            cw(k, dev).wait_recv()
        total = (svq[0, 0] + svq[0, 1]) + (svq[1, 0] + svq[1, 1])
        for row, ref in enumerate((sg_o, ss_o, sb_o)):
            for n in range(ref.shape[0]):
                ref[n : n + 1, :] = total[row : row + 1, n * 128 : (n + 1) * 128]

    def small_sent():
        @pl.when(is_end)
        def _():
            cv(0, mid_dev).wait_send()

        @pl.when(is_mid)
        def _():
            cv(1, other_mid).wait_send()
            cv(2, end_dev).wait_send()

        cv(3, core_dev).wait_send()
        for k, dev in enumerate(square):
            cw(k, dev).wait_send()

    def send_line(a):
        def send(p, keep):
            ce(a, p).start()
            return keep

        @pl.when(is_end)
        def _():
            if a == 1:
                cv(0, mid_dev).start()
            lax.fori_loop(0, n_piece, send, 0)

    def line_rows(p, keep):
        r = z_rows(p)
        v = acc[r, :]
        zs[1, r, :] = v.astype(BF)
        normed, _inv = norm_rows(r)
        svb[0, 0:1, :] += jnp.sum(v * normed, 0, keepdims=True)
        svb[0, 1:2, :] += jnp.sum(v, 0, keepdims=True)
        return keep

    z_ld.wait()
    send_line(0)
    ctx_ld.wait()
    for cp in cs_ld:
        cp.wait()
    for j in range(n_out):
        put_cols(jnp.int32(j), ctx[:, j * W : (j + 1) * W].T)
    hid_ld.wait()
    for q in range(4):
        for s in range(2):
            lo = (2 * q + s) * W
            hid_t[q, s] = hid[:, lo : lo + W].T
    for b in range(n_out):
        ev1(jnp.int32(b))
    gj_ld.wait()
    tok_ld.wait()
    cot_ld.wait()

    def joined(n, keep):
        for side in range(2):
            j = 2 * n + side
            w_qkv(j, side).wait()
            acc_rows(joined_grad(j), (w_a, w_b)[side])

            @pl.when(j + 2 < n_qkv)
            def _(j=j, side=side):
                w_qkv(j + 2, side).start()

            @pl.when(j + 2 >= n_qkv)
            def _(side=side):
                (w_gate, w_up)[side](0).start()

            b = n_out + j
            put_rows(b, joined_grad(j))

            @pl.when(j >= 1)
            def _(b=b):
                ev1(b - 1)

        ev_e(n)

        @pl.when(n >= 1)
        def _():
            ev2(n - 1)

        @pl.when(n >= 2)
        def _():
            ev_m(n - 2)

        return keep

    lax.fori_loop(0, n_qkv // 2, joined, 0)
    gu_ld.wait()

    def gate_grads(gm, g, u):
        sg = jax.nn.sigmoid(g)
        g_up = (gm * (g * sg)).astype(BF)
        g_gate = (gm * u * sg * (1.0 + g * (1.0 - sg))).astype(BF)
        return g_gate, g_up

    def cols_t(left, w_ref, k):
        return lax.dot_general(left, w_ref[0:k, :], (((1,), (1,)), ((), ())), preferred_element_type=F32)

    e0 = n_qkv // 2
    two = n_qkv // 2 - 1

    def bwd(i, keep):
        w_down(i).wait()
        gm = cols_t(cot[...], w_d, W)

        @pl.when(i + 1 < full)
        def _():
            w_down(i + 1).start()

        @pl.when(i + 1 == full)
        def _():
            w_down_t.start()

        g, u = up32(gu[i, 0]), up32(gu[i, 1])
        mixed = act_of(g, u)
        g_gate, g_up = gate_grads(gm, g, u)
        gu[i, 0] = g_gate
        gu[i, 1] = g_up
        w_gate(i).wait()
        acc_rows(g_gate, w_a)
        w_up(i).wait()
        acc_rows(g_up, w_b)

        @pl.when(i + 1 < full)
        def _():
            w_gate(i + 1).start()
            w_up(i + 1).start()

        @pl.when(i + 1 == full)
        def _():
            w_gate_t.start()
            w_up_t.start()

        b = b_pairs + 2 * i
        e = e0 + 2 * i
        put_cols(b, mixed.T)
        ev1(b - 1)
        ev_e(e)
        ev_m(e - 2)
        put_rows(b + 1, gu[i, 0])
        ev1(b)
        ev2(two + i)
        ev_e(e + 1)
        ev_m(e - 1)
        return keep

    lax.fori_loop(0, full, bwd, 0)
    w_down_t.wait()
    gm = cols_t(cot[...], w_d, tail)
    both = up32(gu[full, 0])
    mixed = act_of(both[:, 0:tail], both[:, tail:])
    g_gate, g_up = gate_grads(gm, both[:, 0:tail], both[:, tail:])
    both = jnp.concatenate([g_gate, g_up], axis=1)
    gu[full, 0] = both
    w_gate_t.wait()
    w_up_t.wait()
    acc_rows(both, w_a)
    svb[0] = jnp.zeros_like(svb[0])
    svb[0, 2:3, 0 : n_qkv * W] = bias_ref[...]
    lax.fori_loop(0, n_piece, line_rows, 0)
    send_line(1)

    put_cols(jnp.int32(b_left), mixed.T)
    ev1(jnp.int32(b_left - 1))
    e0 = e0 + 2 * full
    two = two + full
    ev2(jnp.int32(two))
    ev_e(jnp.int32(e0))
    ev_m(jnp.int32(e0 - 2))

    def left_over(i, keep):
        b = b_up + i
        at = jnp.where(i == full, 0, 1)
        put_rows(b, gu[i, at])
        ev1(b - 1)
        ev2(two + 1 + i)
        ev_e(e0 + 1 + i)
        ev_m(e0 - 1 + i)
        return keep

    lax.fori_loop(0, full + 1, left_over, 0)
    ev1(jnp.int32(n_batch - 1))
    e0 = e0 + full + 2
    two_left = two + full + 2

    n_e = 2 * n_piece
    smalls = (small_1, small_2, small_3, small_4)

    def drain(k, keep):
        @pl.when(k + e0 < n_e)
        def _():
            ev_e(k + e0)

        @pl.when(k + e0 - 2 < n_e)
        def _():
            ev_m(k + e0 - 2)

        @pl.when((k >= WAIT2) & (k - WAIT2 + two_left < n_batch))
        def _():
            ev2(k - WAIT2 + two_left)

        for i, small in enumerate(smalls):
            pl.when(k == SMALL_AT + i)(small)

        for h in range(2):
            b = 2 * (k - LATE) + h

            @pl.when((b >= 0) & (b < n_batch))
            def _():
                ev3(b)

        return keep

    steps = max(LATE + (n_batch + 1) // 2, n_e - e0 + 2, WAIT2 + n_batch - two_left)
    lax.fori_loop(0, steps, drain, 0)
    small_5()

    small_sent()

    def finish(b, keep):
        for h in range(2):
            c2(b, h).wait_send()
            c3(b, h).wait_send()
        return keep

    lax.fori_loop(0, n_batch, finish, 0)
    for k in range(4):
        c1(jnp.int32(n_batch - 4 + k)).wait_send()
    for first, count, step, make in groups:
        for i in range(count):
            for h in range(2):
                for cp in make(first + i * step, h, i):
                    cp.wait()

    def finish_line(p, keep):
        for a, ref in ((0, out_o), (1, gin_o)):
            @pl.when(is_mid)
            def _():
                cm(a, p).wait_send()
                co(a, p, ref).wait_send()
                cl(a, p, ref).wait()

            @pl.when(is_end)
            def _():
                ce(a, p).wait_send()
                co(a, p, ref).wait_recv()

        return keep

    lax.fori_loop(0, n_piece, finish_line, 0)


def comm_call(hidden, cot, tokens, ctx, gj, partial, gu, gain, bias_sum, qkv_w, gate_w, up_w, down_w):
    rows, width = hidden.shape
    hd = ctx.shape[1]
    ff = gate_w.shape[1]
    full, tail = ff // W, ff % W
    n_out, n_qkv = hd // W, qkv_w.shape[1] // W
    n_batch = n_out + full + 1 + n_qkv + 2 * full + 1
    n_z = 2 * (rows // PR)
    dims = (rows, width, full, tail, n_out, n_qkv, n_batch)
    piece = (W // 2, W)
    vm, dma = pltpu.VMEM, pltpu.SemaphoreType.DMA
    any_spec = pl.BlockSpec(memory_space=pl.ANY)
    vm_spec = pl.BlockSpec(memory_space=pltpu.VMEM)
    return pl.pallas_call(
        functools.partial(comm_kernel, dims),
        out_shape=(
            jax.ShapeDtypeStruct((rows, width), BF),
            jax.ShapeDtypeStruct((rows, width), BF),
            jax.ShapeDtypeStruct((width // 128, 128), F32),
            jax.ShapeDtypeStruct((width // 128, 128), F32),
            jax.ShapeDtypeStruct((n_qkv * W // 128, 128), F32),
            jax.ShapeDtypeStruct((W, n_qkv * W), BF),
            jax.ShapeDtypeStruct((hd, W), BF),
            jax.ShapeDtypeStruct((W, ff), BF),
            jax.ShapeDtypeStruct((W, ff), BF),
            jax.ShapeDtypeStruct((ff, W), BF),
        ),
        in_specs=[any_spec] * 7 + [vm_spec] * 2 + [any_spec] * 4,
        out_specs=(any_spec,) * 2 + (vm_spec,) * 3 + (any_spec,) * 5,
        scratch_shapes=[
            vm((4, 2, W, rows), BF),
            vm((rows, width), BF),
            vm((2, rows, width // 2), BF),
            vm((rows, width), BF),
            vm((rows, hd), BF),
            vm((2 * n_qkv, rows, W // 2), BF),
            vm((width, W), BF),
            vm((width, W), BF),
            vm((W, width), BF),
            vm((rows, width), F32),
            vm((full + 1, 2, rows, W), BF),
            vm((4, 2, 2, 2) + piece, BF),
            vm((4, 2, 2, 2) + piece, BF),
            vm((n_batch, 2, 2, 2) + piece, BF),
            vm((n_batch, 2, 2) + piece, BF),
            vm((n_batch, 2) + piece, BF),
            vm((2, rows, width), BF),
            vm((2, rows, width), BF),
            vm((2, rows, width), BF),
            vm((5, 8, width), F32),
            vm((4, 8, width), F32),
            vm((2, 2, 8, width), F32),
            dma((15,)),
            dma((3,)),
            dma((4,)),
            dma((n_batch,)),
            dma((n_batch, 2)),
            dma((n_batch, 2)),
            dma((n_batch, 2)),
            dma((n_batch, 2)),
            dma((n_z,)),
            dma((n_z,)),
            dma((n_z,)),
            dma((n_z,)),
            dma((n_z,)),
            dma((n_z,)),
            dma((n_z,)),
            dma((n_batch, 2)),
            dma((7,)),
            dma((7,)),
        ],
        compiler_params=pltpu.CompilerParams(
            collective_id=0, has_side_effects=True, vmem_limit_bytes=67043328
        ),
        name="ffn_and_sums",
    )(hidden, cot, tokens, ctx, gj, partial, gu, gain, bias_sum, qkv_w, gate_w, up_w, down_w)


def forward_kernel(full, tail, hid, ctx, out_w, gate_w, up_w, down_w, z_o, gu_o, acc):
    i = pl.program_id(0)
    width = acc.shape[1]
    blocks = [slice(n, n + 512) for n in range(0, width, 512)]

    def dot(a, b):
        return jnp.dot(a, b, preferred_element_type=F32)

    def act_of(g, u):
        return (g * jax.nn.sigmoid(g) * u).astype(BF)

    @pl.when(i == 0)
    def _():
        for cols in blocks:
            acc[:, cols] = dot(ctx[...], out_w[:, cols])

    @pl.when(i < full)
    def _():
        g = dot(hid[...], gate_w[...])
        u = dot(hid[...], up_w[...])
        gu_o[0, 0] = g.astype(BF)
        gu_o[0, 1] = u.astype(BF)
        mixed = act_of(g, u)
        for cols in blocks:
            acc[:, cols] += dot(mixed, down_w[:, cols])

    @pl.when(i == full)
    def _():
        both = dot(hid[...], jnp.concatenate([gate_w[:, 0:tail], up_w[:, 0:tail]], axis=1))
        gu_o[0, 0] = both.astype(BF)
        gu_o[0, 1] = jnp.zeros_like(both).astype(BF)
        mixed = act_of(both[:, 0:tail], both[:, tail:])
        for cols in blocks:
            z_o[:, cols] = (acc[:, cols] + dot(mixed, down_w[0:tail, cols])).astype(BF)


def forward_call(hidden, ctx, out_w, gate_w, up_w, down_w):
    rows, width = hidden.shape
    hd = ctx.shape[1]
    ff = gate_w.shape[1]
    full, tail = ff // W, ff % W
    once = lambda shape: pl.BlockSpec(shape, lambda i: (0,) * len(shape), pipeline_mode=pl.Buffered(1))
    return pl.pallas_call(
        functools.partial(forward_kernel, full, tail),
        grid=(full + 1,),
        out_shape=(
            jax.ShapeDtypeStruct((rows, width), BF),
            jax.ShapeDtypeStruct((full + 1, 2, rows, W), BF),
        ),
        in_specs=[
            once((rows, width)),
            once((rows, hd)),
            once((hd, width)),
            pl.BlockSpec((width, W), lambda i: (0, i)),
            pl.BlockSpec((width, W), lambda i: (0, i)),
            pl.BlockSpec((W, width), lambda i: (i, 0)),
        ],
        out_specs=(
            once((rows, width)),
            pl.BlockSpec((1, 2, rows, W), lambda i: (i, 0, 0, 0)),
        ),
        scratch_shapes=[pltpu.VMEM((rows, width), F32)],
        compiler_params=pltpu.CompilerParams(vmem_limit_bytes=60 << 20),
        name="forward",
    )(hidden, ctx, out_w, gate_w, up_w, down_w)


PARTS = 4


def finish_kernel(*refs):
    n = len(refs) // 2
    for src, dst in zip(refs[:n], refs[n:]):
        dst[...] = src[...].astype(dst.dtype)


def finish_call(values, types):
    def spec(v):
        if v.shape[0] < 16 * PARTS:
            return pl.BlockSpec(v.shape, lambda i: (0, 0))
        return pl.BlockSpec((v.shape[0] // PARTS, v.shape[1]), lambda i: (i, 0))

    return pl.pallas_call(
        finish_kernel,
        grid=(PARTS,),
        out_shape=tuple(jax.ShapeDtypeStruct(v.shape, t) for v, t in zip(values, types)),
        in_specs=[spec(v) for v in values],
        out_specs=tuple(spec(v) for v in values),
        compiler_params=pltpu.CompilerParams(vmem_limit_bytes=60 << 20),
        name="finish",
    )(*values)


QB = 128
ROWS = 32


def attn_kernel(
    heads_scale, tok, seg_ref, gain_ref, shift_ref, b_ref, w_ref, ow_ref, cot,
    hid, ctx_o, gj_o, bias_o, gain_o,
    bias_m, tab, s_m, g_m, p_m, gs_m, shift_m, b_m,
):
    rows = tok.shape[0]
    nq = rows // QB
    half = ROT // 2

    step = pl.program_id(0)

    @pl.when(step == 0)
    def _():
        for n in range(gain_ref.shape[0]):
            cols = slice(n * QB, (n + 1) * QB)
            gain_o[0:1, cols] = gain_ref[n : n + 1, :].astype(F32)
            shift_m[0:1, cols] = shift_ref[n : n + 1, :].astype(F32)
        b_m[...] = b_ref[...].astype(F32)

        def norm_step(n, keep):
            r = pl.ds(pl.multiple_of(n * 64, 64), 64)
            v = tok[r, :].astype(F32)
            v = v - jnp.mean(v, -1, keepdims=True)
            v = v * lax.rsqrt(jnp.mean(v * v, -1, keepdims=True) + EPSILON)
            hid[r, :] = (v * gain_o[...] + shift_m[...]).astype(BF)
            return keep

        lax.fori_loop(0, rows // 64, norm_step, 0)
        seg = seg_ref[...].astype(F32)
        seg_t = jnp.broadcast_to(seg, (8, rows)).T
        lane = lax.broadcasted_iota(jnp.int32, (QB, QB), 1)
        head_lane = lane % DH
        freq = jnp.ones((1, QB), F32)
        for n in range(1, half):
            freq = jnp.where(head_lane[0:1] % half == n, 10000.0 ** (-2.0 * n / ROT), freq)
        group = QB // nq
        packed = jnp.zeros((QB, QB), F32)
        for i in range(nq):
            lo = max(0, i - 2) * QB
            n = (i + 1) * QB - lo
            q_at = lax.broadcasted_iota(jnp.int32, (QB, n), 0) + i * QB
            k_at = lax.broadcasted_iota(jnp.int32, (QB, n), 1) + lo
            same = seg_t[i * QB : (i + 1) * QB, 0:1] == seg[:, lo : lo + n]
            allowed = same & (q_at >= k_at)
            bias_m[i, :, 0:n] = jnp.where(allowed, 0.0, NEGATIVE)
            place = jnp.sum(jnp.where(allowed, 1.0, 0.0), -1, keepdims=True) - 1.0
            packed = jnp.where(lane // group == i, place, packed)
        angle = packed * freq
        tables = jnp.cos(angle), jnp.sin(angle)
        for i in range(nq):
            cosine, sine = (
                jnp.where(
                    lane < DH,
                    pltpu.roll(t, (QB - group * i) % QB, 1) if i else t,
                    pltpu.roll(t, (QB + DH - group * i) % QB, 1) if DH != group * i else t,
                )
                for t in tables
            )
            for blk in range(3):
                live = head_lane < ROT
                if blk == 1:
                    live = live & (lane >= DH)
                if blk == 2:
                    live = live & (lane < DH)
                scale = jnp.ones((QB, QB), F32)
                if blk == 0:
                    scale = jnp.where(lane < DH, heads_scale, 1.0)
                if blk == 1:
                    scale = jnp.where(lane >= DH, heads_scale, 1.0)
                r = slice(i * QB, (i + 1) * QB)
                tab[blk, 0, r] = jnp.where(live, cosine, 1.0) * scale
                tab[blk, 1, r] = jnp.where(live & (head_lane < half), -sine, 0.0) * scale
                tab[blk, 2, r] = jnp.where(live & (head_lane >= half), sine, 0.0) * scale

    def dot_t(a, b):
        return lax.dot_general(a, b, (((1,), (1,)), ((), ())), preferred_element_type=F32)

    def dot(a, b):
        return jnp.dot(a, b, preferred_element_type=F32)

    joined = dot(hid[...], w_ref[...])
    turned = []
    for blk in range(3):
        v = joined[:, blk * QB : (blk + 1) * QB] + b_m[pl.ds(3 * step + blk, 1), :]
        v = v * tab[blk, 0] + pltpu.roll(v, QB - half, 1) * tab[blk, 1] + pltpu.roll(v, half, 1) * tab[blk, 2]
        turned.append(v.astype(BF))
    gctx = dot_t(cot[...], ow_ref[...]).astype(BF)
    lo_h, hi_h = slice(0, DH), slice(DH, 2 * DH)
    heads = (
        (turned[0][:, lo_h], turned[0][:, hi_h], turned[1][:, lo_h], gctx[:, lo_h]),
        (turned[1][:, hi_h], turned[2][:, lo_h], turned[2][:, hi_h], gctx[:, hi_h]),
    )
    spans = [(max(0, i - 2) * QB, (i + 1) * QB) for i in range(nq)]
    blocks = [(n, i) for i in range(nq) for n in range(2)]
    for n, i in blocks:
        q, k, v, gc = heads[n]
        lo, hi = spans[i]
        s_m[n, i, :, 0 : hi - lo] = dot_t(q[i * QB : hi], k[lo:hi])
        g_m[n, i, :, 0 : hi - lo] = dot_t(gc[i * QB : hi], v[lo:hi])
    for n, i in blocks:
        lo, hi = spans[i]
        for r in range(0, QB, ROWS):
            rr = slice(r, r + ROWS)
            s = s_m[n, i, rr, 0 : hi - lo] + bias_m[i, rr, 0 : hi - lo]
            e = jnp.exp(s - jnp.max(s, -1, keepdims=True))
            p = e * (1.0 / jnp.sum(e, -1, keepdims=True))
            gp = g_m[n, i, rr, 0 : hi - lo]
            p_m[n, i, rr, 0 : hi - lo] = p.astype(BF)
            gs_m[n, i, rr, 0 : hi - lo] = (p * (gp - jnp.sum(p * gp, -1, keepdims=True))).astype(BF)
    grads, contexts = [], []
    for n, (q, k, v, gc) in enumerate(heads):
        out, grad_q, grad_k, grad_v = [], [], [], []
        for i, (lo, hi) in enumerate(spans):
            out.append(dot(p_m[n, i, :, 0 : hi - lo], v[lo:hi]))
            grad_q.append(dot(gs_m[n, i, :, 0 : hi - lo], k[lo:hi]))
        for j in range(nq):
            top = min(j + 3, nq)

            def stack(part):
                cut = []
                for i in range(j, top):
                    at = j * QB - spans[i][0]
                    cut.append(part[n, i, :, at : at + QB].T)
                return jnp.concatenate(cut, 1)

            grad_k.append(dot(stack(gs_m), q[j * QB : top * QB]))
            grad_v.append(dot(stack(p_m), gc[j * QB : top * QB]))
        contexts.append(jnp.concatenate(out, 0))
        grads.append([jnp.concatenate(part, 0) for part in (grad_q, grad_k, grad_v)])
    ctx_o[...] = jnp.concatenate(contexts, 1).astype(BF)
    (q0, k0, v0), (q1, k1, v1) = grads
    for blk, pair in enumerate(((q0, k0), (v0, q1), (k1, v1))):
        g = jnp.concatenate(pair, 1)
        g = g * tab[blk, 0] - pltpu.roll(g, QB - half, 1) * tab[blk, 1] - pltpu.roll(g, half, 1) * tab[blk, 2]
        g = g.astype(BF)
        gj_o[blk] = g
        bias_o[:, blk * QB : (blk + 1) * QB] = jnp.sum(g.astype(F32), 0, keepdims=True)


def attn_call(tokens, segment_ids, gain, shift, qkv_w, qkv_b, out_w, cot):
    rows, width = tokens.shape
    hd = out_w.shape[0]
    steps = hd // (2 * DH)
    three = 3 * QB
    whole = lambda shape: pl.BlockSpec(shape, lambda i: (0,) * len(shape))
    once = lambda shape: pl.BlockSpec(shape, lambda i: (0,) * len(shape), pipeline_mode=pl.Buffered(1))
    return pl.pallas_call(
        functools.partial(attn_kernel, DH ** (-0.5)),
        grid=(steps,),
        out_shape=(
            jax.ShapeDtypeStruct((rows, width), BF),
            jax.ShapeDtypeStruct((rows, hd), BF),
            jax.ShapeDtypeStruct((3 * steps, rows, QB), BF),
            jax.ShapeDtypeStruct((1, 3 * hd), F32),
            jax.ShapeDtypeStruct((1, width), F32),
        ),
        in_specs=[
            once((rows, width)),
            whole((1, rows)),
            whole((width // QB, QB)),
            whole((width // QB, QB)),
            whole((3 * hd // QB, QB)),
            pl.BlockSpec((width, three), lambda i: (0, i)),
            pl.BlockSpec((QB, width), lambda i: (i, 0)),
            once((rows, width)),
        ],
        out_specs=(
            whole((rows, width)),
            pl.BlockSpec((rows, QB), lambda i: (0, i)),
            pl.BlockSpec((3, rows, QB), lambda i: (i, 0, 0)),
            pl.BlockSpec((1, three), lambda i: (0, i)),
            whole((1, width)),
        ),
        scratch_shapes=[
            pltpu.VMEM((rows // QB, QB, three), F32),
            pltpu.VMEM((3, 3, rows, QB), F32),
            pltpu.VMEM((2, rows // QB, QB, three), F32),
            pltpu.VMEM((2, rows // QB, QB, three), F32),
            pltpu.VMEM((2, rows // QB, QB, three), BF),
            pltpu.VMEM((2, rows // QB, QB, three), BF),
            pltpu.VMEM((1, width), F32),
            pltpu.VMEM((3 * hd // QB, QB), F32),
        ],
        compiler_params=pltpu.CompilerParams(vmem_limit_bytes=60 << 20),
        name="attention",
    )(
        tokens, segment_ids, gain.reshape(-1, QB), shift.reshape(-1, QB), qkv_b.reshape(-1, QB), qkv_w, out_w, cot
    )


def fast(
    n_dp,
    n_tensor,
    tokens,
    segment_ids,
    norm_gain,
    norm_bias,
    qkv_weight,
    qkv_bias,
    out_weight,
    gate_weight,
    up_weight,
    down_weight,
    cotangent,
):
    args = (tokens, segment_ids, norm_gain, norm_bias, qkv_weight, qkv_bias, out_weight, gate_weight, up_weight, down_weight, cotangent)
    row_count, width = tokens.shape
    ff = gate_weight.shape[1]
    fits = (
        (n_dp, n_tensor) == (8, 4)
        and segment_ids.shape == (1, row_count)
        and (row_count, width) == (512, 8 * W)
        and ff % W == W // 2
        and qkv_weight.shape[1] % (2 * W) == 0
        and out_weight.shape[0] % W == 0
        and qkv_weight.shape[1] == 3 * out_weight.shape[0]
        and 2 * DH == QB
        and 4 * ROT <= QB
    )
    if not fits:
        return local(*args)
    hidden_in, context, grad_joined, bias_local, gain_row = attn_call(
        tokens, segment_ids, norm_gain, norm_bias, qkv_weight, qkv_bias, out_weight, cotangent
    )
    partial, gate_up = forward_call(hidden_in, context, out_weight, gate_weight, up_weight, down_weight)
    results = comm_call(
        hidden_in, cotangent, tokens, context, grad_joined, partial, gate_up, gain_row, bias_local,
        qkv_weight, gate_weight, up_weight, down_weight,
    )
    output, grad_input, gain_sum, shift_sum, bias_sum, joined_w, out_w, gate_w, up_w, down_w = finish_call(
        results, (BF,) * 2 + (F32,) * 8
    )
    return (
        output,
        grad_input,
        gain_sum.reshape(width),
        shift_sum.reshape(width),
        joined_w,
        bias_sum.reshape(qkv_weight.shape[1]),
        out_w,
        gate_w,
        up_w,
        down_w,
    )


def solution(mesh):
    body = functools.partial(fast, mesh.shape["dp"], mesh.shape["tensor"])
    return jax.shard_map(
        body,
        mesh=mesh,
        in_specs=(
            P("dp", None),
            P("dp", None),
            P(),
            P(),
            P(None, "tensor"),
            P("tensor"),
            P("tensor", None),
            P(None, "tensor"),
            P(None, "tensor"),
            P("tensor", None),
            P("dp", None),
        ),
        out_specs=(
            P("dp", None),
            P("dp", None),
            P(),
            P(),
            P("dp", "tensor"),
            P("tensor"),
            P("tensor", "dp"),
            P("dp", "tensor"),
            P("dp", "tensor"),
            P("tensor", "dp"),
        ),
        check_vma=False,
    )
```
